32 devices in a mesh: dp: 8 (over z, y), sp: 4 (over x, core).
Axes of the slice: x: 2, y: 2, z: 4, core: 2. Of those that a mesh axis runs over, the one named last changes fastest.
Arguments:
- tokens: bfloat16 [4, 4096, 768], P(None, ('dp', 'sp')), may hold values from -6 to 6
- cotangent: bfloat16 [4, 4096, 768], P(None, ('dp', 'sp')), may hold values from -6 to 6
- seq_cut: int32 [4, 8], P(None, 'dp'), may hold values from 128 to 512, as said below
- ln1_gain: bfloat16 [768], P(('dp', 'sp')), may hold values from 0.5 to 1.5
- ln1_bias: bfloat16 [768], P(('dp', 'sp')), may hold values from -3 to 3
- w_qkv: bfloat16 [768, 2304], P(('dp', 'sp')), may hold values from -0.21875 to 0.21875
- b_query: bfloat16 [768], P(('dp', 'sp')), may hold values from -4 to 4
- b_value: bfloat16 [768], P(('dp', 'sp')), may hold values from -0.75 to 0.75
- w_out: bfloat16 [768, 768], P(('dp', 'sp')), may hold values from -6 to 6
- b_out: bfloat16 [768], P(('dp', 'sp')), may hold values from -6 to 6
- ln2_gain: bfloat16 [768], P(('dp', 'sp')), may hold values from 0.5 to 1.5
- ln2_bias: bfloat16 [768], P(('dp', 'sp')), may hold values from -3 to 3
- w_fc: bfloat16 [768, 3072], P(('dp', 'sp')), may hold values from -0.21875 to 0.21875
- b_fc: bfloat16 [3072], P(('dp', 'sp')), may hold values from -4 to 4
- w_proj: bfloat16 [3072, 768], P(('dp', 'sp')), may hold values from -0.75 to 0.75
- b_proj: bfloat16 [768], P(('dp', 'sp')), may hold values from -6 to 6
Outputs:
- layer_out: bfloat16 [4, 4096, 768], P(None, ('dp', 'sp'))
- input_grad: float32 [4, 4096, 768], P(None, ('dp', 'sp'))
- grad_ln1_gain: float32 [768], P(('dp', 'sp'))
- grad_ln1_bias: float32 [768], P(('dp', 'sp'))
- grad_w_qkv: float32 [768, 2304], P(('dp', 'sp'))
- grad_b_query: float32 [768], P(('dp', 'sp'))
- grad_b_value: float32 [768], P(('dp', 'sp'))
- grad_w_out: float32 [768, 768], P(('dp', 'sp'))
- grad_b_out: float32 [768], P(('dp', 'sp'))
- grad_ln2_gain: float32 [768], P(('dp', 'sp'))
- grad_ln2_bias: float32 [768], P(('dp', 'sp'))
- grad_w_fc: float32 [768, 3072], P(('dp', 'sp'))
- grad_b_fc: float32 [3072], P(('dp', 'sp'))
- grad_w_proj: float32 [3072, 768], P(('dp', 'sp'))
- grad_b_proj: float32 [768], P(('dp', 'sp'))
The draws below stay inside these ranges and needn't reach their ends.
Inputs may be any that keep to these rules, and one draw needn't show every extreme that they name: seq_cut[m, g] is where the second sequence of pack g in micro-batch m begins; the value 512 means that the pack holds one sequence.
All inputs are finite; a program needn't handle non-finite values.
Results may differ from the reference program's by a relative error of at most 0.014.
Values may be sent and summed in bfloat16 or wider, within the bound.
A program may use at most 256 MiB of HBM per device.

```python
import jax
import jax.numpy as jnp
from jax import lax

D = 768
HEADS = 12
HEAD = 64
FF = 3072
MICRO = 4
GROUP_TOK = 512
GROUPS = 8
TOKENS = 4096


def draw_seq_cut(key, part):
    cuts = jax.random.randint(key, (MICRO, GROUPS), GROUP_TOK // 4, GROUP_TOK + 1)
    cuts = cuts.at[0, 0].set(GROUP_TOK)
    cuts = cuts.at[MICRO - 1, GROUPS - 1].set(GROUP_TOK // 4)
    return cuts.astype(jnp.int32)


def spiked(array, rng, source, target, shards_of, factor):
    def block_of(axis_at):
        return (jnp.arange(array.shape[axis_at]) // (array.shape[axis_at] // shards_of)).reshape((-1,) + (1,) * (array.ndim - 1 - axis_at))

    one_side = jax.random.permutation(rng, shards_of)[block_of(target)]
    far = (block_of(target) + shards_of // 2) % shards_of
    return jnp.where((block_of(source) == one_side) | (block_of(source) == far), factor * array, array)


def shard_levels(stream_key, dims, shards, least, top_value):
    def one(dim, blocks):
        steps = jax.random.uniform(jax.random.fold_in(jax.random.fold_in(stream_key, 6), dim), (blocks,), jnp.float32, least / len(shards), top_value / len(shards))
        return jnp.repeat(jnp.exp(steps), dims[dim] // blocks).reshape((-1,) + (1,) * (len(dims) - dim - 1))

    factor_of = one(*shards[0])
    for cut in shards[1:]:
        factor_of = factor_of * one(*cut)
    return factor_of


def bell_draw(rng, dims, scale, most, split=(), dtype=jnp.bfloat16):
    drawn = scale * jax.random.normal(rng, dims, jnp.float32)
    if split:
        drawn = drawn * shard_levels(rng, dims, split, -0.22, 0.18)
    return jnp.clip(drawn, -most, most).astype(dtype)


def heavy_noise(stream_key, dims, deviation, most, split, heavy, kind=jnp.bfloat16):
    values = deviation * jax.random.normal(stream_key, dims, jnp.float32)
    if split:
        values = values * shard_levels(stream_key, dims, split, -0.22, 0.18)
    return jnp.clip(spiked(values, jax.random.fold_in(stream_key, 3), *heavy), -most, most).astype(kind)


def setup_inputs(seed: int = 0) -> dict:
    keys = jax.random.split(jax.random.key(seed), 17)
    tokens = bell_draw(keys[0], (MICRO, TOKENS, D), 1.0, 6.0, ((1, 32),))
    cotangent = heavy_noise(keys[1], (MICRO, TOKENS, D), 1.0, 6.0, ((1, 32),), (1, 2, 32, 2.75))
    seq_cut = draw_seq_cut(jax.random.fold_in(keys[16], 71), 0)
    ln1_gain = jnp.clip(1.0 + 0.1 * jax.random.normal(keys[3], (D,), jnp.float32), 0.5, 1.5).astype(jnp.bfloat16)
    ln1_bias = bell_draw(keys[4], (D,), 0.2, 3.0, ((0, 32),))
    w_qkv = bell_draw(keys[5], (D, 3 * D), D ** -0.5, 0.21875, ((0, 32),))
    b_query = bell_draw(keys[6], (D,), 0.3, 4.0, ((0, 32),))
    b_value = bell_draw(keys[7], (D,), 0.05, 0.75, ((0, 32),))
    w_out = bell_draw(keys[8], (D, D), 1 ** -0.5, 6.0, ((0, 32),))
    b_out = bell_draw(keys[9], (D,), 0.5, 6.0, ((0, 32),))
    ln2_gain = jnp.clip(1.0 + 0.1 * jax.random.normal(keys[10], (D,), jnp.float32), 0.5, 1.5).astype(jnp.bfloat16)
    ln2_bias = bell_draw(keys[11], (D,), 0.2, 3.0, ((0, 32),))
    w_fc = bell_draw(keys[12], (D, FF), D ** -0.5, 0.21875, ((0, 32),))
    b_fc = bell_draw(keys[13], (FF,), 0.3, 4.0, ((0, 32),))
    w_proj = bell_draw(keys[14], (FF, D), 64 ** -0.5, 0.75, ((0, 32),))
    b_proj = bell_draw(keys[15], (D,), 0.5, 6.0, ((0, 32),))
    return dict(tokens=tokens, cotangent=cotangent, seq_cut=seq_cut, ln1_gain=ln1_gain, ln1_bias=ln1_bias, w_qkv=w_qkv, b_query=b_query, b_value=b_value, w_out=w_out, b_out=b_out, ln2_gain=ln2_gain, ln2_bias=ln2_bias, w_fc=w_fc, b_fc=b_fc, w_proj=w_proj, b_proj=b_proj)


@jax.custom_vjp
def low(v):
    return lax.optimization_barrier(v.astype(jnp.bfloat16)).astype(jnp.float32)

@jax.custom_vjp
def low_back(v):
    return v

def low_keep(v):
    return (low(v), None)

def low_pass(kept, grad):
    return (grad,)

def back_keep(v):
    return (v, None)

def back_low(kept, grad):
    return (low(grad),)
low.defvjp(low_keep, low_pass)
low_back.defvjp(back_keep, back_low)
EPSILON = 1e-05
BRANCH = 24.0 ** (-0.5)
NEGATIVE = -1e+30

def norm_rows(rows, gain, offset):
    center = lax.optimization_barrier(jnp.mean(rows, axis=-1, keepdims=True))
    centred = rows - center
    spread = lax.optimization_barrier(jnp.mean(centred * centred, axis=-1, keepdims=True))
    return centred * lax.rsqrt(spread + EPSILON) * gain + offset

def layer_forward(rows, params, split_at):
    gain_one, bias_one, w_joint, bias_query, bias_value, w_mix, bias_mix, gain_two, bias_two, w_up, bias_up, w_down, bias_down = params
    highest = lax.Precision.HIGHEST
    normed = norm_rows(rows, gain_one, bias_one)
    joint_bias = jnp.concatenate([bias_query, jnp.zeros_like(bias_query), bias_value])
    joint = low_back(low(jnp.dot(low(normed), w_joint, precision=highest) + joint_bias))
    queries = joint[:, :D].reshape(GROUP_TOK, HEADS, HEAD).transpose(1, 0, 2)
    keys_all = joint[:, D:2 * D].reshape(GROUP_TOK, HEADS, HEAD).transpose(1, 0, 2)
    values_all = joint[:, 2 * D:].reshape(GROUP_TOK, HEADS, HEAD).transpose(1, 0, 2)
    scores = low_back(jnp.einsum('hqd,hkd->hqk', queries, keys_all, precision=highest) * HEAD ** (-0.5))
    positions = lax.iota(jnp.int32, GROUP_TOK)
    causal = positions[None, :] <= positions[:, None]
    same_doc = (positions[None, :] >= split_at) == (positions[:, None] >= split_at)
    scores = jnp.where((causal & same_doc)[None], scores, NEGATIVE)
    probs = low(jax.nn.softmax(scores, axis=-1))
    attended = jnp.einsum('hqk,hkd->hqd', probs, values_all, precision=highest)
    attended = attended.transpose(1, 0, 2).reshape(GROUP_TOK, D)
    attended = low_back(low(attended))
    mixed = low_back(jnp.dot(attended, w_mix, precision=highest) + bias_mix)
    hidden = rows + BRANCH * mixed
    normed_two = low(norm_rows(hidden, gain_two, bias_two))
    pre_act = low_back(jnp.dot(normed_two, w_up, precision=highest) + bias_up)
    activated = low(jax.nn.gelu(pre_act, approximate=True))
    down = low_back(jnp.dot(activated, w_down, precision=highest) + bias_down)
    return hidden + BRANCH * down

def reference(tokens, cotangent, seq_cut, ln1_gain, ln1_bias, w_qkv, b_query, b_value, w_out, b_out, ln2_gain, ln2_bias, w_fc, b_fc, w_proj, b_proj):
    params32 = (ln1_gain.astype(jnp.float32), ln1_bias.astype(jnp.float32), w_qkv.astype(jnp.float32), b_query.astype(jnp.float32), b_value.astype(jnp.float32), w_out.astype(jnp.float32), b_out.astype(jnp.float32), ln2_gain.astype(jnp.float32), ln2_bias.astype(jnp.float32), w_fc.astype(jnp.float32), b_fc.astype(jnp.float32), w_proj.astype(jnp.float32), b_proj.astype(jnp.float32))
    packs = tokens.astype(jnp.float32).reshape(MICRO * GROUPS, GROUP_TOK, D)
    grad_packs = cotangent.astype(jnp.float32).reshape(MICRO * GROUPS, GROUP_TOK, D)
    splits = seq_cut.reshape(MICRO * GROUPS).astype(jnp.int32)

    def one_pack(carried, item):
        pack_rows, grad_rows, split_at = item

        def apply_layer(rows, params):
            return layer_forward(rows, params, split_at)
        result, pull_back = jax.vjp(apply_layer, pack_rows, params32)
        grad_input, grad_params = pull_back(grad_rows)
        carried = tuple((earlier + latest for earlier, latest in zip(carried, grad_params)))
        return (carried, (result.astype(jnp.bfloat16), grad_input))
    initial = tuple((jnp.zeros_like(weight) for weight in params32))
    summed, (results, grads_in) = lax.scan(one_pack, initial, (packs, grad_packs, splits))
    return (results.reshape(MICRO, TOKENS, D), grads_in.reshape(MICRO, TOKENS, D), summed[0], summed[1], summed[2], summed[3], summed[4], summed[5], summed[6], summed[7], summed[8], summed[9], summed[10], summed[11], summed[12])
```

```python
import jax
import jax.numpy as jnp
from jax import lax
from jax.sharding import PartitionSpec as P

HEADS = 12
HEAD = 64
EPSILON = 1e-05
BRANCH = 24.0 ** (-0.5)
NEGATIVE = -1e30
GELU_A = 0.7978845608028654
GELU_B = 0.044715
AXES = ("dp", "sp")
F32 = jnp.float32
BF16 = jnp.bfloat16


def dot(a, b, dims):
    return lax.dot_general(a, b, (dims, ((), ())), preferred_element_type=F32)


def mm(a, b):
    return dot(a, b, ((1,), (0,)))


def mm_nt(a, b):
    return dot(a, b, ((1,), (1,)))


def mm_tn(a, b):
    return dot(a, b, ((0,), (0,)))


def norm_stats(rows):
    center = jnp.mean(rows, axis=-1, keepdims=True)
    centred = rows - center
    inverse = lax.rsqrt(jnp.mean(centred * centred, axis=-1, keepdims=True) + EPSILON)
    return centred * inverse, inverse


def norm_back(xhat, inverse, grad):
    mean_grad = jnp.mean(grad, axis=-1, keepdims=True)
    mean_proj = jnp.mean(grad * xhat, axis=-1, keepdims=True)
    return inverse * (grad - mean_grad - xhat * mean_proj)


def split_heads(rows):
    return rows.reshape(rows.shape[0], HEADS, HEAD).transpose(1, 0, 2)


def join_heads(heads):
    return heads.transpose(1, 0, 2).reshape(heads.shape[1], HEADS * HEAD)


def layer(x16, dy16, cut, big, small):
    w_qkv, w_out, w_fc, w_proj = big
    g1, o1, bq, bv, bo, g2, o2, bf, bp = [v.astype(F32)[None] for v in small]
    length = x16.shape[0]
    x = x16.astype(F32)
    xhat1, inv1 = norm_stats(x)
    h1 = (xhat1 * g1 + o1).astype(BF16)
    bias = jnp.concatenate([bq, jnp.zeros_like(bq), bv], axis=1)
    qkv = (mm(h1, w_qkv) + bias).astype(BF16)
    width = HEADS * HEAD
    q, k, v = (split_heads(qkv[:, i * width : (i + 1) * width]) for i in range(3))
    pos = lax.iota(jnp.int32, length)
    allowed = (pos[None, :] <= pos[:, None]) & ((pos[None, :] >= cut) == (pos[:, None] >= cut))
    scale = HEAD ** (-0.5)
    scores = jnp.einsum("hqd,hkd->hqk", q, k, preferred_element_type=F32) * scale
    scores = jnp.where(allowed[None], scores, NEGATIVE)
    top = jnp.max(scores, axis=-1, keepdims=True)
    expo = jnp.exp(scores - top)
    prob32 = expo / jnp.sum(expo, axis=-1, keepdims=True)
    prob = prob32.astype(BF16)
    attn32 = jnp.einsum("hqk,hkd->hqd", prob, v, preferred_element_type=F32)
    attn = join_heads(attn32).astype(BF16)
    x1 = x + BRANCH * (mm(attn, w_out) + bo)
    xhat2, inv2 = norm_stats(x1)
    h2 = (xhat2 * g2 + o2).astype(BF16)
    pre = mm(h2, w_fc) + bf
    t = jnp.tanh(GELU_A * (pre + GELU_B * pre * pre * pre))
    act = (0.5 * pre * (1 + t)).astype(BF16)
    slope = 0.5 * (1 + t) + 0.5 * pre * (1 - t * t) * (GELU_A * (1 + 3 * GELU_B * pre * pre))
    out = (x1 + BRANCH * (mm(act, w_proj) + bp)).astype(BF16)

    dy = dy16.astype(F32)
    d_mlp = (dy * BRANCH).astype(BF16)
    g_w_proj = mm_tn(act, d_mlp)
    g_b_proj = jnp.sum(d_mlp.astype(F32), axis=0)
    d_pre = (mm_nt(d_mlp, w_proj) * slope).astype(BF16)
    g_w_fc = mm_tn(h2, d_pre)
    g_b_fc = jnp.sum(d_pre.astype(F32), axis=0)
    d_h2 = mm_nt(d_pre, w_fc)
    g_g2 = jnp.sum(d_h2 * xhat2, axis=0)
    g_o2 = jnp.sum(d_h2, axis=0)
    d_x1 = dy + norm_back(xhat2, inv2, d_h2 * g2)
    d_branch = (d_x1 * BRANCH).astype(BF16)
    g_w_out = mm_tn(attn, d_branch)
    g_b_out = jnp.sum(d_branch.astype(F32), axis=0)
    d_attn = split_heads(mm_nt(d_branch, w_out).astype(BF16))
    delta = jnp.sum(d_attn.astype(F32) * attn32, axis=-1, keepdims=True)
    d_prob = jnp.einsum("hqd,hkd->hqk", d_attn, v, preferred_element_type=F32)
    d_scores = (prob32 * (d_prob - delta)).astype(BF16)
    d_q = jnp.einsum("hqk,hkd->hqd", d_scores, k, preferred_element_type=F32) * scale
    d_k = jnp.einsum("hqk,hqd->hkd", d_scores, q, preferred_element_type=F32) * scale
    d_v = jnp.einsum("hqk,hqd->hkd", prob, d_attn, preferred_element_type=F32)
    d_qkv = jnp.concatenate([join_heads(d_q), join_heads(d_k), join_heads(d_v)], axis=1).astype(BF16)
    g_w_qkv = mm_tn(h1, d_qkv)
    g_b_qkv = jnp.sum(d_qkv.astype(F32), axis=0)
    d_h1 = mm_nt(d_qkv, w_qkv)
    g_g1 = jnp.sum(d_h1 * xhat1, axis=0)
    g_o1 = jnp.sum(d_h1, axis=0)
    d_x = d_x1 + norm_back(xhat1, inv1, d_h1 * g1)
    big_grads = (g_w_qkv, g_w_out, g_w_fc, g_w_proj)
    small_grads = (g_g1, g_o1, g_b_qkv[:width], g_b_qkv[2 * width :], g_b_out, g_g2, g_o2, g_b_fc, g_b_proj)
    return out, d_x, big_grads, small_grads


def local(tokens, cotangent, seq_cut, g1, o1, w_qkv, bq, bv, w_out, bo, g2, o2, w_fc, bf, w_proj, bp):
    ways = lax.axis_size("sp")
    devices = ways * lax.axis_size("dp")
    small = (g1, o1, bq, bv, bo, g2, o2, bf, bp)
    sizes = [v.shape[0] for v in small]
    big = [lax.all_gather(w, AXES, axis=0, tiled=True) for w in (w_qkv, w_out, w_fc, w_proj)]
    packed = lax.all_gather(jnp.concatenate(small), AXES, axis=0)
    cuts = [sum(sizes[:i]) for i in range(len(sizes) + 1)]
    vectors = [packed[:, a:b].reshape(-1) for a, b in zip(cuts[:-1], cuts[1:])]
    x16 = lax.all_to_all(tokens, "sp", split_axis=0, concat_axis=1, tiled=True)
    dy16 = lax.all_to_all(cotangent, "sp", split_axis=0, concat_axis=1, tiled=True)
    packs = x16.shape[0]
    first = lax.axis_index("sp") * packs
    outs, grads_in, big_sum, small_sum = [], [], None, None
    for i in range(packs):
        cut = lax.dynamic_slice(seq_cut, (first + i, 0), (1, 1))[0, 0]
        out, d_x, bigs, smalls = layer(x16[i], dy16[i], cut, big, vectors)
        outs.append(out)
        grads_in.append(d_x)
        big_sum = bigs if big_sum is None else [a + b for a, b in zip(big_sum, bigs)]
        small_sum = smalls if small_sum is None else [a + b for a, b in zip(small_sum, smalls)]
    out = lax.all_to_all(jnp.stack(outs), "sp", split_axis=1, concat_axis=0, tiled=True)
    d_x = lax.all_to_all(jnp.stack(grads_in), "sp", split_axis=1, concat_axis=0, tiled=True)
    big_out = [
        lax.psum_scatter(g.astype(BF16), AXES, scatter_dimension=0, tiled=True).astype(F32) for g in big_sum
    ]
    small_pack = jnp.concatenate([g.reshape(devices, -1) for g in small_sum], axis=1)
    small_out = lax.psum_scatter(small_pack, AXES, scatter_dimension=0, tiled=True)[0]
    s = [small_out[a:b] for a, b in zip(cuts[:-1], cuts[1:])]
    return (out, d_x, s[0], s[1], big_out[0], s[2], s[3], big_out[1], s[4], s[5], s[6], big_out[2], s[7], big_out[3], s[8])


def solution(mesh):
    row = P(AXES, None)
    vec = P(AXES)
    act = P(None, AXES, None)
    return jax.shard_map(
        local,
        mesh=mesh,
        in_specs=(act, act, P(None, "dp"), vec, vec, row, vec, vec, row, vec, vec, vec, row, vec, row, vec),
        out_specs=(act, act, vec, vec, row, vec, vec, row, vec, vec, vec, row, vec, row, vec),
        check_vma=False,
    )
```

```python
import functools

import jax
import jax.numpy as jnp
from jax import lax
from jax.experimental import pallas as pl
from jax.experimental.pallas import tpu as pltpu
from jax.sharding import PartitionSpec as P

HEADS = 12
HEAD = 64
EPSILON = 1e-05
BRANCH = 24.0 ** (-0.5)
NEGATIVE = -1e30
GELU_A = 0.7978845608028654
GELU_B = 0.044715
AXES = ("dp", "sp")
F32 = jnp.float32
BF16 = jnp.bfloat16
MESH = pl.DeviceIdType.MESH

def dot(a, b, dims):
    return lax.dot_general(a, b, (dims, ((), ())), preferred_element_type=F32)


def mm(a, b):
    return dot(a, b, ((1,), (0,)))


def mm_nt(a, b):
    return dot(a, b, ((1,), (1,)))


def mm_tn(a, b):
    return dot(a, b, ((0,), (0,)))


def norm_stats(rows):
    center = jnp.mean(rows, axis=-1, keepdims=True)
    centred = rows - center
    inverse = lax.rsqrt(jnp.mean(centred * centred, axis=-1, keepdims=True) + EPSILON)
    return centred * inverse, inverse


def norm_back(xhat, inverse, grad):
    mean_grad = jnp.mean(grad, axis=-1, keepdims=True)
    mean_proj = jnp.mean(grad * xhat, axis=-1, keepdims=True)
    return inverse * (grad - mean_grad - xhat * mean_proj)


def split_heads(rows):
    return rows.reshape(rows.shape[0], HEADS, HEAD).transpose(1, 0, 2)


def join_heads(heads):
    return heads.transpose(1, 0, 2).reshape(heads.shape[1], HEADS * HEAD)


def layer(x16, dy16, cut, big, small):
    w_qkv, w_out, w_fc, w_proj = big
    g1, o1, bq, bv, bo, g2, o2, bf, bp = [v.astype(F32)[None] for v in small]
    length = x16.shape[0]
    x = x16.astype(F32)
    xhat1, inv1 = norm_stats(x)
    h1 = (xhat1 * g1 + o1).astype(BF16)
    bias = jnp.concatenate([bq, jnp.zeros_like(bq), bv], axis=1)
    qkv = (mm(h1, w_qkv) + bias).astype(BF16)
    width = HEADS * HEAD
    q, k, v = (split_heads(qkv[:, i * width : (i + 1) * width]) for i in range(3))
    pos = lax.iota(jnp.int32, length)
    allowed = (pos[None, :] <= pos[:, None]) & ((pos[None, :] >= cut) == (pos[:, None] >= cut))
    scale = HEAD ** (-0.5)
    scores = jnp.einsum("hqd,hkd->hqk", q, k, preferred_element_type=F32) * scale
    scores = jnp.where(allowed[None], scores, NEGATIVE)
    top = jnp.max(scores, axis=-1, keepdims=True)
    expo = jnp.exp(scores - top)
    prob32 = expo / jnp.sum(expo, axis=-1, keepdims=True)
    prob = prob32.astype(BF16)
    attn32 = jnp.einsum("hqk,hkd->hqd", prob, v, preferred_element_type=F32)
    attn = join_heads(attn32).astype(BF16)
    x1 = x + BRANCH * (mm(attn, w_out) + bo)
    xhat2, inv2 = norm_stats(x1)
    h2 = (xhat2 * g2 + o2).astype(BF16)
    pre = mm(h2, w_fc) + bf
    t = jnp.tanh(GELU_A * (pre + GELU_B * pre * pre * pre))
    act = (0.5 * pre * (1 + t)).astype(BF16)
    slope = 0.5 * (1 + t) + 0.5 * pre * (1 - t * t) * (GELU_A * (1 + 3 * GELU_B * pre * pre))
    out = (x1 + BRANCH * (mm(act, w_proj) + bp)).astype(BF16)

    dy = dy16.astype(F32)
    d_mlp = (dy * BRANCH).astype(BF16)
    g_w_proj = mm_tn(act, d_mlp)
    g_b_proj = jnp.sum(d_mlp.astype(F32), axis=0)
    d_pre = (mm_nt(d_mlp, w_proj) * slope).astype(BF16)
    g_w_fc = mm_tn(h2, d_pre)
    g_b_fc = jnp.sum(d_pre.astype(F32), axis=0)
    d_h2 = mm_nt(d_pre, w_fc)
    g_g2 = jnp.sum(d_h2 * xhat2, axis=0)
    g_o2 = jnp.sum(d_h2, axis=0)
    d_x1 = dy + norm_back(xhat2, inv2, d_h2 * g2)
    d_branch = (d_x1 * BRANCH).astype(BF16)
    g_w_out = mm_tn(attn, d_branch)
    g_b_out = jnp.sum(d_branch.astype(F32), axis=0)
    d_attn = split_heads(mm_nt(d_branch, w_out).astype(BF16))
    delta = jnp.sum(d_attn.astype(F32) * attn32, axis=-1, keepdims=True)
    d_prob = jnp.einsum("hqd,hkd->hqk", d_attn, v, preferred_element_type=F32)
    d_scores = (prob32 * (d_prob - delta)).astype(BF16)
    d_q = jnp.einsum("hqk,hkd->hqd", d_scores, k, preferred_element_type=F32) * scale
    d_k = jnp.einsum("hqk,hqd->hkd", d_scores, q, preferred_element_type=F32) * scale
    d_v = jnp.einsum("hqk,hqd->hkd", prob, d_attn, preferred_element_type=F32)
    d_qkv = jnp.concatenate([join_heads(d_q), join_heads(d_k), join_heads(d_v)], axis=1).astype(BF16)
    g_w_qkv = mm_tn(h1, d_qkv)
    g_b_qkv = jnp.sum(d_qkv.astype(F32), axis=0)
    d_h1 = mm_nt(d_qkv, w_qkv)
    g_g1 = jnp.sum(d_h1 * xhat1, axis=0)
    g_o1 = jnp.sum(d_h1, axis=0)
    d_x = d_x1 + norm_back(xhat1, inv1, d_h1 * g1)
    big_grads = (g_w_qkv, g_w_out, g_w_fc, g_w_proj)
    small_grads = (g_g1, g_o1, g_b_qkv[:width], g_b_qkv[2 * width :], g_b_out, g_g2, g_o2, g_b_fc, g_b_proj)
    return out, d_x, big_grads, small_grads


def local(tokens, cotangent, seq_cut, g1, o1, w_qkv, bq, bv, w_out, bo, g2, o2, w_fc, bf, w_proj, bp):
    ways = lax.axis_size("sp")
    devices = ways * lax.axis_size("dp")
    small = (g1, o1, bq, bv, bo, g2, o2, bf, bp)
    sizes = [v.shape[0] for v in small]
    big = [lax.all_gather(w, AXES, axis=0, tiled=True) for w in (w_qkv, w_out, w_fc, w_proj)]
    packed = lax.all_gather(jnp.concatenate(small), AXES, axis=0)
    cuts = [sum(sizes[:i]) for i in range(len(sizes) + 1)]
    vectors = [packed[:, a:b].reshape(-1) for a, b in zip(cuts[:-1], cuts[1:])]
    x16 = lax.all_to_all(tokens, "sp", split_axis=0, concat_axis=1, tiled=True)
    dy16 = lax.all_to_all(cotangent, "sp", split_axis=0, concat_axis=1, tiled=True)
    packs = x16.shape[0]
    first = lax.axis_index("sp") * packs
    outs, grads_in, big_sum, small_sum = [], [], None, None
    for i in range(packs):
        cut = lax.dynamic_slice(seq_cut, (first + i, 0), (1, 1))[0, 0]
        out, d_x, bigs, smalls = layer(x16[i], dy16[i], cut, big, vectors)
        outs.append(out)
        grads_in.append(d_x)
        big_sum = bigs if big_sum is None else [a + b for a, b in zip(big_sum, bigs)]
        small_sum = smalls if small_sum is None else [a + b for a, b in zip(small_sum, smalls)]
    out = lax.all_to_all(jnp.stack(outs), "sp", split_axis=1, concat_axis=0, tiled=True)
    d_x = lax.all_to_all(jnp.stack(grads_in), "sp", split_axis=1, concat_axis=0, tiled=True)
    big_out = [
        lax.psum_scatter(g.astype(BF16), AXES, scatter_dimension=0, tiled=True).astype(F32) for g in big_sum
    ]
    small_pack = jnp.concatenate([g.reshape(devices, -1) for g in small_sum], axis=1)
    small_out = lax.psum_scatter(small_pack, AXES, scatter_dimension=0, tiled=True)[0]
    s = [small_out[a:b] for a, b in zip(cuts[:-1], cuts[1:])]
    return (out, d_x, s[0], s[1], big_out[0], s[2], s[3], big_out[1], s[4], s[5], s[6], big_out[2], s[7], big_out[3], s[8])

T, D, FF, HALF = 512, 768, 3072, 384
ZS = 4
ZA = 3
ROWS = 32


class Bag:
    pass


def rows_loop(count, step, body):
    def one(i, carry):
        body(pl.multiple_of(i * step, step))
        return carry

    lax.fori_loop(0, count // step, one, 0)


def fold8(values):
    return jnp.sum(values.reshape(values.shape[0] // 8, 8, values.shape[1]), axis=0)


def zero_sums(count):
    return tuple(jnp.zeros((8, D), F32) for _ in range(count))


NAMES = (
    "tok", "cot", "cut", "wq", "wo", "wf", "wp", "small", "out_o", "dx_o", "gq_o", "go_o", "gf_o", "gp_o", "gs_o",
    "W", "Wp", "Sw", "sq", "so", "sf", "sp_", "ssm", "vec", "G", "Gp", "rA1", "rB1", "pA1", "pB1", "rA2", "rB2",
    "pA2", "pB2", "rz", "pz", "tot", "ptot", "fr", "pfr", "xb", "cb", "h1c", "qkvb", "attnc", "x1", "h2c", "actc",
    "slope", "dpre_p", "acc", "dbr", "dbr_p", "dml", "dml_p", "dat", "dqp", "ob", "mask", "lse", "lseT", "gsm", "gs",
    "gr", "ssem", "rsem", "lsem",
)
SEMS = 220


def scratch_shapes():
    v = pltpu.VMEM
    return [
        v((8, 2, ZS, 2, 2, 48, HALF), BF16),
        v((2, ZS, 2, 2, 192, HALF), BF16),
        v((2, ZS, 2, 2, 16, HALF), BF16),
        v((24, 3 * D), BF16),
        v((24, D), BF16),
        v((24, FF), BF16),
        v((96, D), BF16),
        v((16, D), BF16),
        v((16, D), F32),
        v((8, ZS, 2, 2, 48, HALF), BF16),
        v((ZS, 2, 2, 192, HALF), BF16),
        v((8, ZA, 2, 48, HALF), BF16),
        v((8, ZS - ZA, 2, 48, HALF), BF16),
        v((ZA, 2, 192, HALF), BF16),
        v((ZS - ZA, 2, 192, HALF), BF16),
        v((8, ZA, 48, HALF), BF16),
        v((8, ZS - ZA, 48, HALF), BF16),
        v((ZA, 192, HALF), BF16),
        v((ZS - ZA, 192, HALF), BF16),
        v((8, 3, 48, HALF), BF16),
        v((3, 192, HALF), BF16),
        v((8, 48, HALF), F32),
        v((192, HALF), F32),
        v((8, 24, HALF), F32),
        v((96, HALF), F32),
        v((4, 128, D), BF16),
        v((4, 128, D), BF16),
        v((2, T, D), BF16),
        v((6, T, HALF), BF16),
        v((2, T, D), BF16),
        v((T, D), F32),
        v((2, T, D), BF16),
        v((2, T, FF), BF16),
        v((T, FF), BF16),
        v((T, FF // 2), BF16),
        v((T, D), F32),
        v((T, D), BF16),
        v((T, HALF), BF16),
        v((T, D), BF16),
        v((T, HALF), BF16),
        v((T, D), BF16),
        v((3, T, HALF), BF16),
        v((T, D), BF16),
        v((T, T), F32),
        v((T, 128), F32),
        v((128, T), F32),
        v((16, D), F32),
        v((3, 16, D), F32),
        v((6, 16, D), F32),
        pltpu.SemaphoreType.DMA((SEMS,)),
        pltpu.SemaphoreType.DMA((SEMS,)),
        pltpu.SemaphoreType.DMA((4,)),
    ]


def mega(*refs):
    r = Bag()
    assert len(refs) == len(NAMES), (len(refs), len(NAMES))
    for name, ref in zip(NAMES, refs):
        setattr(r, name, ref)
    dp, sp = lax.axis_index("dp"), lax.axis_index("sp")
    z, y = dp // 2, lax.rem(dp, 2)
    x, c = sp // 2, lax.rem(sp, 2)
    nx, ny, nc = 1 - x, 1 - y, 1 - c
    partner = {"dp": dp, "sp": x * 2 + nc}
    xpeer = {"dp": dp, "sp": nx * 2 + c}
    ypeer = {"dp": z * 2 + ny, "sp": sp}
    every, low_z, high_z = pl.ds(0, ZS), pl.ds(0, ZA), pl.ds(ZA, ZS - ZA)
    both = pl.ds(0, 2)

    def zshift(k):
        return lax.rem(z + k, ZS)

    def zpeer(k):
        return {"dp": zshift(k) * 2 + y, "sp": sp}

    def speer(k):
        return lax.rem(sp + k, 4)

    table = {}
    started = {}

    def slot(key):
        return table.setdefault(key, len(table))

    def send(key, src, dst, device):
        i = slot(key)
        copy = pltpu.make_async_remote_copy(
            src_ref=src, dst_ref=dst, send_sem=r.ssem.at[i], recv_sem=r.rsem.at[i], device_id=device, device_id_type=MESH
        )
        copy.start()
        started[key] = copy
        return copy

    def arrive(key, dst):
        i = slot(key)
        pltpu.make_async_remote_copy(
            src_ref=dst, dst_ref=dst, send_sem=r.ssem.at[i], recv_sem=r.rsem.at[i], device_id=partner, device_id_type=MESH
        ).wait_recv()

    barrier = pltpu.get_barrier_semaphore()
    peers = [{"dp": dp, "sp": speer(k)} for k in (1, 2, 3)] + [ypeer] + [zpeer(k) for k in (1, 2, 3)]
    for peer in peers:
        pl.semaphore_signal(barrier, inc=1, device_id=peer, device_id_type=MESH)
    pl.semaphore_wait(barrier, len(peers))

    def view(u, h, zs, ys, xs):
        kind, first, count = u
        if kind == "s":
            return r.Sw.at[h, zs, ys, xs]
        if kind == "p":
            return r.Wp.at[h, zs, ys, xs, pl.ds(first, count), :]
        return r.W.at[pl.ds(first, count), h, zs, ys, xs]

    def ag1(u):
        for k in (1, 2, 3):
            v = view(u, c, z, y, x)
            send((u, "z", k), v, v, zpeer(k))

    def ag2(u):
        for k in (1, 2, 3):
            arrive((u, "z", k), view(u, c, zshift(ZS - k), y, x))
        v = view(u, c, low_z, y, x)
        send((u, "2a"), v, v, xpeer)
        v = view(u, c, high_z, y, x)
        send((u, "2b"), v, v, ypeer)
        v = view(u, c, every, y, x)
        send((u, "c0"), v, v, partner)

    def ag3(u):
        arrive((u, "2a"), view(u, c, low_z, y, nx))
        v = view(u, c, low_z, y, both)
        send((u, "3a"), v, v, ypeer)
        arrive((u, "2b"), view(u, c, high_z, ny, x))
        v = view(u, c, high_z, both, x)
        send((u, "3b"), v, v, xpeer)
        v = view(u, c, low_z, y, nx)
        send((u, "c1"), v, v, partner)
        v = view(u, c, high_z, ny, x)
        send((u, "c2"), v, v, partner)

    def ag4(u):
        v = view(u, c, low_z, ny, both)
        arrive((u, "3a"), v)
        send((u, "c3"), v, v, partner)
        v = view(u, c, high_z, both, nx)
        arrive((u, "3b"), v)
        send((u, "c4"), v, v, partner)

    def ag5(u):
        arrive((u, "c0"), view(u, nc, every, y, x))
        arrive((u, "c1"), view(u, nc, low_z, y, nx))
        arrive((u, "c2"), view(u, nc, high_z, ny, x))
        arrive((u, "c3"), view(u, nc, low_z, ny, both))
        arrive((u, "c4"), view(u, nc, high_z, both, nx))

    US = ("s", 0, 16)
    UQ = [("w", i, 1) for i in range(3)]
    UO = ("w", 3, 1)
    UF = [("w", 4, 2), ("w", 6, 2)]
    UP = [("p", 0, 96), ("p", 96, 96)]

    swaps = [("small", r.small, r.ssm), ("wq", r.wq, r.sq), ("wo", r.wo, r.so), ("wf", r.wf, r.sf), ("wp", r.wp, r.sp_)]
    for key, src, dst in swaps:
        send(key, src, dst, partner)

    def send_pack(key, src, dst):
        for k in (1, 2, 3):
            send((key, k), src.at[speer(k)], dst.at[sp], {"dp": dp, "sp": speer(k)})

    send_pack("tok", r.tok, r.xb)
    own_tok = pltpu.make_async_copy(r.tok.at[sp], r.xb.at[sp], r.lsem.at[0])
    own_tok.start()
    own_cot = pltpu.make_async_copy(r.cot.at[sp], r.cb.at[sp], r.lsem.at[1])
    own_cot.start()
    first_core = c == 0

    def pair_rows(own, other, col, width):
        a = own[:, pl.ds(pl.multiple_of(col, 128), width)].astype(F32)
        b = other[:, pl.ds(pl.multiple_of(col, 128), width)].astype(F32)
        return jnp.concatenate([jnp.where(first_core, a, b), jnp.where(first_core, b, a)], axis=0).astype(BF16)

    arrive("small", r.ssm)
    cols = pl.ds(pl.multiple_of(c * HALF, 128), HALF)
    r.Sw[c, z, y, x] = (r.small[:, cols].astype(F32) + r.ssm[:, cols].astype(F32)).astype(BF16)
    ag1(US)
    arrive("wq", r.sq)
    for i in range(3):
        for j in range(3):
            r.W[i, c, z, y, x, :, pl.ds(128 * j, 128)] = pair_rows(r.wq, r.sq, j * D + 128 * (3 * c + i), 128)
        ag1(UQ[i])
    arrive("wo", r.so)
    r.W[3, c, z, y, x] = pair_rows(r.wo, r.so, c * HALF, HALF)
    ag1(UO)
    arrive("wf", r.sf)
    for i in range(4):
        r.W[4 + i, c, z, y, x] = pair_rows(r.wf, r.sf, c * (FF // 2) + i * HALF, HALF)
    ag1(UF[0])
    ag1(UF[1])
    arrive("wp", r.sp_)
    r.Wp[c, z, y, x, pl.ds(pl.multiple_of(96 * c, 32), 96), :] = r.wp[:, cols]
    r.Wp[c, z, y, x, pl.ds(pl.multiple_of(96 * nc, 32), 96), :] = r.sp_[:, cols]
    ag1(UP[0])
    ag1(UP[1])

    def dot(a, b, ca, cb):
        return lax.dot_general(a, b, (((ca,), (cb,)), ((), ())), preferred_element_type=F32)

    def wide(item):
        return jnp.concatenate([r.W[item, h].reshape(D, HALF) for h in (0, 1)], axis=1)

    def tile_x(buf, row):
        return buf[row // 128, pl.ds(pl.multiple_of(lax.rem(row, 128), ROWS), ROWS), :].astype(F32)

    def vrow(i):
        return r.vec[i : i + 1, :]

    def stats(v):
        center = jnp.mean(v, axis=-1, keepdims=True)
        centred = v - center
        inverse = lax.rsqrt(jnp.mean(centred * centred, axis=-1, keepdims=True) + EPSILON)
        return centred * inverse, inverse

    def norm_back(xhat, inverse, grad):
        return inverse * (grad - jnp.mean(grad, axis=-1, keepdims=True) - xhat * jnp.mean(grad * xhat, axis=-1, keepdims=True))

    def build_mask():
        def body(row):
            q = lax.broadcasted_iota(jnp.int32, (ROWS, T), 0) + row
            k = lax.broadcasted_iota(jnp.int32, (ROWS, T), 1)
            cut = r.cut[sp, 0]
            ok = (k <= q) & ((k >= cut) == (q >= cut))
            r.mask[pl.ds(row, ROWS), :] = jnp.where(ok, 0.0, NEGATIVE)

        rows_loop(T, ROWS, body)

    def build_mask_t():
        def body(row):
            k = lax.broadcasted_iota(jnp.int32, (ROWS, T), 0) + row
            q = lax.broadcasted_iota(jnp.int32, (ROWS, T), 1)
            cut = r.cut[sp, 0]
            ok = (k <= q) & ((k >= cut) == (q >= cut))
            r.mask[pl.ds(row, ROWS), :] = jnp.where(ok, 0.0, NEGATIVE)

        rows_loop(T, ROWS, body)

    def small_vectors():
        for h in (0, 1):
            total = jnp.zeros((16, HALF), F32)
            for zz in range(ZS):
                for yy in (0, 1):
                    for xx in (0, 1):
                        total = total + r.Sw[h, zz, yy, xx].astype(F32)
            r.vec[:, pl.ds(h * HALF, HALF)] = total

    def norm_one():
        def body(row):
            xhat, _ = stats(tile_x(r.xb, row))
            r.h1c[0, pl.ds(row, ROWS), :] = (xhat * vrow(0) + vrow(1)).astype(BF16)

        rows_loop(T, ROWS, body)

    def qkv_item(i):
        res = dot(r.h1c[0], wide(i), 1, 0)
        for h in (0, 1):
            p = 3 * h + i
            q = res[:, h * HALF : h * HALF + 128] + r.vec[2:3, 128 * p : 128 * p + 128]
            k = res[:, h * HALF + 128 : h * HALF + 256]
            v = res[:, h * HALF + 256 : h * HALF + 384] + r.vec[3:4, 128 * p : 128 * p + 128]
            r.qkvb[p, :, 0:128] = (q.astype(BF16).astype(F32) * (HEAD**-0.5)).astype(BF16)
            r.qkvb[p, :, 128:256] = k.astype(BF16)
            r.qkvb[p, :, 256:384] = v.astype(BF16)

    QB = 256

    def lane_masks(rows):
        lane = lax.broadcasted_iota(jnp.int32, (rows, 128), 1)
        return lane

    def attend_pair(p):
        lane = lane_masks(QB)

        def block(qb):
            keys = QB * (qb + 1)
            rows = pl.ds(QB * qb, QB)
            q2 = r.qkvb[p, rows, 0:128]
            k2 = r.qkvb[p, 0:keys, 128:256]
            v2 = r.qkvb[p, 0:keys, 256:384]
            outs = []
            for hh in (0, 1):
                mine = (lane < HEAD) if hh == 0 else (lane >= HEAD)
                qm = jnp.where(mine, q2, jnp.zeros_like(q2))
                s = dot(qm, k2, 1, 1) + r.mask[rows, 0:keys]
                top = jnp.max(s, axis=1, keepdims=True)
                e = jnp.exp(s - top)
                total = jnp.sum(e, axis=1, keepdims=True)
                outs.append(dot(e.astype(BF16), v2, 1, 0) / total)
                r.lse[rows, :] = jnp.where(lane == 2 * p + hh, top + jnp.log(total), r.lse[rows, :])
            both_heads = jnp.where(lane < HEAD, outs[0], outs[1]).astype(BF16)
            r.attnc[0, rows, pl.ds(pl.multiple_of(128 * p, 128), 128)] = both_heads

        for qb in range(T // QB):
            block(qb)

    def out_proj():
        r.acc[...] = dot(r.attnc[0], wide(3), 1, 0)

        def body(row):
            v = tile_x(r.xb, row) + BRANCH * (r.acc[pl.ds(row, ROWS), :] + vrow(4))
            r.x1[pl.ds(row, ROWS), :] = v
            xhat, _ = stats(v)
            r.h2c[0, pl.ds(row, ROWS), :] = (xhat * vrow(5) + vrow(6)).astype(BF16)

        rows_loop(T, ROWS, body)

    def up_item(i):
        r.acc[...] = dot(r.h2c[0], wide(4 + i), 1, 0)
        for h in (0, 1):
            col = pl.multiple_of(h * (FF // 2) + i * HALF, 128)
            at = h * 2 + i // 2
            bias = r.vec[pl.ds(8 + at, 1), pl.ds(pl.multiple_of(lax.rem(i, 2) * HALF, 128), HALF)]

            def body(row):
                pre = r.acc[pl.ds(row, ROWS), pl.ds(h * HALF, HALF)] + bias
                square = pre * pre
                t = jnp.tanh(pre * (GELU_A + (GELU_A * GELU_B) * square))
                half_one = 0.5 * (1.0 + t)
                r.actc[0, pl.ds(row, ROWS), pl.ds(col, HALF)] = (pre * half_one).astype(BF16)
                inner = GELU_A + (3.0 * GELU_A * GELU_B) * square
                r.slope[pl.ds(row, ROWS), pl.ds(col, HALF)] = (
                    half_one + (0.5 * pre) * (1.0 - t * t) * inner
                ).astype(BF16)

            rows_loop(T, ROWS, body)

    def wp_group(g):
        return jnp.concatenate([r.Wp[h, g].reshape(D, HALF) for h in (0, 1)], axis=1)

    def group_cols(g):
        return pl.ds(pl.multiple_of(g * D, 128), D)

    def mlp_grad_rows():
        def body(row, sums):
            d = (tile_x(r.cb, row) * BRANCH).astype(BF16)
            r.dml[pl.ds(row, ROWS), :] = d
            return sums + fold8(d.astype(F32))

        sums = lax.fori_loop(0, T // ROWS, lambda i, s: body(pl.multiple_of(i * ROWS, ROWS), s), jnp.zeros((8, D), F32))
        r.gsm[7:8, :] = jnp.sum(sums, axis=0, keepdims=True)

    def layer_out():
        r.acc[...] = dot(r.actc[0, :, 0:D], wp_group(0), 1, 0)

        def group(g, carry):
            r.acc[...] += dot(r.actc[0, :, group_cols(g)], wp_group(g), 1, 0)
            return carry

        lax.fori_loop(1, 4, group, 0)

        def body(row):
            v = r.x1[pl.ds(row, ROWS), :] + BRANCH * (r.acc[pl.ds(row, ROWS), :] + vrow(7))
            r.ob[pl.ds(row, ROWS), :] = v.astype(BF16)

        rows_loop(T, ROWS, body)

    def send_rows(key, dst, sem):
        for k in (1, 2, 3):
            src = r.ob.at[pl.ds(pl.multiple_of(128 * speer(k), 128), 128), :]
            send((key, k), src, dst.at[sp], {"dp": dp, "sp": speer(k)})
        own = pltpu.make_async_copy(r.ob.at[pl.ds(pl.multiple_of(128 * sp, 128), 128), :], dst.at[sp], r.lsem.at[sem])
        own.start()
        return own

    def down_back():
        def group(g, carry):
            r.acc[...] = dot(r.dml[...], wp_group(g), 1, 1)

            def body(i, sums):
                row = pl.multiple_of(i * ROWS, ROWS)
                here = (pl.ds(row, ROWS), group_cols(g))
                d = (r.acc[pl.ds(row, ROWS), :] * r.slope[here].astype(F32)).astype(BF16)
                r.slope[here] = d
                return sums + fold8(d.astype(F32))

            sums = lax.fori_loop(0, T // ROWS, body, jnp.zeros((8, D), F32))
            r.gsm[pl.ds(8 + g, 1), :] = jnp.sum(sums, axis=0, keepdims=True)
            return carry

        lax.fori_loop(0, 4, group, 0)

    def up_back():
        def one(i):
            lhs = jnp.concatenate(
                [r.slope[:, pl.ds(pl.multiple_of(h * (FF // 2) + i * HALF, 128), HALF)] for h in (0, 1)], axis=1
            )
            return dot(lhs, wide(4 + i), 1, 1)

        r.acc[...] = one(0)

        def item(i, carry):
            r.acc[...] += one(i)
            return carry

        lax.fori_loop(1, 4, item, 0)

    def half_cols(ref, core):
        return ref.at[:, pl.ds(pl.multiple_of(core * HALF, 128), HALF)]

    def proj_grad():
        def chunk(f, carry):
            at = pl.ds(pl.multiple_of(f * HALF, 128), HALF)
            res = dot(r.actc[0, :, at], half_cols(r.dml, c)[...], 0, 0) + dot(r.actc[1, :, at], r.dml_p[...], 0, 0)
            r.Gp[f // 2, lax.rem(f, 2)] = res.astype(BF16).reshape(2, 192, HALF)
            return carry

        lax.fori_loop(0, 8, chunk, 0)

    def up_grad(u):
        own = r.slope[:, pl.ds(pl.multiple_of(c * (FF // 2) + u * D, 128), D)]
        res = dot(r.h2c[0], own, 0, 0) + dot(r.h2c[1], r.dpre_p[:, u * D : u * D + D], 0, 0)
        for k in (0, 1):
            r.G[4 + 2 * u + k] = res[:, k * HALF : k * HALF + HALF].astype(BF16).reshape(ZS, 2, 2, 48, HALF)

    def norm_two_back():
        def body(i, sums):
            row = pl.multiple_of(i * ROWS, ROWS)
            here = pl.ds(row, ROWS)
            xhat, inverse = stats(r.x1[here, :])
            d_h2 = r.acc[here, :]
            d_x1 = tile_x(r.cb, row) + norm_back(xhat, inverse, d_h2 * vrow(5))
            r.x1[here, :] = d_x1
            d_branch = (d_x1 * BRANCH).astype(BF16)
            r.dbr[here, :] = d_branch
            return (
                sums[0] + fold8(d_h2 * xhat),
                sums[1] + fold8(d_h2),
                sums[2] + fold8(d_branch.astype(F32)),
            )

        sums = lax.fori_loop(0, T // ROWS, body, zero_sums(3))
        for k, at in enumerate((5, 6, 4)):
            r.gsm[at : at + 1, :] = jnp.sum(sums[k], axis=0, keepdims=True)

    def out_back():
        r.dat[...] = dot(r.dbr[...], wide(3), 1, 1).astype(BF16)

    def out_grad():
        res = dot(r.attnc[0], half_cols(r.dbr, c)[...], 0, 0) + dot(r.attnc[1], r.dbr_p[...], 0, 0)
        r.G[3] = res.astype(BF16).reshape(ZS, 2, 2, 48, HALF)

    def flip_lse():
        r.lseT[...] = jnp.transpose(r.lse[...])

    def attend_back_pair(p):
        KB = 256
        cols = pl.ds(pl.multiple_of(128 * p, 128), 128)
        lane = lane_masks(KB)
        da = r.dat[:, cols]
        prod = da.astype(F32) * r.attnc[0, :, cols].astype(F32)
        pick = jnp.where(
            (lax.broadcasted_iota(jnp.int32, (8, 128), 1) // HEAD) == lax.broadcasted_iota(jnp.int32, (8, 128), 0), 1.0, 0.0
        ).astype(F32)
        delta = lax.dot_general(
            pick, prod, (((1,), (1,)), ((), ())), preferred_element_type=F32, precision=lax.Precision.HIGHEST
        )
        q2 = r.qkvb[p, :, 0:128]
        dq_parts = [None, None]
        results = []
        for kb in (0, 1):
            first = KB * kb
            keys = pl.ds(first, KB)
            k2 = r.qkvb[p, keys, 128:256]
            v2 = r.qkvb[p, keys, 256:384]
            dks, dvs, dqs = [], [], []
            for hh in (0, 1):
                mine = (lane < HEAD) if hh == 0 else (lane >= HEAD)
                km = jnp.where(mine, k2, jnp.zeros_like(k2))
                vm = jnp.where(mine, v2, jnp.zeros_like(v2))
                logs = r.lseT[pl.ds(2 * p + hh, 1), :]
                s = dot(km, q2[first:], 1, 1) + r.mask[keys, first:]
                prob = jnp.exp(s - logs[:, first:])
                dprob = dot(vm, da[first:], 1, 1)
                ds = (prob * (dprob - delta[hh : hh + 1, first:])).astype(BF16)
                dvs.append(dot(prob.astype(BF16), da[first:], 1, 0))
                dks.append(dot(ds, q2[first:], 1, 0))
                dqs.append(dot(ds, km, 0, 0))
            dk = jnp.where(lane < HEAD, dks[0], dks[1]).astype(BF16)
            dv = jnp.where(lane < HEAD, dvs[0], dvs[1]).astype(BF16)
            results.append((dk, dv, dqs[0] + dqs[1]))
        (dk0, dv0, dq0), (dk1, dv1, dq1) = results
        scale = HEAD**-0.5
        dq_low = (dq0[:KB] * scale).astype(BF16)
        dq_high = ((dq0[KB:] + dq1) * scale).astype(BF16)
        r.qkvb[p, 0:KB, 0:128] = dq_low
        r.qkvb[p, KB:T, 0:128] = dq_high
        r.qkvb[p, 0:KB, 128:256] = dk0
        r.qkvb[p, KB:T, 128:256] = dk1
        r.qkvb[p, 0:KB, 256:384] = dv0
        r.qkvb[p, KB:T, 256:384] = dv1
        at = pl.ds(pl.multiple_of(128 * p, 128), 128)
        r.gsm[2:3, at] = jnp.sum(dq_low.astype(F32), axis=0, keepdims=True) + jnp.sum(
            dq_high.astype(F32), axis=0, keepdims=True
        )
        r.gsm[3:4, at] = jnp.sum(dv0.astype(F32), axis=0, keepdims=True) + jnp.sum(
            dv1.astype(F32), axis=0, keepdims=True
        )

    def qkv_grad(i):
        res = dot(r.h1c[0], r.qkvb[3 * c + i], 0, 0) + dot(r.h1c[1], r.dqp[i], 0, 0)
        r.G[i] = res.astype(BF16).reshape(ZS, 2, 2, 48, HALF)

    def qkv_back():
        def one(i):
            lhs = jnp.concatenate([r.qkvb[i], r.qkvb[3 + i]], axis=1)
            return dot(lhs, wide(i), 1, 1)

        r.acc[...] = one(0)

        def item(i, carry):
            r.acc[...] += one(i)
            return carry

        lax.fori_loop(1, 3, item, 0)

    def norm_one_back():
        def body(i, sums):
            row = pl.multiple_of(i * ROWS, ROWS)
            here = pl.ds(row, ROWS)
            xhat, inverse = stats(tile_x(r.xb, row))
            d_h1 = r.acc[here, :]
            d_x = r.x1[here, :] + norm_back(xhat, inverse, d_h1 * vrow(0))
            r.ob[here, :] = d_x.astype(BF16)
            return (sums[0] + fold8(d_h1 * xhat), sums[1] + fold8(d_h1))

        sums = lax.fori_loop(0, T // ROWS, body, zero_sums(2))
        for k, at in enumerate((0, 1)):
            r.gsm[at : at + 1, :] = jnp.sum(sums[k], axis=0, keepdims=True)

    def gview(u, zs, ys, xs):
        kind, first, count = u
        if kind == "p":
            return r.Gp.at[zs, ys, xs, pl.ds(first, count), :]
        return r.G.at[pl.ds(first, count), zs, ys, xs]

    def rview(u, plain, proj):
        kind, first, count = u
        if kind == "p":
            at = (pl.ds(0, proj.shape[0]),) + (pl.ds(0, 2),) * (len(proj.shape) - 3) + (pl.ds(first, count), slice(None))
            return proj.at[at]
        return plain.at[pl.ds(first, count)]

    def add_into(dst, extra):
        dst[...] = (dst[...].astype(F32) + extra[...].astype(F32)).astype(BF16)

    def rs1(u):
        send((u, "r1a"), gview(u, low_z, ny, both), rview(u, r.rA1, r.pA1), ypeer)
        send((u, "r1b"), gview(u, high_z, both, nx), rview(u, r.rB1, r.pB1), xpeer)

    def rs2(u):
        va, vb = rview(u, r.rA1, r.pA1), rview(u, r.rB1, r.pB1)
        arrive((u, "r1a"), va)
        add_into(gview(u, low_z, y, both), va)
        send((u, "r2a"), gview(u, low_z, y, nx), rview(u, r.rA2, r.pA2), xpeer)
        arrive((u, "r1b"), vb)
        add_into(gview(u, high_z, both, x), vb)
        send((u, "r2b"), gview(u, high_z, ny, x), rview(u, r.rB2, r.pB2), ypeer)

    def zslot(u, k):
        kind, first, count = u
        if kind == "p":
            return r.pz.at[k - 1, pl.ds(first, count), :]
        return r.rz.at[pl.ds(first, count), k - 1]

    def rs3(u):
        va, vb = rview(u, r.rA2, r.pA2), rview(u, r.rB2, r.pB2)
        arrive((u, "r2a"), va)
        add_into(gview(u, low_z, y, x), va)
        arrive((u, "r2b"), vb)
        add_into(gview(u, high_z, y, x), vb)
        for k in (1, 2, 3):
            send((u, "rz", k), gview(u, zshift(k), y, x), zslot(u, k), zpeer(k))

    def rs4(u):
        kind, first, count = u
        for k in (1, 2, 3):
            arrive((u, "rz", k), zslot(u, k))
        total = gview(u, z, y, x)[...].astype(F32)
        for k in (1, 2, 3):
            total = total + zslot(u, k)[...].astype(F32)
        if kind == "p":
            r.ptot[pl.ds(first, count), :] = total
        else:
            r.tot[pl.ds(first, count)] = total
            give = pl.ds(pl.multiple_of(24 * nc, 8), 24)
            send((u, "fin"), r.tot.at[pl.ds(first, count), give, :], r.fr.at[pl.ds(first, count)], partner)

    def rs5(u):
        kind, first, count = u
        arrive((u, "fin"), r.fr.at[pl.ds(first, count)])
        keep = pl.ds(pl.multiple_of(24 * c, 8), 24)
        for it in range(first, first + count):
            for core, part in ((c, r.tot[it, keep, :]), (nc, r.fr[it])):
                if it < 3:
                    for j in range(3):
                        at = pl.multiple_of(j * D + 128 * (3 * core + it), 128)
                        r.gq_o[:, pl.ds(at, 128)] = part[:, 128 * j : 128 * j + 128]
                elif it == 3:
                    r.go_o[:, pl.ds(pl.multiple_of(core * HALF, 128), HALF)] = part
                else:
                    at = pl.multiple_of(core * (FF // 2) + (it - 4) * HALF, 128)
                    r.gf_o[:, pl.ds(at, HALF)] = part

    def rs_proj_send():
        give = pl.ds(pl.multiple_of(96 * nc, 32), 96)
        send("pfin", r.ptot.at[give, :], r.pfr, partner)

    def rs_proj_done():
        arrive("pfin", r.pfr)
        keep = pl.ds(pl.multiple_of(96 * c, 32), 96)
        r.gp_o[:, pl.ds(pl.multiple_of(c * HALF, 128), HALF)] = r.ptot[keep, :]
        r.gp_o[:, pl.ds(pl.multiple_of(nc * HALF, 128), HALF)] = r.pfr[...]

    def small_send(key, src, at, peer):
        send(("small", key), src, r.gr.at[at], peer)

    def small_add(keys, first, into):
        total = r.gsm[...] if into is None else r.gs[into]
        for n, key in enumerate(keys):
            arrive(("small", key), r.gr.at[first + n])
            total = total + r.gr[first + n]
        return total

    ag2(US)
    ag2(UQ[0])
    build_mask()
    ag3(US)
    ag2(UQ[1])
    ag3(UQ[0])
    ag4(US)
    ag5(US)
    small_vectors()
    for k in (1, 2, 3):
        arrive(("tok", k), r.xb.at[lax.rem(sp + 4 - k, 4)])
    own_tok.wait()
    norm_one()
    send("h1", r.h1c.at[0], r.h1c.at[1], partner)
    ag2(UQ[2])
    ag3(UQ[1])
    ag4(UQ[0])
    ag2(UO)
    ag3(UQ[2])
    ag4(UQ[1])
    ag5(UQ[0])

    def pairs(body, i):
        def one(h, carry):
            body(3 * h + i)
            return carry

        lax.fori_loop(0, 2, one, 0)

    qkv_item(0)
    pairs(attend_pair, 0)
    ag2(UF[0])
    ag3(UO)
    ag4(UQ[2])
    ag5(UQ[1])
    qkv_item(1)
    pairs(attend_pair, 1)
    ag2(UF[1])
    ag3(UF[0])
    ag4(UO)
    ag5(UQ[2])
    send_pack("cot", r.cot, r.cb)
    qkv_item(2)
    pairs(attend_pair, 2)
    send("attn", r.attnc.at[0], r.attnc.at[1], partner)
    ag2(UP[0])
    ag3(UF[1])
    ag4(UF[0])
    ag5(UO)
    out_proj()
    send("h2", r.h2c.at[0], r.h2c.at[1], partner)
    flip_lse()
    build_mask_t()
    ag2(UP[1])
    ag3(UP[0])
    ag4(UF[1])
    ag5(UF[0])
    for k in (1, 2, 3):
        arrive(("cot", k), r.cb.at[lax.rem(sp + 4 - k, 4)])
    own_cot.wait()
    mlp_grad_rows()
    send("dml", half_cols(r.dml, nc), r.dml_p, partner)

    def up_two(first):
        def one(i, carry):
            up_item(i)
            return carry

        lax.fori_loop(first, first + 2, one, 0)

    up_two(0)
    ag3(UP[1])
    ag4(UP[0])
    ag5(UF[1])
    up_two(2)
    send("act", r.actc.at[0], r.actc.at[1], partner)
    ag4(UP[1])
    arrive("dml", r.dml_p)
    arrive("act", r.actc.at[1])
    proj_grad()
    rs1(UP[0])
    rs1(UP[1])
    ag5(UP[0])
    ag5(UP[1])
    layer_out()
    own_out = send_rows("out", r.out_o, 2)
    down_back()
    send("dpre", r.slope.at[:, pl.ds(pl.multiple_of(nc * (FF // 2), 128), FF // 2)], r.dpre_p, partner)
    rs2(UP[0])
    up_back()
    rs2(UP[1])
    rs3(UP[0])
    arrive("h2", r.h2c.at[1])
    arrive("dpre", r.dpre_p)
    up_grad(0)
    rs1(UF[0])
    rs3(UP[1])
    up_grad(1)
    rs1(UF[1])
    norm_two_back()
    send("dbr", half_cols(r.dbr, nc), r.dbr_p, partner)
    rs2(UF[0])
    rs4(UP[0])
    out_back()
    rs2(UF[1])
    rs3(UF[0])
    rs4(UP[1])
    rs_proj_send()
    arrive("attn", r.attnc.at[1])
    arrive("dbr", r.dbr_p)
    out_grad()
    rs1(UO)
    arrive("h1", r.h1c.at[1])

    def give_qkv(i):
        send(("dq", i), r.qkvb.at[3 * nc + i], r.dqp.at[i], partner)

    pairs(attend_back_pair, 0)
    give_qkv(0)
    rs3(UF[1])
    rs2(UO)
    rs4(UF[0])
    pairs(attend_back_pair, 1)
    give_qkv(1)
    arrive(("dq", 0), r.dqp.at[0])
    qkv_grad(0)
    rs1(UQ[0])
    rs3(UO)
    rs4(UF[1])
    pairs(attend_back_pair, 2)
    give_qkv(2)
    arrive(("dq", 1), r.dqp.at[1])
    qkv_grad(1)
    rs1(UQ[1])
    rs2(UQ[0])
    arrive(("dq", 2), r.dqp.at[2])
    qkv_grad(2)
    rs1(UQ[2])
    rs2(UQ[1])
    rs3(UQ[0])
    rs4(UO)
    qkv_back()
    rs2(UQ[2])
    rs3(UQ[1])
    own_out.wait()
    for k in (1, 2, 3):
        started.pop(("out", k)).wait_send()
    norm_one_back()
    own_dx = send_rows("dx", r.dx_o, 3)
    r.gsm[12:16, :] = jnp.zeros((4, D), F32)
    small_send("core", r.gsm, 0, partner)
    rs3(UQ[2])
    rs4(UQ[0])
    r.gs[0] = small_add(["core"], 0, None)
    small_send("x", r.gs.at[0], 1, xpeer)
    rs5(UF[0])
    rs5(UF[1])
    r.gs[1] = small_add(["x"], 1, 0)
    small_send("y", r.gs.at[1], 2, ypeer)
    rs4(UQ[1])
    rs5(UO)
    rs_proj_done()
    r.gs[2] = small_add(["y"], 2, 1)
    for k in (1, 2, 3):
        small_send(("z", k), r.gs.at[2], 2 + k, zpeer(k))
    rs4(UQ[2])
    rs5(UQ[0])
    rs5(UQ[1])
    r.gs_o[...] = small_add([("z", 1), ("z", 2), ("z", 3)], 3, 2)
    rs5(UQ[2])
    for name, dst in (("out", r.out_o), ("dx", r.dx_o)):
        for k in (1, 2, 3):
            arrive((name, k), dst.at[lax.rem(sp + 4 - k, 4)])
    own_dx.wait()
    for copy in started.values():
        copy.wait_send()
    assert len(table) <= SEMS, len(table)


def fused(tokens, cotangent, seq_cut, g1, o1, w_qkv, bq, bv, w_out, bo, g2, o2, w_fc, bf, w_proj, bp):
    device = lax.axis_index("dp") * 4 + lax.axis_index("sp")
    small = jnp.zeros((16, D), BF16)
    small = lax.dynamic_update_slice(small, jnp.stack([g1, o1, bq, bv, bo, g2, o2, bp]), (0, 24 * device))
    small = lax.dynamic_update_slice(small, bf[None], (8 + device // 8, 96 * (device % 8)))
    vmem = pl.BlockSpec(memory_space=pltpu.VMEM)
    anywhere = pl.BlockSpec(memory_space=pl.ANY)
    s = jax.ShapeDtypeStruct
    out, d_x, gq, go, gf, gp, gs = pl.pallas_call(
        mega,
        out_shape=(
            s((4, 128, D), BF16),
            s((4, 128, D), BF16),
            s((24, 3 * D), F32),
            s((24, D), F32),
            s((24, FF), F32),
            s((96, D), F32),
            s((16, D), F32),
        ),
        in_specs=[anywhere, anywhere, pl.BlockSpec(memory_space=pltpu.SMEM)] + [vmem] * 5,
        out_specs=(anywhere, anywhere) + (vmem,) * 5,
        scratch_shapes=scratch_shapes(),
        compiler_params=pltpu.CompilerParams(collective_id=0, has_side_effects=True, vmem_limit_bytes=67043328),
    )(tokens, cotangent, seq_cut, w_qkv, w_out, w_fc, w_proj, small)
    rows = lax.dynamic_slice(gs, (0, 24 * device), (8, 24))
    g_bf = lax.dynamic_slice(gs, (8 + device // 8, 96 * (device % 8)), (1, 96))[0]
    return (out, d_x.astype(F32), rows[0], rows[1], gq, rows[2], rows[3], go, rows[4], rows[5], rows[6], gf, g_bf, gp, rows[7])


def solution(mesh):
    row = P(AXES, None)
    vec = P(AXES)
    act = P(None, AXES, None)
    body = fused if dict(mesh.shape) == {"dp": 8, "sp": 4} else local
    return jax.shard_map(
        body,
        mesh=mesh,
        in_specs=(act, act, P(None, "dp"), vec, vec, row, vec, vec, row, vec, vec, vec, row, vec, row, vec),
        out_specs=(act, act, vec, vec, row, vec, vec, row, vec, vec, vec, row, vec, row, vec),
        check_vma=False,
    )
```

```python
import functools

import jax
import jax.numpy as jnp
from jax import lax
from jax.experimental import pallas as pl
from jax.experimental.pallas import tpu as pltpu
from jax.sharding import PartitionSpec as P

HEADS = 12
HEAD = 64
EPSILON = 1e-05
BRANCH = 24.0 ** (-0.5)
NEGATIVE = -1e30
GELU_A = 0.7978845608028654
GELU_B = 0.044715
AXES = ("dp", "sp")
F32 = jnp.float32
BF16 = jnp.bfloat16
MESH = pl.DeviceIdType.MESH

def dot(a, b, dims):
    return lax.dot_general(a, b, (dims, ((), ())), preferred_element_type=F32)


def mm(a, b):
    return dot(a, b, ((1,), (0,)))


def mm_nt(a, b):
    return dot(a, b, ((1,), (1,)))


def mm_tn(a, b):
    return dot(a, b, ((0,), (0,)))


def norm_stats(rows):
    center = jnp.mean(rows, axis=-1, keepdims=True)
    centred = rows - center
    inverse = lax.rsqrt(jnp.mean(centred * centred, axis=-1, keepdims=True) + EPSILON)
    return centred * inverse, inverse


def norm_back(xhat, inverse, grad):
    mean_grad = jnp.mean(grad, axis=-1, keepdims=True)
    mean_proj = jnp.mean(grad * xhat, axis=-1, keepdims=True)
    return inverse * (grad - mean_grad - xhat * mean_proj)


def split_heads(rows):
    return rows.reshape(rows.shape[0], HEADS, HEAD).transpose(1, 0, 2)


def join_heads(heads):
    return heads.transpose(1, 0, 2).reshape(heads.shape[1], HEADS * HEAD)


def layer(x16, dy16, cut, big, small):
    w_qkv, w_out, w_fc, w_proj = big
    g1, o1, bq, bv, bo, g2, o2, bf, bp = [v.astype(F32)[None] for v in small]
    length = x16.shape[0]
    x = x16.astype(F32)
    xhat1, inv1 = norm_stats(x)
    h1 = (xhat1 * g1 + o1).astype(BF16)
    bias = jnp.concatenate([bq, jnp.zeros_like(bq), bv], axis=1)
    qkv = (mm(h1, w_qkv) + bias).astype(BF16)
    width = HEADS * HEAD
    q, k, v = (split_heads(qkv[:, i * width : (i + 1) * width]) for i in range(3))
    pos = lax.iota(jnp.int32, length)
    allowed = (pos[None, :] <= pos[:, None]) & ((pos[None, :] >= cut) == (pos[:, None] >= cut))
    scale = HEAD ** (-0.5)
    scores = jnp.einsum("hqd,hkd->hqk", q, k, preferred_element_type=F32) * scale
    scores = jnp.where(allowed[None], scores, NEGATIVE)
    top = jnp.max(scores, axis=-1, keepdims=True)
    expo = jnp.exp(scores - top)
    prob32 = expo / jnp.sum(expo, axis=-1, keepdims=True)
    prob = prob32.astype(BF16)
    attn32 = jnp.einsum("hqk,hkd->hqd", prob, v, preferred_element_type=F32)
    attn = join_heads(attn32).astype(BF16)
    x1 = x + BRANCH * (mm(attn, w_out) + bo)
    xhat2, inv2 = norm_stats(x1)
    h2 = (xhat2 * g2 + o2).astype(BF16)
    pre = mm(h2, w_fc) + bf
    t = jnp.tanh(GELU_A * (pre + GELU_B * pre * pre * pre))
    act = (0.5 * pre * (1 + t)).astype(BF16)
    slope = 0.5 * (1 + t) + 0.5 * pre * (1 - t * t) * (GELU_A * (1 + 3 * GELU_B * pre * pre))
    out = (x1 + BRANCH * (mm(act, w_proj) + bp)).astype(BF16)

    dy = dy16.astype(F32)
    d_mlp = (dy * BRANCH).astype(BF16)
    g_w_proj = mm_tn(act, d_mlp)
    g_b_proj = jnp.sum(d_mlp.astype(F32), axis=0)
    d_pre = (mm_nt(d_mlp, w_proj) * slope).astype(BF16)
    g_w_fc = mm_tn(h2, d_pre)
    g_b_fc = jnp.sum(d_pre.astype(F32), axis=0)
    d_h2 = mm_nt(d_pre, w_fc)
    g_g2 = jnp.sum(d_h2 * xhat2, axis=0)
    g_o2 = jnp.sum(d_h2, axis=0)
    d_x1 = dy + norm_back(xhat2, inv2, d_h2 * g2)
    d_branch = (d_x1 * BRANCH).astype(BF16)
    g_w_out = mm_tn(attn, d_branch)
    g_b_out = jnp.sum(d_branch.astype(F32), axis=0)
    d_attn = split_heads(mm_nt(d_branch, w_out).astype(BF16))
    delta = jnp.sum(d_attn.astype(F32) * attn32, axis=-1, keepdims=True)
    d_prob = jnp.einsum("hqd,hkd->hqk", d_attn, v, preferred_element_type=F32)
    d_scores = (prob32 * (d_prob - delta)).astype(BF16)
    d_q = jnp.einsum("hqk,hkd->hqd", d_scores, k, preferred_element_type=F32) * scale
    d_k = jnp.einsum("hqk,hqd->hkd", d_scores, q, preferred_element_type=F32) * scale
    d_v = jnp.einsum("hqk,hqd->hkd", prob, d_attn, preferred_element_type=F32)
    d_qkv = jnp.concatenate([join_heads(d_q), join_heads(d_k), join_heads(d_v)], axis=1).astype(BF16)
    g_w_qkv = mm_tn(h1, d_qkv)
    g_b_qkv = jnp.sum(d_qkv.astype(F32), axis=0)
    d_h1 = mm_nt(d_qkv, w_qkv)
    g_g1 = jnp.sum(d_h1 * xhat1, axis=0)
    g_o1 = jnp.sum(d_h1, axis=0)
    d_x = d_x1 + norm_back(xhat1, inv1, d_h1 * g1)
    big_grads = (g_w_qkv, g_w_out, g_w_fc, g_w_proj)
    small_grads = (g_g1, g_o1, g_b_qkv[:width], g_b_qkv[2 * width :], g_b_out, g_g2, g_o2, g_b_fc, g_b_proj)
    return out, d_x, big_grads, small_grads


def local(tokens, cotangent, seq_cut, g1, o1, w_qkv, bq, bv, w_out, bo, g2, o2, w_fc, bf, w_proj, bp):
    ways = lax.axis_size("sp")
    devices = ways * lax.axis_size("dp")
    small = (g1, o1, bq, bv, bo, g2, o2, bf, bp)
    sizes = [v.shape[0] for v in small]
    big = [lax.all_gather(w, AXES, axis=0, tiled=True) for w in (w_qkv, w_out, w_fc, w_proj)]
    packed = lax.all_gather(jnp.concatenate(small), AXES, axis=0)
    cuts = [sum(sizes[:i]) for i in range(len(sizes) + 1)]
    vectors = [packed[:, a:b].reshape(-1) for a, b in zip(cuts[:-1], cuts[1:])]
    x16 = lax.all_to_all(tokens, "sp", split_axis=0, concat_axis=1, tiled=True)
    dy16 = lax.all_to_all(cotangent, "sp", split_axis=0, concat_axis=1, tiled=True)
    packs = x16.shape[0]
    first = lax.axis_index("sp") * packs
    outs, grads_in, big_sum, small_sum = [], [], None, None
    for i in range(packs):
        cut = lax.dynamic_slice(seq_cut, (first + i, 0), (1, 1))[0, 0]
        out, d_x, bigs, smalls = layer(x16[i], dy16[i], cut, big, vectors)
        outs.append(out)
        grads_in.append(d_x)
        big_sum = bigs if big_sum is None else [a + b for a, b in zip(big_sum, bigs)]
        small_sum = smalls if small_sum is None else [a + b for a, b in zip(small_sum, smalls)]
    out = lax.all_to_all(jnp.stack(outs), "sp", split_axis=1, concat_axis=0, tiled=True)
    d_x = lax.all_to_all(jnp.stack(grads_in), "sp", split_axis=1, concat_axis=0, tiled=True)
    big_out = [
        lax.psum_scatter(g.astype(BF16), AXES, scatter_dimension=0, tiled=True).astype(F32) for g in big_sum
    ]
    small_pack = jnp.concatenate([g.reshape(devices, -1) for g in small_sum], axis=1)
    small_out = lax.psum_scatter(small_pack, AXES, scatter_dimension=0, tiled=True)[0]
    s = [small_out[a:b] for a, b in zip(cuts[:-1], cuts[1:])]
    return (out, d_x, s[0], s[1], big_out[0], s[2], s[3], big_out[1], s[4], s[5], s[6], big_out[2], s[7], big_out[3], s[8])

T, D, FF, HALF = 512, 768, 3072, 384
ZS = 4
ZA = 3
ROWS = 32


class Bag:
    pass


def rows_loop(count, step, body):
    def one(i, carry):
        body(pl.multiple_of(i * step, step))
        return carry

    lax.fori_loop(0, count // step, one, 0)


def fold8(values):
    return jnp.sum(values.reshape(values.shape[0] // 8, 8, values.shape[1]), axis=0)


def zero_sums(count):
    return tuple(jnp.zeros((8, D), F32) for _ in range(count))


NAMES = (
    "tok", "cot", "cut", "wq", "wo", "wf", "wp", "small", "out_o", "dx_o", "gq_o", "go_o", "gf_o", "gp_o", "gs_o",
    "W", "Wp", "Sw", "sq", "so", "sf", "sp_", "ssm", "vec", "G", "Gp", "rA1", "rB1", "pA1", "pB1", "rA2", "rB2",
    "pA2", "pB2", "rz", "pz", "zL", "yL", "xL", "tot", "ptot", "fr", "pfr", "xb", "cb", "h1c", "qkvb", "attnc", "x1", "h2c", "actc",
    "slope", "dpre_p", "acc", "dbr", "dbr_p", "dml", "dml_p", "dat", "dqp", "ob", "mask", "lse", "lseT", "gsm", "gs",
    "gr", "ssem", "rsem", "lsem",
)
SEMS = 220


def scratch_shapes():
    v = pltpu.VMEM
    return [
        v((8, 2, ZS, 2, 2, 48, HALF), BF16),
        v((2, ZS, 2, 2, 192, HALF), BF16),
        v((2, ZS, 2, 2, 16, HALF), BF16),
        v((24, 3 * D), BF16),
        v((24, D), BF16),
        v((24, FF), BF16),
        v((96, D), BF16),
        v((16, D), BF16),
        v((16, D), F32),
        v((8, ZS, 2, 2, 48, HALF), BF16),
        v((ZS, 2, 2, 192, HALF), BF16),
        v((8, ZA, 2, 48, HALF), BF16),
        v((8, ZS - ZA, 2, 48, HALF), BF16),
        v((ZA, 2, 96, HALF), BF16),
        v((ZS - ZA, 2, 96, HALF), BF16),
        v((8, ZA, 48, HALF), BF16),
        v((8, ZS - ZA, 48, HALF), BF16),
        v((ZA, 96, HALF), BF16),
        v((ZS - ZA, 96, HALF), BF16),
        v((8, 3, 48, HALF), BF16),
        v((3, 96, HALF), BF16),
        v((3, 2, 2, 96, HALF), BF16),
        v((2, 96, HALF), BF16),
        v((96, HALF), BF16),
        v((8, 48, HALF), F32),
        v((192, HALF), F32),
        v((8, 24, HALF), F32),
        v((96, HALF), F32),
        v((4, 128, D), BF16),
        v((4, 128, D), BF16),
        v((2, T, D), BF16),
        v((6, T, HALF), BF16),
        v((2, T, D), BF16),
        v((T, D), F32),
        v((2, T, D), BF16),
        v((2, T, FF), BF16),
        v((T, FF), BF16),
        v((T, FF // 2), BF16),
        v((T, D), F32),
        v((T, D), BF16),
        v((T, HALF), BF16),
        v((T, D), BF16),
        v((T, HALF), BF16),
        v((T, D), BF16),
        v((3, T, HALF), BF16),
        v((T, D), BF16),
        v((T, T), F32),
        v((T, 128), F32),
        v((128, T), F32),
        v((16, D), F32),
        v((3, 16, D), F32),
        v((6, 16, D), F32),
        pltpu.SemaphoreType.DMA((SEMS,)),
        pltpu.SemaphoreType.DMA((SEMS,)),
        pltpu.SemaphoreType.DMA((4,)),
    ]


def mega(*refs):
    r = Bag()
    assert len(refs) == len(NAMES), (len(refs), len(NAMES))
    for name, ref in zip(NAMES, refs):
        setattr(r, name, ref)
    dp, sp = lax.axis_index("dp"), lax.axis_index("sp")
    z, y = dp // 2, lax.rem(dp, 2)
    x, c = sp // 2, lax.rem(sp, 2)
    nx, ny, nc = 1 - x, 1 - y, 1 - c
    partner = {"dp": dp, "sp": x * 2 + nc}
    xpeer = {"dp": dp, "sp": nx * 2 + c}
    ypeer = {"dp": z * 2 + ny, "sp": sp}
    every, low_z, high_z = pl.ds(0, ZS), pl.ds(0, ZA), pl.ds(ZA, ZS - ZA)
    both = pl.ds(0, 2)

    def zshift(k):
        return lax.rem(z + k, ZS)

    def zpeer(k):
        return {"dp": zshift(k) * 2 + y, "sp": sp}

    def speer(k):
        return lax.rem(sp + k, 4)

    table = {}
    started = {}

    def slot(key):
        return table.setdefault(key, len(table))

    def send(key, src, dst, device):
        i = slot(key)
        copy = pltpu.make_async_remote_copy(
            src_ref=src, dst_ref=dst, send_sem=r.ssem.at[i], recv_sem=r.rsem.at[i], device_id=device, device_id_type=MESH
        )
        copy.start()
        started[key] = copy
        return copy

    def arrive(key, dst):
        i = slot(key)
        pltpu.make_async_remote_copy(
            src_ref=dst, dst_ref=dst, send_sem=r.ssem.at[i], recv_sem=r.rsem.at[i], device_id=partner, device_id_type=MESH
        ).wait_recv()

    barrier = pltpu.get_barrier_semaphore()
    peers = [{"dp": dp, "sp": speer(k)} for k in (1, 2, 3)] + [ypeer] + [zpeer(k) for k in (1, 2, 3)]
    for peer in peers:
        pl.semaphore_signal(barrier, inc=1, device_id=peer, device_id_type=MESH)
    pl.semaphore_wait(barrier, len(peers))

    def view(u, h, zs, ys, xs):
        kind, first, count = u
        if kind == "s":
            return r.Sw.at[h, zs, ys, xs]
        if kind in "pl":
            return r.Wp.at[h, zs, ys, xs, pl.ds(first, count), :]
        return r.W.at[pl.ds(first, count), h, zs, ys, xs]

    def ag1(u):
        for k in (1, 2, 3):
            v = view(u, c, z, y, x)
            send((u, "z", k), v, v, zpeer(k))

    def ag2(u):
        for k in (1, 2, 3):
            arrive((u, "z", k), view(u, c, zshift(ZS - k), y, x))
        v = view(u, c, low_z, y, x)
        send((u, "2a"), v, v, xpeer)
        v = view(u, c, high_z, y, x)
        send((u, "2b"), v, v, ypeer)
        v = view(u, c, every, y, x)
        send((u, "c0"), v, v, partner)

    def ag3a(u):
        arrive((u, "2a"), view(u, c, low_z, y, nx))
        v = view(u, c, low_z, y, both)
        send((u, "3a"), v, v, ypeer)
        v = view(u, c, low_z, y, nx)
        send((u, "c1"), v, v, partner)

    def ag3b(u):
        arrive((u, "2b"), view(u, c, high_z, ny, x))
        v = view(u, c, high_z, both, x)
        send((u, "3b"), v, v, xpeer)
        v = view(u, c, high_z, ny, x)
        send((u, "c2"), v, v, partner)

    def ag4a(u):
        v = view(u, c, low_z, ny, both)
        arrive((u, "3a"), v)
        send((u, "c3"), v, v, partner)

    def ag4b(u):
        v = view(u, c, high_z, both, nx)
        arrive((u, "3b"), v)
        send((u, "c4"), v, v, partner)

    def ag5(u):
        arrive((u, "c0"), view(u, nc, every, y, x))
        arrive((u, "c1"), view(u, nc, low_z, y, nx))
        arrive((u, "c2"), view(u, nc, high_z, ny, x))
        arrive((u, "c3"), view(u, nc, low_z, ny, both))
        arrive((u, "c4"), view(u, nc, high_z, both, nx))

    def late1(u):
        v = view(u, c, z, y, x)
        send((u, "lx"), v, v, xpeer)
        send((u, "ly"), v, v, ypeer)

    def late2(u):
        v = view(u, c, z, y, nx)
        arrive((u, "lx"), v)
        send((u, "ld"), v, v, ypeer)

    def late3(u):
        arrive((u, "ly"), view(u, c, z, ny, x))
        arrive((u, "ld"), view(u, c, z, ny, nx))
        v = view(u, c, z, both, both)
        for k in (1, 2, 3):
            send((u, "lz", k), v, v, zpeer(k))
        send((u, "c", 0), v, v, partner)

    def late4(u, k):
        v = view(u, c, zshift(ZS - k), both, both)
        arrive((u, "lz", k), v)
        send((u, "c", k), v, v, partner)

    def late5(u):
        for k in (0, 1, 2, 3):
            arrive((u, "c", k), view(u, nc, zshift(ZS - k), both, both))

    US = ("s", 0, 16)
    UQ = [("w", i, 1) for i in range(3)]
    UO = ("w", 3, 1)
    UF = [("w", 4, 2), ("w", 6, 2)]
    UP = ("p", 0, 96)
    UL = ("l", 96, 96)

    swaps = [("small", r.small, r.ssm), ("wq", r.wq, r.sq), ("wp", r.wp, r.sp_), ("wo", r.wo, r.so), ("wf", r.wf, r.sf)]
    for key, src, dst in swaps:
        send(key, src, dst, partner)

    def send_pack(key, src, dst):
        for k in (2, 1, 3):
            send((key, k), src.at[speer(k)], dst.at[sp], {"dp": dp, "sp": speer(k)})

    own_tok = pltpu.make_async_copy(r.tok.at[sp], r.xb.at[sp], r.lsem.at[0])
    own_tok.start()
    own_cot = pltpu.make_async_copy(r.cot.at[sp], r.cb.at[sp], r.lsem.at[1])
    own_cot.start()
    first_core = c == 0

    def pair_rows(own, other, col, width):
        a = own[:, pl.ds(pl.multiple_of(col, 128), width)].astype(F32)
        b = other[:, pl.ds(pl.multiple_of(col, 128), width)].astype(F32)
        return jnp.concatenate([jnp.where(first_core, a, b), jnp.where(first_core, b, a)], axis=0).astype(BF16)

    arrive("small", r.ssm)
    cols = pl.ds(pl.multiple_of(c * HALF, 128), HALF)
    r.Sw[c, z, y, x] = (r.small[:, cols].astype(F32) + r.ssm[:, cols].astype(F32)).astype(BF16)
    ag1(US)
    arrive("wq", r.sq)
    for i in range(3):
        for j in range(3):
            r.W[i, c, z, y, x, :, pl.ds(128 * j, 128)] = pair_rows(r.wq, r.sq, j * D + 128 * (3 * c + i), 128)
        ag1(UQ[i])
    arrive("wp", r.sp_)
    r.Wp[c, z, y, x, pl.ds(pl.multiple_of(96 * c, 32), 96), :] = r.wp[:, cols]
    r.Wp[c, z, y, x, pl.ds(pl.multiple_of(96 * nc, 32), 96), :] = r.sp_[:, cols]
    arrive("wo", r.so)
    r.W[3, c, z, y, x] = pair_rows(r.wo, r.so, c * HALF, HALF)
    ag1(UO)
    arrive("wf", r.sf)
    for i in range(4):
        r.W[4 + i, c, z, y, x] = pair_rows(r.wf, r.sf, c * (FF // 2) + i * HALF, HALF)
    ag1(UF[0])
    ag1(UF[1])
    ag1(UP)

    def dot(a, b, ca, cb):
        return lax.dot_general(a, b, (((ca,), (cb,)), ((), ())), preferred_element_type=F32)

    def wide(item):
        return jnp.concatenate([r.W[item, h].reshape(D, HALF) for h in (0, 1)], axis=1)

    def tile_x(buf, row):
        return buf[row // 128, pl.ds(pl.multiple_of(lax.rem(row, 128), ROWS), ROWS), :].astype(F32)

    def vrow(i):
        return r.vec[i : i + 1, :]

    def stats(v):
        center = jnp.mean(v, axis=-1, keepdims=True)
        centred = v - center
        inverse = lax.rsqrt(jnp.mean(centred * centred, axis=-1, keepdims=True) + EPSILON)
        return centred * inverse, inverse

    def norm_back(xhat, inverse, grad):
        return inverse * (grad - jnp.mean(grad, axis=-1, keepdims=True) - xhat * jnp.mean(grad * xhat, axis=-1, keepdims=True))

    def build_mask():
        def body(row):
            q = lax.broadcasted_iota(jnp.int32, (ROWS, T), 0) + row
            k = lax.broadcasted_iota(jnp.int32, (ROWS, T), 1)
            cut = r.cut[sp, 0]
            ok = (k <= q) & ((k >= cut) == (q >= cut))
            r.mask[pl.ds(row, ROWS), :] = jnp.where(ok, 0.0, NEGATIVE)

        rows_loop(T, ROWS, body)

    def build_mask_t():
        def body(row):
            k = lax.broadcasted_iota(jnp.int32, (ROWS, T), 0) + row
            q = lax.broadcasted_iota(jnp.int32, (ROWS, T), 1)
            cut = r.cut[sp, 0]
            ok = (k <= q) & ((k >= cut) == (q >= cut))
            r.mask[pl.ds(row, ROWS), :] = jnp.where(ok, 0.0, NEGATIVE)

        rows_loop(T, ROWS, body)

    def small_vectors():
        for h in (0, 1):
            total = jnp.zeros((16, HALF), F32)
            for zz in range(ZS):
                for yy in (0, 1):
                    for xx in (0, 1):
                        total = total + r.Sw[h, zz, yy, xx].astype(F32)
            r.vec[:, pl.ds(h * HALF, HALF)] = total

    def norm_one():
        def body(row):
            xhat, _ = stats(tile_x(r.xb, row))
            r.h1c[0, pl.ds(row, ROWS), :] = (xhat * vrow(0) + vrow(1)).astype(BF16)

        rows_loop(T, ROWS, body)

    def qkv_item(i):
        res = dot(r.h1c[0], wide(i), 1, 0)
        for h in (0, 1):
            p = 3 * h + i
            q = res[:, h * HALF : h * HALF + 128] + r.vec[2:3, 128 * p : 128 * p + 128]
            k = res[:, h * HALF + 128 : h * HALF + 256]
            v = res[:, h * HALF + 256 : h * HALF + 384] + r.vec[3:4, 128 * p : 128 * p + 128]
            r.qkvb[p, :, 0:128] = (q.astype(BF16).astype(F32) * (HEAD**-0.5)).astype(BF16)
            r.qkvb[p, :, 128:256] = k.astype(BF16)
            r.qkvb[p, :, 256:384] = v.astype(BF16)

    QB = 256

    def lane_masks(rows):
        lane = lax.broadcasted_iota(jnp.int32, (rows, 128), 1)
        return lane

    def attend_pair(p):
        lane = lane_masks(QB)

        def block(qb):
            keys = QB * (qb + 1)
            rows = pl.ds(QB * qb, QB)
            q2 = r.qkvb[p, rows, 0:128]
            k2 = r.qkvb[p, 0:keys, 128:256]
            v2 = r.qkvb[p, 0:keys, 256:384]
            outs = []
            for hh in (0, 1):
                mine = (lane < HEAD) if hh == 0 else (lane >= HEAD)
                qm = jnp.where(mine, q2, jnp.zeros_like(q2))
                s = dot(qm, k2, 1, 1) + r.mask[rows, 0:keys]
                top = jnp.max(s, axis=1, keepdims=True)
                e = jnp.exp(s - top)
                total = jnp.sum(e, axis=1, keepdims=True)
                outs.append(dot(e.astype(BF16), v2, 1, 0) / total)
                r.lse[rows, :] = jnp.where(lane == 2 * p + hh, top + jnp.log(total), r.lse[rows, :])
            both_heads = jnp.where(lane < HEAD, outs[0], outs[1]).astype(BF16)
            r.attnc[0, rows, pl.ds(pl.multiple_of(128 * p, 128), 128)] = both_heads

        for qb in range(T // QB):
            block(qb)

    def out_proj():
        r.acc[...] = dot(r.attnc[0], wide(3), 1, 0)

        def body(row):
            v = tile_x(r.xb, row) + BRANCH * (r.acc[pl.ds(row, ROWS), :] + vrow(4))
            r.x1[pl.ds(row, ROWS), :] = v
            xhat, _ = stats(v)
            r.h2c[0, pl.ds(row, ROWS), :] = (xhat * vrow(5) + vrow(6)).astype(BF16)

        rows_loop(T, ROWS, body)

    def up_item(i):
        r.acc[...] = dot(r.h2c[0], wide(4 + i), 1, 0)
        for h in (0, 1):
            col = pl.multiple_of(h * (FF // 2) + i * HALF, 128)
            at = h * 2 + i // 2
            bias = r.vec[pl.ds(8 + at, 1), pl.ds(pl.multiple_of(lax.rem(i, 2) * HALF, 128), HALF)]

            def body(row):
                pre = r.acc[pl.ds(row, ROWS), pl.ds(h * HALF, HALF)] + bias
                square = pre * pre
                t = jnp.tanh(pre * (GELU_A + (GELU_A * GELU_B) * square))
                half_one = 0.5 * (1.0 + t)
                r.actc[0, pl.ds(row, ROWS), pl.ds(col, HALF)] = (pre * half_one).astype(BF16)
                inner = GELU_A + (3.0 * GELU_A * GELU_B) * square
                r.slope[pl.ds(row, ROWS), pl.ds(col, HALF)] = (
                    half_one + (0.5 * pre) * (1.0 - t * t) * inner
                ).astype(BF16)

            rows_loop(T, ROWS, body)

    def wp_group(g):
        return jnp.concatenate([r.Wp[h, g].reshape(D, HALF) for h in (0, 1)], axis=1)

    def group_cols(g):
        return pl.ds(pl.multiple_of(g * D, 128), D)

    def mlp_grad_rows():
        def body(row, sums):
            d = (tile_x(r.cb, row) * BRANCH).astype(BF16)
            r.dml[pl.ds(row, ROWS), :] = d
            return sums + fold8(d.astype(F32))

        sums = lax.fori_loop(0, T // ROWS, lambda i, s: body(pl.multiple_of(i * ROWS, ROWS), s), jnp.zeros((8, D), F32))
        r.gsm[7:8, :] = jnp.sum(sums, axis=0, keepdims=True)

    def layer_out():
        r.acc[...] = dot(r.actc[0, :, 0:D], wp_group(0), 1, 0)

        def group(g, carry):
            r.acc[...] += dot(r.actc[0, :, group_cols(g)], wp_group(g), 1, 0)
            return carry

        lax.fori_loop(1, 4, group, 0)

        def body(row):
            v = r.x1[pl.ds(row, ROWS), :] + BRANCH * (r.acc[pl.ds(row, ROWS), :] + vrow(7))
            r.ob[pl.ds(row, ROWS), :] = v.astype(BF16)

        rows_loop(T, ROWS, body)

    def send_rows(key, dst, sem):
        for k in (1, 2, 3):
            src = r.ob.at[pl.ds(pl.multiple_of(128 * speer(k), 128), 128), :]
            send((key, k), src, dst.at[sp], {"dp": dp, "sp": speer(k)})
        own = pltpu.make_async_copy(r.ob.at[pl.ds(pl.multiple_of(128 * sp, 128), 128), :], dst.at[sp], r.lsem.at[sem])
        own.start()
        return own

    def down_back():
        def group(g, carry):
            r.acc[...] = dot(r.dml[...], wp_group(g), 1, 1)

            def body(i, sums):
                row = pl.multiple_of(i * ROWS, ROWS)
                here = (pl.ds(row, ROWS), group_cols(g))
                d = (r.acc[pl.ds(row, ROWS), :] * r.slope[here].astype(F32)).astype(BF16)
                r.slope[here] = d
                return sums + fold8(d.astype(F32))

            sums = lax.fori_loop(0, T // ROWS, body, jnp.zeros((8, D), F32))
            r.gsm[pl.ds(8 + g, 1), :] = jnp.sum(sums, axis=0, keepdims=True)
            return carry

        lax.fori_loop(0, 4, group, 0)

    def up_back():
        def one(i):
            lhs = jnp.concatenate(
                [r.slope[:, pl.ds(pl.multiple_of(h * (FF // 2) + i * HALF, 128), HALF)] for h in (0, 1)], axis=1
            )
            return dot(lhs, wide(4 + i), 1, 1)

        r.acc[...] = one(0)

        def item(i, carry):
            r.acc[...] += one(i)
            return carry

        lax.fori_loop(1, 4, item, 0)

    def half_cols(ref, core):
        return ref.at[:, pl.ds(pl.multiple_of(core * HALF, 128), HALF)]

    def proj_grad(first):
        def chunk(f, carry):
            at = pl.ds(pl.multiple_of(f * HALF, 128), HALF)
            res = dot(r.actc[0, :, at], half_cols(r.dml, c)[...], 0, 0) + dot(r.actc[1, :, at], r.dml_p[...], 0, 0)
            r.Gp[f // 2, lax.rem(f, 2)] = res.astype(BF16).reshape(2, 192, HALF)
            return carry

        lax.fori_loop(first, first + 4, chunk, 0)

    def up_grad(u):
        own = r.slope[:, pl.ds(pl.multiple_of(c * (FF // 2) + u * D, 128), D)]
        res = dot(r.h2c[0], own, 0, 0) + dot(r.h2c[1], r.dpre_p[:, u * D : u * D + D], 0, 0)
        for k in (0, 1):
            r.G[4 + 2 * u + k] = res[:, k * HALF : k * HALF + HALF].astype(BF16).reshape(ZS, 2, 2, 48, HALF)

    def norm_two_back():
        def body(i, sums):
            row = pl.multiple_of(i * ROWS, ROWS)
            here = pl.ds(row, ROWS)
            xhat, inverse = stats(r.x1[here, :])
            d_h2 = r.acc[here, :]
            d_x1 = tile_x(r.cb, row) + norm_back(xhat, inverse, d_h2 * vrow(5))
            r.x1[here, :] = d_x1
            d_branch = (d_x1 * BRANCH).astype(BF16)
            r.dbr[here, :] = d_branch
            return (
                sums[0] + fold8(d_h2 * xhat),
                sums[1] + fold8(d_h2),
                sums[2] + fold8(d_branch.astype(F32)),
            )

        sums = lax.fori_loop(0, T // ROWS, body, zero_sums(3))
        for k, at in enumerate((5, 6, 4)):
            r.gsm[at : at + 1, :] = jnp.sum(sums[k], axis=0, keepdims=True)

    def out_back():
        r.dat[...] = dot(r.dbr[...], wide(3), 1, 1).astype(BF16)

    def out_grad():
        res = dot(r.attnc[0], half_cols(r.dbr, c)[...], 0, 0) + dot(r.attnc[1], r.dbr_p[...], 0, 0)
        r.G[3] = res.astype(BF16).reshape(ZS, 2, 2, 48, HALF)

    def flip_lse():
        r.lseT[...] = jnp.transpose(r.lse[...])

    def attend_back_pair(p):
        KB = 256
        cols = pl.ds(pl.multiple_of(128 * p, 128), 128)
        lane = lane_masks(KB)
        da = r.dat[:, cols]
        prod = da.astype(F32) * r.attnc[0, :, cols].astype(F32)
        pick = jnp.where(
            (lax.broadcasted_iota(jnp.int32, (8, 128), 1) // HEAD) == lax.broadcasted_iota(jnp.int32, (8, 128), 0), 1.0, 0.0
        ).astype(F32)
        delta = lax.dot_general(
            pick, prod, (((1,), (1,)), ((), ())), preferred_element_type=F32, precision=lax.Precision.HIGHEST
        )
        q2 = r.qkvb[p, :, 0:128]
        dq_parts = [None, None]
        results = []
        for kb in (0, 1):
            first = KB * kb
            keys = pl.ds(first, KB)
            k2 = r.qkvb[p, keys, 128:256]
            v2 = r.qkvb[p, keys, 256:384]
            dks, dvs, dqs = [], [], []
            for hh in (0, 1):
                mine = (lane < HEAD) if hh == 0 else (lane >= HEAD)
                km = jnp.where(mine, k2, jnp.zeros_like(k2))
                vm = jnp.where(mine, v2, jnp.zeros_like(v2))
                logs = r.lseT[pl.ds(2 * p + hh, 1), :]
                s = dot(km, q2[first:], 1, 1) + r.mask[keys, first:]
                prob = jnp.exp(s - logs[:, first:])
                dprob = dot(vm, da[first:], 1, 1)
                ds = (prob * (dprob - delta[hh : hh + 1, first:])).astype(BF16)
                dvs.append(dot(prob.astype(BF16), da[first:], 1, 0))
                dks.append(dot(ds, q2[first:], 1, 0))
                dqs.append(dot(ds, km, 0, 0))
            dk = jnp.where(lane < HEAD, dks[0], dks[1]).astype(BF16)
            dv = jnp.where(lane < HEAD, dvs[0], dvs[1]).astype(BF16)
            results.append((dk, dv, dqs[0] + dqs[1]))
        (dk0, dv0, dq0), (dk1, dv1, dq1) = results
        scale = HEAD**-0.5
        dq_low = (dq0[:KB] * scale).astype(BF16)
        dq_high = ((dq0[KB:] + dq1) * scale).astype(BF16)
        r.qkvb[p, 0:KB, 0:128] = dq_low
        r.qkvb[p, KB:T, 0:128] = dq_high
        r.qkvb[p, 0:KB, 128:256] = dk0
        r.qkvb[p, KB:T, 128:256] = dk1
        r.qkvb[p, 0:KB, 256:384] = dv0
        r.qkvb[p, KB:T, 256:384] = dv1
        at = pl.ds(pl.multiple_of(128 * p, 128), 128)
        r.gsm[2:3, at] = jnp.sum(dq_low.astype(F32), axis=0, keepdims=True) + jnp.sum(
            dq_high.astype(F32), axis=0, keepdims=True
        )
        r.gsm[3:4, at] = jnp.sum(dv0.astype(F32), axis=0, keepdims=True) + jnp.sum(
            dv1.astype(F32), axis=0, keepdims=True
        )

    def qkv_grad(i):
        res = dot(r.h1c[0], r.qkvb[3 * c + i], 0, 0) + dot(r.h1c[1], r.dqp[i], 0, 0)
        r.G[i] = res.astype(BF16).reshape(ZS, 2, 2, 48, HALF)

    def qkv_back():
        def one(i):
            lhs = jnp.concatenate([r.qkvb[i], r.qkvb[3 + i]], axis=1)
            return dot(lhs, wide(i), 1, 1)

        r.acc[...] = one(0)

        def item(i, carry):
            r.acc[...] += one(i)
            return carry

        lax.fori_loop(1, 3, item, 0)

    def norm_one_back():
        def body(i, sums):
            row = pl.multiple_of(i * ROWS, ROWS)
            here = pl.ds(row, ROWS)
            xhat, inverse = stats(tile_x(r.xb, row))
            d_h1 = r.acc[here, :]
            d_x = r.x1[here, :] + norm_back(xhat, inverse, d_h1 * vrow(0))
            r.ob[here, :] = d_x.astype(BF16)
            return (sums[0] + fold8(d_h1 * xhat), sums[1] + fold8(d_h1))

        sums = lax.fori_loop(0, T // ROWS, body, zero_sums(2))
        for k, at in enumerate((0, 1)):
            r.gsm[at : at + 1, :] = jnp.sum(sums[k], axis=0, keepdims=True)

    def gview(u, zs, ys, xs):
        kind, first, count = u
        if kind in "pl":
            return r.Gp.at[zs, ys, xs, pl.ds(first, count), :]
        return r.G.at[pl.ds(first, count), zs, ys, xs]

    def rview(u, plain, proj):
        kind, first, count = u
        if kind == "p":
            at = (pl.ds(0, proj.shape[0]),) + (pl.ds(0, 2),) * (len(proj.shape) - 3) + (pl.ds(first, count), slice(None))
            return proj.at[at]
        return plain.at[pl.ds(first, count)]

    def add_into(dst, extra):
        dst[...] = (dst[...].astype(F32) + extra[...].astype(F32)).astype(BF16)

    def rs1(u):
        send((u, "r1a"), gview(u, low_z, ny, both), rview(u, r.rA1, r.pA1), ypeer)
        send((u, "r1b"), gview(u, high_z, both, nx), rview(u, r.rB1, r.pB1), xpeer)

    def rs2a(u):
        va = rview(u, r.rA1, r.pA1)
        arrive((u, "r1a"), va)
        add_into(gview(u, low_z, y, both), va)
        send((u, "r2a"), gview(u, low_z, y, nx), rview(u, r.rA2, r.pA2), xpeer)

    def rs2b(u):
        vb = rview(u, r.rB1, r.pB1)
        arrive((u, "r1b"), vb)
        add_into(gview(u, high_z, both, x), vb)
        send((u, "r2b"), gview(u, high_z, ny, x), rview(u, r.rB2, r.pB2), ypeer)

    def zslot(u, k):
        kind, first, count = u
        if kind == "p":
            return r.pz.at[k - 1, pl.ds(first, count), :]
        return r.rz.at[pl.ds(first, count), k - 1]

    def rs3(u):
        va, vb = rview(u, r.rA2, r.pA2), rview(u, r.rB2, r.pB2)
        arrive((u, "r2a"), va)
        add_into(gview(u, low_z, y, x), va)
        arrive((u, "r2b"), vb)
        add_into(gview(u, high_z, y, x), vb)
        for k in (1, 2, 3):
            send((u, "rz", k), gview(u, zshift(k), y, x), zslot(u, k), zpeer(k))

    def rs4(u):
        kind, first, count = u
        for k in (1, 2, 3):
            arrive((u, "rz", k), zslot(u, k))
        total = gview(u, z, y, x)[...].astype(F32)
        for k in (1, 2, 3):
            total = total + zslot(u, k)[...].astype(F32)
        if kind == "p":
            r.ptot[pl.ds(first, count), :] = total
        else:
            r.tot[pl.ds(first, count)] = total
            give = pl.ds(pl.multiple_of(24 * nc, 8), 24)
            send((u, "fin"), r.tot.at[pl.ds(first, count), give, :], r.fr.at[pl.ds(first, count)], partner)

    def rs5(u):
        kind, first, count = u
        arrive((u, "fin"), r.fr.at[pl.ds(first, count)])
        keep = pl.ds(pl.multiple_of(24 * c, 8), 24)
        for it in range(first, first + count):
            for core, part in ((c, r.tot[it, keep, :]), (nc, r.fr[it])):
                if it < 3:
                    for j in range(3):
                        at = pl.multiple_of(j * D + 128 * (3 * core + it), 128)
                        r.gq_o[:, pl.ds(at, 128)] = part[:, 128 * j : 128 * j + 128]
                elif it == 3:
                    r.go_o[:, pl.ds(pl.multiple_of(core * HALF, 128), HALF)] = part
                else:
                    at = pl.multiple_of(core * (FF // 2) + (it - 4) * HALF, 128)
                    r.gf_o[:, pl.ds(at, HALF)] = part

    def back1(u):
        for k in (1, 2, 3):
            send((u, "b1", k), gview(u, zshift(k), both, both), r.zL.at[k - 1], zpeer(k))

    def back2(u):
        for k in (1, 2, 3):
            arrive((u, "b1", k), r.zL.at[k - 1])
        for yy in (0, 1):
            for xx in (0, 1):
                here = gview(u, z, yy, xx)
                total = here[...].astype(F32)
                for k in (1, 2, 3):
                    total = total + r.zL[k - 1, yy, xx].astype(F32)
                here[...] = total.astype(BF16)
        send((u, "b2"), gview(u, z, ny, both), r.yL, ypeer)

    def back3(u):
        arrive((u, "b2"), r.yL)
        add_into(gview(u, z, y, both), r.yL)
        send((u, "b3"), gview(u, z, y, nx), r.xL, xpeer)

    def back4(u):
        kind, first, count = u
        arrive((u, "b3"), r.xL)
        r.ptot[pl.ds(first, count), :] = gview(u, z, y, x)[...].astype(F32) + r.xL[...].astype(F32)

    def rs_proj_send():
        give = pl.ds(pl.multiple_of(96 * nc, 32), 96)
        send("pfin", r.ptot.at[give, :], r.pfr, partner)

    def rs_proj_done():
        arrive("pfin", r.pfr)
        keep = pl.ds(pl.multiple_of(96 * c, 32), 96)
        r.gp_o[:, pl.ds(pl.multiple_of(c * HALF, 128), HALF)] = r.ptot[keep, :]
        r.gp_o[:, pl.ds(pl.multiple_of(nc * HALF, 128), HALF)] = r.pfr[...]

    def small_send(key, src, at, peer):
        send(("small", key), src, r.gr.at[at], peer)

    def small_add(keys, first, into):
        total = r.gsm[...] if into is None else r.gs[into]
        for n, key in enumerate(keys):
            arrive(("small", key), r.gr.at[first + n])
            total = total + r.gr[first + n]
        return total

    tasks = {}

    def pairs(body, i):
        def one(h, carry):
            body(3 * h + i)
            return carry

        lax.fori_loop(0, 2, one, 0)

    def comm(name, u):
        tasks["2" + name] = lambda: ag2(u)
        tasks["3a" + name] = lambda: ag3a(u)
        tasks["3b" + name] = lambda: ag3b(u)
        tasks["4a" + name] = lambda: ag4a(u)
        tasks["4b" + name] = lambda: ag4b(u)
        if name != "s":
            tasks["r1" + name] = lambda: rs1(u)
            tasks["r2a" + name] = lambda: rs2a(u)
            tasks["r2b" + name] = lambda: rs2b(u)
            tasks["r3" + name] = lambda: rs3(u)
            tasks["r4" + name] = lambda: rs4(u)
            if name != "p":
                tasks["r5" + name] = lambda: rs5(u)

    for name, u in (
        ("s", US), ("q0", UQ[0]), ("q1", UQ[1]), ("q2", UQ[2]), ("o", UO), ("f0", UF[0]), ("f1", UF[1]), ("p", UP)
    ):
        comm(name, u)
    tasks["l2"] = lambda: late2(UL)
    tasks["l3"] = lambda: late3(UL)
    tasks["l41"] = lambda: late4(UL, 1)
    tasks["l42"] = lambda: late4(UL, 2)
    tasks["l43"] = lambda: late4(UL, 3)
    tasks["b1"] = lambda: back1(UL)
    tasks["b2"] = lambda: back2(UL)
    tasks["b3"] = lambda: back3(UL)
    tasks["b4"] = lambda: back4(UL)

    def task(body):
        tasks[body.__name__] = body

    @task
    def mask():
        build_mask()

    @task
    def first_norm():
        ag5(US)
        for k in (1, 2, 3):
            arrive(("tok", k), r.xb.at[lax.rem(sp + 4 - k, 4)])
        own_tok.wait()
        small_vectors()
        norm_one()
        send("h1", r.h1c.at[0], r.h1c.at[1], partner)

    def qkv(i):
        def run():
            ag5(UQ[i])
            qkv_item(i)

        return run

    def attend(i):
        return lambda: pairs(attend_pair, i)

    def attend_back(i):
        def run():
            pairs(attend_back_pair, i)
            send(("dq", i), r.qkvb.at[3 * nc + i], r.dqp.at[i], partner)

        return run

    def grad_qkv(i):
        def run():
            if i == 0:
                arrive("h1", r.h1c.at[1])
            arrive(("dq", i), r.dqp.at[i])
            qkv_grad(i)

        return run

    for i in range(3):
        tasks["qkv" + str(i)] = qkv(i)
        tasks["attend" + str(i)] = attend(i)
        tasks["attend_back" + str(i)] = attend_back(i)
        tasks["qkv_grad" + str(i)] = grad_qkv(i)

    @task
    def send_tok():
        send_pack("tok", r.tok, r.xb)

    tasks["l1"] = lambda: late1(UL)

    @task
    def send_cot():
        send_pack("cot", r.cot, r.cb)

    @task
    def out():
        send("attn", r.attnc.at[0], r.attnc.at[1], partner)
        ag5(UO)
        out_proj()
        send("h2", r.h2c.at[0], r.h2c.at[1], partner)

    @task
    def flip():
        flip_lse()
        build_mask_t()

    @task
    def rows():
        for k in (1, 2, 3):
            arrive(("cot", k), r.cb.at[lax.rem(sp + 4 - k, 4)])
        own_cot.wait()
        mlp_grad_rows()
        send("dml", half_cols(r.dml, nc), r.dml_p, partner)

    def act_cols(core, j, h):
        return r.actc.at[core, :, pl.ds(h * (FF // 2) + j * D, D)]

    def up(j):
        def run():
            ag5(UF[j])

            def one(i, carry):
                up_item(i)
                return carry

            lax.fori_loop(2 * j, 2 * j + 2, one, 0)
            for h in (0, 1):
                send(("act", j, h), act_cols(0, j, h), act_cols(1, j, h), partner)

        return run

    def proj(j):
        def run():
            if j == 0:
                arrive("dml", r.dml_p)
                for k in (0, 1):
                    for h in (0, 1):
                        arrive(("act", k, h), act_cols(1, k, h))
            proj_grad(4 * j)

        return run

    def up_weight(j):
        def run():
            if j == 0:
                arrive("h2", r.h2c.at[1])
                arrive("dpre", r.dpre_p)
            up_grad(j)

        return run

    for j in range(2):
        tasks["up" + str(j)] = up(j)
        tasks["proj" + str(j)] = proj(j)
        tasks["up_grad" + str(j)] = up_weight(j)

    @task
    def whole():
        ag5(UP)
        late5(UL)

    own = {}

    @task
    def final():
        layer_out()
        own["out"] = send_rows("out", r.out_o, 2)

    @task
    def down():
        down_back()
        send("dpre", r.slope.at[:, pl.ds(pl.multiple_of(nc * (FF // 2), 128), FF // 2)], r.dpre_p, partner)

    @task
    def up_input():
        up_back()

    @task
    def second_norm():
        norm_two_back()
        send("dbr", half_cols(r.dbr, nc), r.dbr_p, partner)

    @task
    def out_input():
        out_back()

    @task
    def out_weight():
        arrive("attn", r.attnc.at[1])
        arrive("dbr", r.dbr_p)
        out_grad()

    @task
    def qkv_input():
        qkv_back()

    @task
    def last_norm():
        own["out"].wait()
        for k in (1, 2, 3):
            started.pop(("out", k)).wait_send()
        norm_one_back()
        r.gsm[12:16, :] = jnp.zeros((4, D), F32)
        small_send("x", r.gsm, 0, xpeer)
        own["dx"] = send_rows("dx", r.dx_o, 3)

    @task
    def small1():
        r.gs[0] = small_add(["x"], 0, None)
        small_send("core", r.gs.at[0], 1, partner)

    @task
    def small2():
        r.gs[1] = small_add(["core"], 1, 0)
        small_send("y", r.gs.at[1], 2, ypeer)

    @task
    def small3():
        r.gs[2] = small_add(["y"], 2, 1)
        for k in (1, 2, 3):
            small_send(("z", k), r.gs.at[2], 2 + k, zpeer(k))

    @task
    def small4():
        r.gs_o[...] = small_add([("z", 1), ("z", 2), ("z", 3)], 3, 2)

    @task
    def proj_send():
        rs_proj_send()

    @task
    def proj_done():
        rs_proj_done()

    t = Bag()
    for name, body in tasks.items():
        setattr(t, "g" + name, body)
    t.gsend_tok()
    t.g2s()
    t.gmask()
    t.gl1()
    t.g2q0()
    t.g3bs()
    t.g2q1()
    t.g3bq0()
    t.g3as()
    t.g3bq1()
    t.gl2()
    t.g4as()
    t.g4bs()
    t.g3aq0()
    t.g2q2()
    t.g3aq1()
    t.g4bq0()
    t.g2o()
    t.g4bq1()
    t.gl3()
    t.g4aq0()
    t.gfirst_norm()
    t.g3aq2()
    t.gqkv0()
    t.g3bq2()
    t.g2f0()
    t.g3ao()
    t.g4aq1()
    t.g3bo()
    t.gsend_cot()
    t.gqkv1()
    t.gattend0()
    t.gattend1()
    t.g2f1()
    t.g4bo()
    t.g3af0()
    t.g4bq2()
    t.g4aq2()
    t.g4ao()
    t.gqkv2()
    t.g3bf0()
    t.gattend2()
    t.gout()
    t.g3af1()
    t.g3bf1()
    t.g2p()
    t.g4af0()
    t.g4bf0()
    t.gflip()
    t.gup0()
    t.g4bf1()
    t.g4af1()
    t.gl41()
    t.g3ap()
    t.gl42()
    t.grows()
    t.g3bp()
    t.gup1()
    t.gl43()
    t.g4bp()
    t.gproj0()
    t.g4ap()
    t.gproj1()
    t.gwhole()
    t.gr1p()
    t.gb1()
    t.gdown()
    t.gr2bp()
    t.gfinal()
    t.gup_input()
    t.gr2ap()
    t.gup_grad0()
    t.gr1f0()
    t.gsecond_norm()
    t.gup_grad1()
    t.gout_input()
    t.gout_weight()
    t.gr1f1()
    t.gattend_back0()
    t.gr2bf0()
    t.gr2af0()
    t.gattend_back1()
    t.gr1o()
    t.gr2bf1()
    t.gr3p()
    t.gqkv_grad0()
    t.gattend_back2()
    t.gr2af1()
    t.gqkv_input()
    t.gr3f0()
    t.gr1q0()
    t.gr2bo()
    t.gqkv_grad1()
    t.gqkv_grad2()
    t.gr1q2()
    t.gr1q1()
    t.gr2ao()
    t.glast_norm()
    t.gr3f1()
    t.gr2bq0()
    t.gr2bq1()
    t.gsmall1()
    t.gr3o()
    t.gb2()
    t.gr2aq0()
    t.gr4f1()
    t.gr5f1()
    t.gr2aq2()
    t.gr2bq2()
    t.gr3q0()
    t.gr4f0()
    t.gr2aq1()
    t.gr3q2()
    t.gr4p()
    t.gr4o()
    t.gr5f0()
    t.gr5o()
    t.gr3q1()
    t.gb3()
    t.gsmall2()
    t.gsmall3()
    t.gr4q2()
    t.gb4()
    t.gproj_send()
    t.gr4q0()
    t.gproj_done()
    t.gr4q1()
    t.gr5q2()
    t.gr5q1()
    t.gsmall4()
    t.gr5q0()
    for name, dst in (("out", r.out_o), ("dx", r.dx_o)):
        for k in (1, 2, 3):
            arrive((name, k), dst.at[lax.rem(sp + 4 - k, 4)])
    own["dx"].wait()
    for copy in started.values():
        copy.wait_send()
    assert len(table) <= SEMS, len(table)


def fused(tokens, cotangent, seq_cut, g1, o1, w_qkv, bq, bv, w_out, bo, g2, o2, w_fc, bf, w_proj, bp):
    device = lax.axis_index("dp") * 4 + lax.axis_index("sp")
    small = jnp.zeros((16, D), BF16)
    small = lax.dynamic_update_slice(small, jnp.stack([g1, o1, bq, bv, bo, g2, o2, bp]), (0, 24 * device))
    small = lax.dynamic_update_slice(small, bf[None], (8 + device // 8, 96 * (device % 8)))
    vmem = pl.BlockSpec(memory_space=pltpu.VMEM)
    anywhere = pl.BlockSpec(memory_space=pl.ANY)
    s = jax.ShapeDtypeStruct
    out, d_x, gq, go, gf, gp, gs = pl.pallas_call(
        mega,
        out_shape=(
            s((4, 128, D), BF16),
            s((4, 128, D), BF16),
            s((24, 3 * D), F32),
            s((24, D), F32),
            s((24, FF), F32),
            s((96, D), F32),
            s((16, D), F32),
        ),
        in_specs=[anywhere, anywhere, pl.BlockSpec(memory_space=pltpu.SMEM)] + [vmem] * 5,
        out_specs=(anywhere, anywhere) + (vmem,) * 5,
        scratch_shapes=scratch_shapes(),
        compiler_params=pltpu.CompilerParams(collective_id=0, has_side_effects=True, vmem_limit_bytes=67043328),
    )(tokens, cotangent, seq_cut, w_qkv, w_out, w_fc, w_proj, small)
    rows = lax.dynamic_slice(gs, (0, 24 * device), (8, 24))
    g_bf = lax.dynamic_slice(gs, (8 + device // 8, 96 * (device % 8)), (1, 96))[0]
    return (out, d_x.astype(F32), rows[0], rows[1], gq, rows[2], rows[3], go, rows[4], rows[5], rows[6], gf, g_bf, gp, rows[7])


def solution(mesh):
    row = P(AXES, None)
    vec = P(AXES)
    act = P(None, AXES, None)
    body = fused if dict(mesh.shape) == {"dp": 8, "sp": 4} else local
    return jax.shard_map(
        body,
        mesh=mesh,
        in_specs=(act, act, P(None, "dp"), vec, vec, row, vec, vec, row, vec, vec, vec, row, vec, row, vec),
        out_specs=(act, act, vec, vec, row, vec, vec, row, vec, vec, vec, row, vec, row, vec),
        check_vma=False,
    )
```

```python
import functools

import jax
import jax.numpy as jnp
from jax import lax
from jax.experimental import pallas as pl
from jax.experimental.pallas import tpu as pltpu
from jax.sharding import PartitionSpec as P

HEADS = 12
HEAD = 64
EPSILON = 1e-05
BRANCH = 24.0 ** (-0.5)
NEGATIVE = -1e30
GELU_A = 0.7978845608028654
GELU_B = 0.044715
AXES = ("dp", "sp")
F32 = jnp.float32
BF16 = jnp.bfloat16
MESH = pl.DeviceIdType.MESH

def dot(a, b, dims):
    return lax.dot_general(a, b, (dims, ((), ())), preferred_element_type=F32)


def mm(a, b):
    return dot(a, b, ((1,), (0,)))


def mm_nt(a, b):
    return dot(a, b, ((1,), (1,)))


def mm_tn(a, b):
    return dot(a, b, ((0,), (0,)))


def norm_stats(rows):
    center = jnp.mean(rows, axis=-1, keepdims=True)
    centred = rows - center
    inverse = lax.rsqrt(jnp.mean(centred * centred, axis=-1, keepdims=True) + EPSILON)
    return centred * inverse, inverse


def norm_back(xhat, inverse, grad):
    mean_grad = jnp.mean(grad, axis=-1, keepdims=True)
    mean_proj = jnp.mean(grad * xhat, axis=-1, keepdims=True)
    return inverse * (grad - mean_grad - xhat * mean_proj)


def split_heads(rows):
    return rows.reshape(rows.shape[0], HEADS, HEAD).transpose(1, 0, 2)


def join_heads(heads):
    return heads.transpose(1, 0, 2).reshape(heads.shape[1], HEADS * HEAD)


def layer(x16, dy16, cut, big, small):
    w_qkv, w_out, w_fc, w_proj = big
    g1, o1, bq, bv, bo, g2, o2, bf, bp = [v.astype(F32)[None] for v in small]
    length = x16.shape[0]
    x = x16.astype(F32)
    xhat1, inv1 = norm_stats(x)
    h1 = (xhat1 * g1 + o1).astype(BF16)
    bias = jnp.concatenate([bq, jnp.zeros_like(bq), bv], axis=1)
    qkv = (mm(h1, w_qkv) + bias).astype(BF16)
    width = HEADS * HEAD
    q, k, v = (split_heads(qkv[:, i * width : (i + 1) * width]) for i in range(3))
    pos = lax.iota(jnp.int32, length)
    allowed = (pos[None, :] <= pos[:, None]) & ((pos[None, :] >= cut) == (pos[:, None] >= cut))
    scale = HEAD ** (-0.5)
    scores = jnp.einsum("hqd,hkd->hqk", q, k, preferred_element_type=F32) * scale
    scores = jnp.where(allowed[None], scores, NEGATIVE)
    top = jnp.max(scores, axis=-1, keepdims=True)
    expo = jnp.exp(scores - top)
    prob32 = expo / jnp.sum(expo, axis=-1, keepdims=True)
    prob = prob32.astype(BF16)
    attn32 = jnp.einsum("hqk,hkd->hqd", prob, v, preferred_element_type=F32)
    attn = join_heads(attn32).astype(BF16)
    x1 = x + BRANCH * (mm(attn, w_out) + bo)
    xhat2, inv2 = norm_stats(x1)
    h2 = (xhat2 * g2 + o2).astype(BF16)
    pre = mm(h2, w_fc) + bf
    t = jnp.tanh(GELU_A * (pre + GELU_B * pre * pre * pre))
    act = (0.5 * pre * (1 + t)).astype(BF16)
    slope = 0.5 * (1 + t) + 0.5 * pre * (1 - t * t) * (GELU_A * (1 + 3 * GELU_B * pre * pre))
    out = (x1 + BRANCH * (mm(act, w_proj) + bp)).astype(BF16)

    dy = dy16.astype(F32)
    d_mlp = (dy * BRANCH).astype(BF16)
    g_w_proj = mm_tn(act, d_mlp)
    g_b_proj = jnp.sum(d_mlp.astype(F32), axis=0)
    d_pre = (mm_nt(d_mlp, w_proj) * slope).astype(BF16)
    g_w_fc = mm_tn(h2, d_pre)
    g_b_fc = jnp.sum(d_pre.astype(F32), axis=0)
    d_h2 = mm_nt(d_pre, w_fc)
    g_g2 = jnp.sum(d_h2 * xhat2, axis=0)
    g_o2 = jnp.sum(d_h2, axis=0)
    d_x1 = dy + norm_back(xhat2, inv2, d_h2 * g2)
    d_branch = (d_x1 * BRANCH).astype(BF16)
    g_w_out = mm_tn(attn, d_branch)
    g_b_out = jnp.sum(d_branch.astype(F32), axis=0)
    d_attn = split_heads(mm_nt(d_branch, w_out).astype(BF16))
    delta = jnp.sum(d_attn.astype(F32) * attn32, axis=-1, keepdims=True)
    d_prob = jnp.einsum("hqd,hkd->hqk", d_attn, v, preferred_element_type=F32)
    d_scores = (prob32 * (d_prob - delta)).astype(BF16)
    d_q = jnp.einsum("hqk,hkd->hqd", d_scores, k, preferred_element_type=F32) * scale
    d_k = jnp.einsum("hqk,hqd->hkd", d_scores, q, preferred_element_type=F32) * scale
    d_v = jnp.einsum("hqk,hqd->hkd", prob, d_attn, preferred_element_type=F32)
    d_qkv = jnp.concatenate([join_heads(d_q), join_heads(d_k), join_heads(d_v)], axis=1).astype(BF16)
    g_w_qkv = mm_tn(h1, d_qkv)
    g_b_qkv = jnp.sum(d_qkv.astype(F32), axis=0)
    d_h1 = mm_nt(d_qkv, w_qkv)
    g_g1 = jnp.sum(d_h1 * xhat1, axis=0)
    g_o1 = jnp.sum(d_h1, axis=0)
    d_x = d_x1 + norm_back(xhat1, inv1, d_h1 * g1)
    big_grads = (g_w_qkv, g_w_out, g_w_fc, g_w_proj)
    small_grads = (g_g1, g_o1, g_b_qkv[:width], g_b_qkv[2 * width :], g_b_out, g_g2, g_o2, g_b_fc, g_b_proj)
    return out, d_x, big_grads, small_grads


def local(tokens, cotangent, seq_cut, g1, o1, w_qkv, bq, bv, w_out, bo, g2, o2, w_fc, bf, w_proj, bp):
    ways = lax.axis_size("sp")
    devices = ways * lax.axis_size("dp")
    small = (g1, o1, bq, bv, bo, g2, o2, bf, bp)
    sizes = [v.shape[0] for v in small]
    big = [lax.all_gather(w, AXES, axis=0, tiled=True) for w in (w_qkv, w_out, w_fc, w_proj)]
    packed = lax.all_gather(jnp.concatenate(small), AXES, axis=0)
    cuts = [sum(sizes[:i]) for i in range(len(sizes) + 1)]
    vectors = [packed[:, a:b].reshape(-1) for a, b in zip(cuts[:-1], cuts[1:])]
    x16 = lax.all_to_all(tokens, "sp", split_axis=0, concat_axis=1, tiled=True)
    dy16 = lax.all_to_all(cotangent, "sp", split_axis=0, concat_axis=1, tiled=True)
    packs = x16.shape[0]
    first = lax.axis_index("sp") * packs
    outs, grads_in, big_sum, small_sum = [], [], None, None
    for i in range(packs):
        cut = lax.dynamic_slice(seq_cut, (first + i, 0), (1, 1))[0, 0]
        out, d_x, bigs, smalls = layer(x16[i], dy16[i], cut, big, vectors)
        outs.append(out)
        grads_in.append(d_x)
        big_sum = bigs if big_sum is None else [a + b for a, b in zip(big_sum, bigs)]
        small_sum = smalls if small_sum is None else [a + b for a, b in zip(small_sum, smalls)]
    out = lax.all_to_all(jnp.stack(outs), "sp", split_axis=1, concat_axis=0, tiled=True)
    d_x = lax.all_to_all(jnp.stack(grads_in), "sp", split_axis=1, concat_axis=0, tiled=True)
    big_out = [
        lax.psum_scatter(g.astype(BF16), AXES, scatter_dimension=0, tiled=True).astype(F32) for g in big_sum
    ]
    small_pack = jnp.concatenate([g.reshape(devices, -1) for g in small_sum], axis=1)
    small_out = lax.psum_scatter(small_pack, AXES, scatter_dimension=0, tiled=True)[0]
    s = [small_out[a:b] for a, b in zip(cuts[:-1], cuts[1:])]
    return (out, d_x, s[0], s[1], big_out[0], s[2], s[3], big_out[1], s[4], s[5], s[6], big_out[2], s[7], big_out[3], s[8])

T, D, FF, HALF = 512, 768, 3072, 384
ZS = 4
ZA = 3
PZ = 3
ROWS = 32


class Bag:
    pass


def rows_loop(count, step, body):
    def one(i, carry):
        body(pl.multiple_of(i * step, step))
        return carry

    lax.fori_loop(0, count // step, one, 0)


def fold8(values):
    return jnp.sum(values.reshape(values.shape[0] // 8, 8, values.shape[1]), axis=0)


def zero_sums(count):
    return tuple(jnp.zeros((8, D), F32) for _ in range(count))


NAMES = (
    "tok", "cot", "cut", "wq", "wo", "wf", "wp", "flat", "out_o", "dx_o", "gq_o", "go_o", "gf_o", "gp_o", "gs_o",
    "W", "Wp", "Sw", "sq", "so", "sf", "sp_", "ssm", "vec", "G", "Gp", "rA1", "rB1", "pA1", "pB1", "rA2", "rB2",
    "pA2", "pB2", "rz", "pz", "zL", "yL", "xL", "tot", "ptot", "fr", "pfr", "xb", "cb", "h1c", "qkvb", "attnc", "x1", "h2c", "actc",
    "slope", "dpre_p", "acc", "dbr", "dbr_p", "dml", "dml_p", "dat", "dqp", "ob", "mask", "lse", "lseT", "gsm", "gs",
    "gr", "small", "ssem", "rsem", "lsem",
)
SEMS = 220


def scratch_shapes():
    v = pltpu.VMEM
    return [
        v((8, 2, ZS, 2, 2, 48, HALF), BF16),
        v((2, ZS, 2, 2, 192, HALF), BF16),
        v((2, ZS, 2, 2, 16, HALF), BF16),
        v((24, 3 * D), BF16),
        v((24, D), BF16),
        v((24, FF), BF16),
        v((96, D), BF16),
        v((16, D), BF16),
        v((16, D), F32),
        v((8, ZS, 2, 2, 48, HALF), BF16),
        v((ZS, 2, 2, 192, HALF), BF16),
        v((8, ZA, 2, 48, HALF), BF16),
        v((8, ZS - ZA, 2, 48, HALF), BF16),
        v((PZ, 2, 96, HALF), BF16),
        v((ZS - PZ, 2, 96, HALF), BF16),
        v((8, ZA, 48, HALF), BF16),
        v((8, ZS - ZA, 48, HALF), BF16),
        v((PZ, 96, HALF), BF16),
        v((ZS - PZ, 96, HALF), BF16),
        v((8, 3, 48, HALF), BF16),
        v((3, 96, HALF), BF16),
        v((3, 2, 2, 96, HALF), BF16),
        v((2, 96, HALF), BF16),
        v((96, HALF), BF16),
        v((8, 48, HALF), F32),
        v((192, HALF), F32),
        v((8, 24, HALF), F32),
        v((96, HALF), F32),
        v((4, 128, D), BF16),
        v((4, 128, D), BF16),
        v((2, T, D), BF16),
        v((6, T, HALF), BF16),
        v((2, T, D), BF16),
        v((T, D), F32),
        v((2, T, D), BF16),
        v((2, T, FF), BF16),
        v((T, FF), BF16),
        v((T, FF // 2), BF16),
        v((T, D), F32),
        v((T, D), BF16),
        v((T, HALF), BF16),
        v((T, D), BF16),
        v((T, HALF), BF16),
        v((T, D), BF16),
        v((3, T, HALF), BF16),
        v((T, D), BF16),
        v((T, T), F32),
        v((T, 128), F32),
        v((128, T), F32),
        v((16, D), F32),
        v((4, 16, D), F32),
        v((6, 16, D), F32),
        v((16, D), BF16),
        pltpu.SemaphoreType.DMA((SEMS,)),
        pltpu.SemaphoreType.DMA((SEMS,)),
        pltpu.SemaphoreType.DMA((4,)),
    ]


def mega(*refs):
    r = Bag()
    assert len(refs) == len(NAMES), (len(refs), len(NAMES))
    for name, ref in zip(NAMES, refs):
        setattr(r, name, ref)
    dp, sp = lax.axis_index("dp"), lax.axis_index("sp")
    z, y = dp // 2, lax.rem(dp, 2)
    x, c = sp // 2, lax.rem(sp, 2)
    nx, ny, nc = 1 - x, 1 - y, 1 - c
    partner = {"dp": dp, "sp": x * 2 + nc}
    xpeer = {"dp": dp, "sp": nx * 2 + c}
    ypeer = {"dp": z * 2 + ny, "sp": sp}
    every = pl.ds(0, ZS)

    def low_z(u):
        return pl.ds(0, PZ if u[0] == "p" else ZA)

    def high_z(u):
        first = PZ if u[0] == "p" else ZA
        return pl.ds(first, ZS - first)

    both = pl.ds(0, 2)

    def zshift(k):
        return lax.rem(z + k, ZS)

    def zpeer(k):
        return {"dp": zshift(k) * 2 + y, "sp": sp}

    def speer(k):
        return lax.rem(sp + k, 4)

    table = {}
    started = {}

    def slot(key):
        return table.setdefault(key, len(table))

    def send(key, src, dst, device):
        i = slot(key)
        copy = pltpu.make_async_remote_copy(
            src_ref=src, dst_ref=dst, send_sem=r.ssem.at[i], recv_sem=r.rsem.at[i], device_id=device, device_id_type=MESH
        )
        copy.start()
        started[key] = copy
        return copy

    def arrive(key, dst):
        i = slot(key)
        pltpu.make_async_remote_copy(
            src_ref=dst, dst_ref=dst, send_sem=r.ssem.at[i], recv_sem=r.rsem.at[i], device_id=partner, device_id_type=MESH
        ).wait_recv()

    barrier = pltpu.get_barrier_semaphore()
    peers = [{"dp": dp, "sp": speer(k)} for k in (1, 2, 3)] + [ypeer] + [zpeer(k) for k in (1, 2, 3)]
    for peer in peers:
        pl.semaphore_signal(barrier, inc=1, device_id=peer, device_id_type=MESH)
    pl.semaphore_wait(barrier, len(peers))

    def view(u, h, zs, ys, xs):
        kind, first, count = u
        if kind == "s":
            return r.Sw.at[h, zs, ys, xs]
        if kind in "pl":
            return r.Wp.at[h, zs, ys, xs, pl.ds(first, count), :]
        return r.W.at[pl.ds(first, count), h, zs, ys, xs]

    def ag1(u):
        for k in (1, 2, 3):
            v = view(u, c, z, y, x)
            send((u, "z", k), v, v, zpeer(k))

    def ag2(u):
        for k in (1, 2, 3):
            arrive((u, "z", k), view(u, c, zshift(ZS - k), y, x))
        v = view(u, c, low_z(u), y, x)
        send((u, "2a"), v, v, xpeer)
        v = view(u, c, high_z(u), y, x)
        send((u, "2b"), v, v, ypeer)
        v = view(u, c, every, y, x)
        send((u, "c0"), v, v, partner)

    def ag3a(u):
        arrive((u, "2a"), view(u, c, low_z(u), y, nx))
        v = view(u, c, low_z(u), y, both)
        send((u, "3a"), v, v, ypeer)
        v = view(u, c, low_z(u), y, nx)
        send((u, "c1"), v, v, partner)

    def ag3b(u):
        arrive((u, "2b"), view(u, c, high_z(u), ny, x))
        v = view(u, c, high_z(u), both, x)
        send((u, "3b"), v, v, xpeer)
        v = view(u, c, high_z(u), ny, x)
        send((u, "c2"), v, v, partner)

    def ag4a(u):
        v = view(u, c, low_z(u), ny, both)
        arrive((u, "3a"), v)
        send((u, "c3"), v, v, partner)

    def ag4b(u):
        v = view(u, c, high_z(u), both, nx)
        arrive((u, "3b"), v)
        send((u, "c4"), v, v, partner)

    def ag5(u):
        arrive((u, "c0"), view(u, nc, every, y, x))
        arrive((u, "c1"), view(u, nc, low_z(u), y, nx))
        arrive((u, "c2"), view(u, nc, high_z(u), ny, x))
        arrive((u, "c3"), view(u, nc, low_z(u), ny, both))
        arrive((u, "c4"), view(u, nc, high_z(u), both, nx))

    def late1(u):
        v = view(u, c, z, y, x)
        send((u, "lx"), v, v, xpeer)
        send((u, "ly"), v, v, ypeer)

    def late2(u):
        v = view(u, c, z, y, nx)
        arrive((u, "lx"), v)
        send((u, "ld"), v, v, ypeer)

    def late3(u):
        arrive((u, "ly"), view(u, c, z, ny, x))
        arrive((u, "ld"), view(u, c, z, ny, nx))
        v = view(u, c, z, both, both)
        for k in (1, 2, 3):
            send((u, "lz", k), v, v, zpeer(k))
        send((u, "c", 0), v, v, partner)

    def late4(u, k):
        v = view(u, c, zshift(ZS - k), both, both)
        arrive((u, "lz", k), v)
        send((u, "c", k), v, v, partner)

    def late5(u):
        for k in (0, 1, 2, 3):
            arrive((u, "c", k), view(u, nc, zshift(ZS - k), both, both))

    US = ("s", 0, 16)
    UQ = [("w", i, 1) for i in range(3)]
    UO = ("w", 3, 1)
    UF = [("w", 4, 2), ("w", 6, 2)]
    UP = ("p", 0, 96)
    UL = ("l", 96, 96)

    device = dp * 4 + sp
    low = 24 * device
    wide_row, wide_low = device // 8, 96 * lax.rem(device, 8)

    def build_small():
        i = lax.broadcasted_iota(jnp.int32, (384, 1), 0)
        part = sum((i >= 24 * m).astype(jnp.int32) for m in range(1, 8))
        target = jnp.where(i < 192, low + i - 24 * part, wide_low + i - 192)
        target = jnp.where(i < 288, target, -1)
        j = lax.broadcasted_iota(jnp.int32, (384, D), 1)
        place = jnp.where(j == target, 1.0, 0.0).astype(BF16)
        row = lax.broadcasted_iota(jnp.int32, (16, 384), 0)
        lane = lax.broadcasted_iota(jnp.int32, (16, 384), 1)
        mine = (row < 8) & (lane >= 24 * row) & (lane < 24 * row + 24)
        mine = mine | ((row == 8 + wide_row) & (lane >= 192))
        values = jnp.where(mine, jnp.broadcast_to(r.flat[...].astype(F32), (16, 384)), 0.0).astype(BF16)
        r.small[...] = lax.dot_general(values, place, (((1,), (0,)), ((), ())), preferred_element_type=F32).astype(BF16)

    def pick_small():
        j = lax.broadcasted_iota(jnp.int32, (D, 128), 0)
        lane = lax.broadcasted_iota(jnp.int32, (D, 128), 1)
        take = ((lane < 24) & (j == low + lane)) | ((lane >= 32) & (j == wide_low + lane - 32))
        picked = lax.dot_general(
            r.gs[3], jnp.where(take, 1.0, 0.0), (((1,), (0,)), ((), ())), preferred_element_type=F32,
            precision=lax.Precision.HIGHEST,
        )
        row = lax.broadcasted_iota(jnp.int32, (16, 128), 0)
        one = jnp.sum(jnp.where(row == 8 + wide_row, picked, 0.0), axis=0, keepdims=True)
        r.gs_o[...] = jnp.where(row < 8, picked, one)

    swaps = [("wq", r.wq, r.sq), ("wp", r.wp, r.sp_), ("wo", r.wo, r.so), ("wf", r.wf, r.sf)]
    for key, src, dst in swaps:
        send(key, src, dst, partner)
    build_small()
    send("small", r.small, r.ssm, partner)

    def send_pack(key, src, dst, shifts):
        for k in shifts:
            send((key, k), src.at[speer(k)], dst.at[sp], {"dp": dp, "sp": speer(k)})

    own_tok = pltpu.make_async_copy(r.tok.at[sp], r.xb.at[sp], r.lsem.at[0])
    own_tok.start()
    own_cot = pltpu.make_async_copy(r.cot.at[sp], r.cb.at[sp], r.lsem.at[1])
    own_cot.start()
    first_core = c == 0

    def pair_rows(own, other, col, width):
        a = own[:, pl.ds(pl.multiple_of(col, 128), width)].astype(F32)
        b = other[:, pl.ds(pl.multiple_of(col, 128), width)].astype(F32)
        return jnp.concatenate([jnp.where(first_core, a, b), jnp.where(first_core, b, a)], axis=0).astype(BF16)

    arrive("small", r.ssm)
    cols = pl.ds(pl.multiple_of(c * HALF, 128), HALF)
    r.Sw[c, z, y, x] = (r.small[:, cols].astype(F32) + r.ssm[:, cols].astype(F32)).astype(BF16)
    ag1(US)
    arrive("wq", r.sq)
    for i in range(3):
        for j in range(3):
            r.W[i, c, z, y, x, :, pl.ds(128 * j, 128)] = pair_rows(r.wq, r.sq, j * D + 128 * (3 * c + i), 128)
        ag1(UQ[i])
    arrive("wp", r.sp_)
    r.Wp[c, z, y, x, pl.ds(pl.multiple_of(96 * c, 32), 96), :] = r.wp[:, cols]
    r.Wp[c, z, y, x, pl.ds(pl.multiple_of(96 * nc, 32), 96), :] = r.sp_[:, cols]
    arrive("wo", r.so)
    r.W[3, c, z, y, x] = pair_rows(r.wo, r.so, c * HALF, HALF)
    ag1(UO)
    arrive("wf", r.sf)
    for i in range(4):
        r.W[4 + i, c, z, y, x] = pair_rows(r.wf, r.sf, c * (FF // 2) + i * HALF, HALF)
    ag1(UF[0])
    ag1(UF[1])
    ag1(UP)

    def dot(a, b, ca, cb):
        return lax.dot_general(a, b, (((ca,), (cb,)), ((), ())), preferred_element_type=F32)

    def wide(item):
        return jnp.concatenate([r.W[item, h].reshape(D, HALF) for h in (0, 1)], axis=1)

    def tile_x(buf, row):
        return buf[row // 128, pl.ds(pl.multiple_of(lax.rem(row, 128), ROWS), ROWS), :].astype(F32)

    def vrow(i):
        return r.vec[i : i + 1, :]

    def stats(v):
        center = jnp.mean(v, axis=-1, keepdims=True)
        centred = v - center
        inverse = lax.rsqrt(jnp.mean(centred * centred, axis=-1, keepdims=True) + EPSILON)
        return centred * inverse, inverse

    def norm_back(xhat, inverse, grad):
        return inverse * (grad - jnp.mean(grad, axis=-1, keepdims=True) - xhat * jnp.mean(grad * xhat, axis=-1, keepdims=True))

    def build_mask():
        def body(row):
            q = lax.broadcasted_iota(jnp.int32, (ROWS, T), 0) + row
            k = lax.broadcasted_iota(jnp.int32, (ROWS, T), 1)
            cut = r.cut[pl.ds(sp, 1), :]
            ok = (k <= q) & ((k >= cut) == (q >= cut))
            r.mask[pl.ds(row, ROWS), :] = jnp.where(ok, 0.0, NEGATIVE)

        rows_loop(T, ROWS, body)

    def build_mask_t():
        def body(row):
            k = lax.broadcasted_iota(jnp.int32, (ROWS, T), 0) + row
            q = lax.broadcasted_iota(jnp.int32, (ROWS, T), 1)
            cut = r.cut[pl.ds(sp, 1), :]
            ok = (k <= q) & ((k >= cut) == (q >= cut))
            r.mask[pl.ds(row, ROWS), :] = jnp.where(ok, 0.0, NEGATIVE)

        rows_loop(T, ROWS, body)

    def small_vectors():
        for h in (0, 1):
            total = jnp.zeros((16, HALF), F32)
            for zz in range(ZS):
                for yy in (0, 1):
                    for xx in (0, 1):
                        total = total + r.Sw[h, zz, yy, xx].astype(F32)
            r.vec[:, pl.ds(h * HALF, HALF)] = total

    def norm_one():
        def body(row):
            xhat, _ = stats(tile_x(r.xb, row))
            r.h1c[0, pl.ds(row, ROWS), :] = (xhat * vrow(0) + vrow(1)).astype(BF16)

        rows_loop(T, ROWS, body)

    def qkv_item(i):
        res = dot(r.h1c[0], wide(i), 1, 0)
        for h in (0, 1):
            p = 3 * h + i
            q = res[:, h * HALF : h * HALF + 128] + r.vec[2:3, 128 * p : 128 * p + 128]
            k = res[:, h * HALF + 128 : h * HALF + 256]
            v = res[:, h * HALF + 256 : h * HALF + 384] + r.vec[3:4, 128 * p : 128 * p + 128]
            r.qkvb[p, :, 0:128] = (q.astype(BF16).astype(F32) * (HEAD**-0.5)).astype(BF16)
            r.qkvb[p, :, 128:256] = k.astype(BF16)
            r.qkvb[p, :, 256:384] = v.astype(BF16)

    QB = 256

    def lane_masks(rows):
        lane = lax.broadcasted_iota(jnp.int32, (rows, 128), 1)
        return lane

    def attend_pair(p):
        lane = lane_masks(QB)

        def block(qb):
            keys = QB * (qb + 1)
            rows = pl.ds(QB * qb, QB)
            q2 = r.qkvb[p, rows, 0:128]
            k2 = r.qkvb[p, 0:keys, 128:256]
            v2 = r.qkvb[p, 0:keys, 256:384]
            outs = []
            for hh in (0, 1):
                mine = (lane < HEAD) if hh == 0 else (lane >= HEAD)
                qm = jnp.where(mine, q2, jnp.zeros_like(q2))
                s = dot(qm, k2, 1, 1) + r.mask[rows, 0:keys]
                top = jnp.max(s, axis=1, keepdims=True)
                e = jnp.exp(s - top)
                total = jnp.sum(e, axis=1, keepdims=True)
                outs.append(dot(e.astype(BF16), v2, 1, 0) / total)
                r.lse[rows, :] = jnp.where(lane == 2 * p + hh, top + jnp.log(total), r.lse[rows, :])
            both_heads = jnp.where(lane < HEAD, outs[0], outs[1]).astype(BF16)
            r.attnc[0, rows, pl.ds(pl.multiple_of(128 * p, 128), 128)] = both_heads

        for qb in range(T // QB):
            block(qb)

    def out_proj():
        r.acc[...] = dot(r.attnc[0], wide(3), 1, 0)

        def body(row):
            v = tile_x(r.xb, row) + BRANCH * (r.acc[pl.ds(row, ROWS), :] + vrow(4))
            r.x1[pl.ds(row, ROWS), :] = v
            xhat, _ = stats(v)
            r.h2c[0, pl.ds(row, ROWS), :] = (xhat * vrow(5) + vrow(6)).astype(BF16)

        rows_loop(T, ROWS, body)

    def up_item(i):
        r.acc[...] = dot(r.h2c[0], wide(4 + i), 1, 0)
        for h in (0, 1):
            col = pl.multiple_of(h * (FF // 2) + i * HALF, 128)
            at = h * 2 + i // 2
            bias = r.vec[pl.ds(8 + at, 1), pl.ds(pl.multiple_of(lax.rem(i, 2) * HALF, 128), HALF)]

            def body(row):
                pre = r.acc[pl.ds(row, ROWS), pl.ds(h * HALF, HALF)] + bias
                square = pre * pre
                t = jnp.tanh(pre * (GELU_A + (GELU_A * GELU_B) * square))
                half_one = 0.5 * (1.0 + t)
                r.actc[0, pl.ds(row, ROWS), pl.ds(col, HALF)] = (pre * half_one).astype(BF16)
                inner = GELU_A + (3.0 * GELU_A * GELU_B) * square
                r.slope[pl.ds(row, ROWS), pl.ds(col, HALF)] = (
                    half_one + (0.5 * pre) * (1.0 - t * t) * inner
                ).astype(BF16)

            rows_loop(T, ROWS, body)

    def wp_group(g):
        return jnp.concatenate([r.Wp[h, g].reshape(D, HALF) for h in (0, 1)], axis=1)

    def group_cols(g):
        return pl.ds(pl.multiple_of(g * D, 128), D)

    def mlp_grad_rows():
        def body(row, sums):
            d = (tile_x(r.cb, row) * BRANCH).astype(BF16)
            r.dml[pl.ds(row, ROWS), :] = d
            return sums + fold8(d.astype(F32))

        sums = lax.fori_loop(0, T // ROWS, lambda i, s: body(pl.multiple_of(i * ROWS, ROWS), s), jnp.zeros((8, D), F32))
        r.gsm[7:8, :] = jnp.sum(sums, axis=0, keepdims=True)

    def layer_out():
        r.acc[...] = dot(r.actc[0, :, 0:D], wp_group(0), 1, 0)

        def group(g, carry):
            r.acc[...] += dot(r.actc[0, :, group_cols(g)], wp_group(g), 1, 0)
            return carry

        lax.fori_loop(1, 4, group, 0)

        def body(row):
            v = r.x1[pl.ds(row, ROWS), :] + BRANCH * (r.acc[pl.ds(row, ROWS), :] + vrow(7))
            r.ob[pl.ds(row, ROWS), :] = v.astype(BF16)

        rows_loop(T, ROWS, body)

    def send_rows(key, dst, shifts):
        for k in shifts:
            src = r.ob.at[pl.ds(pl.multiple_of(128 * speer(k), 128), 128), :]
            send((key, k), src, dst.at[sp], {"dp": dp, "sp": speer(k)})
    def keep_rows(dst, sem):
        own = pltpu.make_async_copy(r.ob.at[pl.ds(pl.multiple_of(128 * sp, 128), 128), :], dst.at[sp], r.lsem.at[sem])
        own.start()
        return own

    def down_back():
        def group(g, carry):
            r.acc[...] = dot(r.dml[...], wp_group(g), 1, 1)

            def body(i, sums):
                row = pl.multiple_of(i * ROWS, ROWS)
                here = (pl.ds(row, ROWS), group_cols(g))
                d = (r.acc[pl.ds(row, ROWS), :] * r.slope[here].astype(F32)).astype(BF16)
                r.slope[here] = d
                return sums + fold8(d.astype(F32))

            sums = lax.fori_loop(0, T // ROWS, body, jnp.zeros((8, D), F32))
            r.gsm[pl.ds(8 + g, 1), :] = jnp.sum(sums, axis=0, keepdims=True)
            return carry

        lax.fori_loop(0, 4, group, 0)

    def up_back():
        def one(i):
            lhs = jnp.concatenate(
                [r.slope[:, pl.ds(pl.multiple_of(h * (FF // 2) + i * HALF, 128), HALF)] for h in (0, 1)], axis=1
            )
            return dot(lhs, wide(4 + i), 1, 1)

        r.acc[...] = one(0)

        def item(i, carry):
            r.acc[...] += one(i)
            return carry

        lax.fori_loop(1, 4, item, 0)

    def half_cols(ref, core):
        return ref.at[:, pl.ds(pl.multiple_of(core * HALF, 128), HALF)]

    def proj_grad(first):
        def chunk(n, carry):
            f = 2 * first + lax.rem(n, 2) + 4 * (n // 2)
            at = pl.ds(pl.multiple_of(f * HALF, 128), HALF)
            res = dot(r.actc[0, :, at], half_cols(r.dml, c)[...], 0, 0) + dot(r.actc[1, :, at], r.dml_p[...], 0, 0)
            r.Gp[f // 2, lax.rem(f, 2)] = res.astype(BF16).reshape(2, 192, HALF)
            return carry

        lax.fori_loop(0, 4, chunk, 0)

    def up_grad(u):
        own = r.slope[:, pl.ds(pl.multiple_of(c * (FF // 2) + u * D, 128), D)]
        res = dot(r.h2c[0], own, 0, 0) + dot(r.h2c[1], r.dpre_p[:, u * D : u * D + D], 0, 0)
        for k in (0, 1):
            r.G[4 + 2 * u + k] = res[:, k * HALF : k * HALF + HALF].astype(BF16).reshape(ZS, 2, 2, 48, HALF)

    def norm_two_back():
        def body(i, sums):
            row = pl.multiple_of(i * ROWS, ROWS)
            here = pl.ds(row, ROWS)
            xhat, inverse = stats(r.x1[here, :])
            d_h2 = r.acc[here, :]
            d_x1 = tile_x(r.cb, row) + norm_back(xhat, inverse, d_h2 * vrow(5))
            r.x1[here, :] = d_x1
            d_branch = (d_x1 * BRANCH).astype(BF16)
            r.dbr[here, :] = d_branch
            return (
                sums[0] + fold8(d_h2 * xhat),
                sums[1] + fold8(d_h2),
                sums[2] + fold8(d_branch.astype(F32)),
            )

        sums = lax.fori_loop(0, T // ROWS, body, zero_sums(3))
        for k, at in enumerate((5, 6, 4)):
            r.gsm[at : at + 1, :] = jnp.sum(sums[k], axis=0, keepdims=True)

    def out_back():
        r.dat[...] = dot(r.dbr[...], wide(3), 1, 1).astype(BF16)

    def out_grad():
        res = dot(r.attnc[0], half_cols(r.dbr, c)[...], 0, 0) + dot(r.attnc[1], r.dbr_p[...], 0, 0)
        r.G[3] = res.astype(BF16).reshape(ZS, 2, 2, 48, HALF)

    def flip_lse():
        r.lseT[...] = jnp.transpose(r.lse[...])

    def attend_back_pair(p):
        KB = 256
        cols = pl.ds(pl.multiple_of(128 * p, 128), 128)
        lane = lane_masks(KB)
        da = r.dat[:, cols]
        prod = da.astype(F32) * r.attnc[0, :, cols].astype(F32)
        pick = jnp.where(
            (lax.broadcasted_iota(jnp.int32, (8, 128), 1) // HEAD) == lax.broadcasted_iota(jnp.int32, (8, 128), 0), 1.0, 0.0
        ).astype(F32)
        delta = lax.dot_general(
            pick, prod, (((1,), (1,)), ((), ())), preferred_element_type=F32, precision=lax.Precision.HIGHEST
        )
        q2 = r.qkvb[p, :, 0:128]
        dq_parts = [None, None]
        results = []
        for kb in (0, 1):
            first = KB * kb
            keys = pl.ds(first, KB)
            k2 = r.qkvb[p, keys, 128:256]
            v2 = r.qkvb[p, keys, 256:384]
            dks, dvs, dqs = [], [], []
            for hh in (0, 1):
                mine = (lane < HEAD) if hh == 0 else (lane >= HEAD)
                km = jnp.where(mine, k2, jnp.zeros_like(k2))
                vm = jnp.where(mine, v2, jnp.zeros_like(v2))
                logs = r.lseT[pl.ds(2 * p + hh, 1), :]
                s = dot(km, q2[first:], 1, 1) + r.mask[keys, first:]
                prob = jnp.exp(s - logs[:, first:])
                dprob = dot(vm, da[first:], 1, 1)
                ds = (prob * (dprob - delta[hh : hh + 1, first:])).astype(BF16)
                dvs.append(dot(prob.astype(BF16), da[first:], 1, 0))
                dks.append(dot(ds, q2[first:], 1, 0))
                dqs.append(dot(ds, km, 0, 0))
            dk = jnp.where(lane < HEAD, dks[0], dks[1]).astype(BF16)
            dv = jnp.where(lane < HEAD, dvs[0], dvs[1]).astype(BF16)
            results.append((dk, dv, dqs[0] + dqs[1]))
        (dk0, dv0, dq0), (dk1, dv1, dq1) = results
        scale = HEAD**-0.5
        dq_low = (dq0[:KB] * scale).astype(BF16)
        dq_high = ((dq0[KB:] + dq1) * scale).astype(BF16)
        r.qkvb[p, 0:KB, 0:128] = dq_low
        r.qkvb[p, KB:T, 0:128] = dq_high
        r.qkvb[p, 0:KB, 128:256] = dk0
        r.qkvb[p, KB:T, 128:256] = dk1
        r.qkvb[p, 0:KB, 256:384] = dv0
        r.qkvb[p, KB:T, 256:384] = dv1
        at = pl.ds(pl.multiple_of(128 * p, 128), 128)
        r.gsm[2:3, at] = jnp.sum(dq_low.astype(F32), axis=0, keepdims=True) + jnp.sum(
            dq_high.astype(F32), axis=0, keepdims=True
        )
        r.gsm[3:4, at] = jnp.sum(dv0.astype(F32), axis=0, keepdims=True) + jnp.sum(
            dv1.astype(F32), axis=0, keepdims=True
        )

    def qkv_grad(i):
        res = dot(r.h1c[0], r.qkvb[3 * c + i], 0, 0) + dot(r.h1c[1], r.dqp[i], 0, 0)
        r.G[i] = res.astype(BF16).reshape(ZS, 2, 2, 48, HALF)

    def qkv_back():
        def one(i):
            lhs = jnp.concatenate([r.qkvb[i], r.qkvb[3 + i]], axis=1)
            return dot(lhs, wide(i), 1, 1)

        r.acc[...] = one(0)

        def item(i, carry):
            r.acc[...] += one(i)
            return carry

        lax.fori_loop(1, 3, item, 0)

    def norm_one_back():
        def body(i, sums):
            row = pl.multiple_of(i * ROWS, ROWS)
            here = pl.ds(row, ROWS)
            xhat, inverse = stats(tile_x(r.xb, row))
            d_h1 = r.acc[here, :]
            d_x = r.x1[here, :] + norm_back(xhat, inverse, d_h1 * vrow(0))
            r.ob[here, :] = d_x.astype(BF16)
            return (sums[0] + fold8(d_h1 * xhat), sums[1] + fold8(d_h1))

        sums = lax.fori_loop(0, T // ROWS, body, zero_sums(2))
        for k, at in enumerate((0, 1)):
            r.gsm[at : at + 1, :] = jnp.sum(sums[k], axis=0, keepdims=True)

    def gview(u, zs, ys, xs):
        kind, first, count = u
        if kind in "pl":
            return r.Gp.at[zs, ys, xs, pl.ds(first, count), :]
        return r.G.at[pl.ds(first, count), zs, ys, xs]

    def rview(u, plain, proj):
        kind, first, count = u
        if kind == "p":
            at = (pl.ds(0, proj.shape[0]),) + (pl.ds(0, 2),) * (len(proj.shape) - 3) + (pl.ds(first, count), slice(None))
            return proj.at[at]
        return plain.at[pl.ds(first, count)]

    def add_into(dst, extra):
        dst[...] = (dst[...].astype(F32) + extra[...].astype(F32)).astype(BF16)

    def rs1(u):
        send((u, "r1a"), gview(u, low_z(u), ny, both), rview(u, r.rA1, r.pA1), ypeer)
        send((u, "r1b"), gview(u, high_z(u), both, nx), rview(u, r.rB1, r.pB1), xpeer)

    def rs2a(u):
        va = rview(u, r.rA1, r.pA1)
        arrive((u, "r1a"), va)
        add_into(gview(u, low_z(u), y, both), va)
        send((u, "r2a"), gview(u, low_z(u), y, nx), rview(u, r.rA2, r.pA2), xpeer)

    def rs2b(u):
        vb = rview(u, r.rB1, r.pB1)
        arrive((u, "r1b"), vb)
        add_into(gview(u, high_z(u), both, x), vb)
        send((u, "r2b"), gview(u, high_z(u), ny, x), rview(u, r.rB2, r.pB2), ypeer)

    def zslot(u, k):
        kind, first, count = u
        if kind == "p":
            return r.pz.at[k - 1, pl.ds(first, count), :]
        return r.rz.at[pl.ds(first, count), k - 1]

    def rs3(u):
        va, vb = rview(u, r.rA2, r.pA2), rview(u, r.rB2, r.pB2)
        arrive((u, "r2a"), va)
        add_into(gview(u, low_z(u), y, x), va)
        arrive((u, "r2b"), vb)
        add_into(gview(u, high_z(u), y, x), vb)
        for k in (1, 2, 3):
            send((u, "rz", k), gview(u, zshift(k), y, x), zslot(u, k), zpeer(k))

    def rs4(u):
        kind, first, count = u
        for k in (1, 2, 3):
            arrive((u, "rz", k), zslot(u, k))
        total = gview(u, z, y, x)[...].astype(F32)
        for k in (1, 2, 3):
            total = total + zslot(u, k)[...].astype(F32)
        if kind == "p":
            r.ptot[pl.ds(first, count), :] = total
        else:
            r.tot[pl.ds(first, count)] = total
            give = pl.ds(pl.multiple_of(24 * nc, 8), 24)
            send((u, "fin"), r.tot.at[pl.ds(first, count), give, :], r.fr.at[pl.ds(first, count)], partner)

    def rs5(u):
        kind, first, count = u
        arrive((u, "fin"), r.fr.at[pl.ds(first, count)])
        keep = pl.ds(pl.multiple_of(24 * c, 8), 24)
        for it in range(first, first + count):
            for core, part in ((c, r.tot[it, keep, :]), (nc, r.fr[it])):
                if it < 3:
                    for j in range(3):
                        at = pl.multiple_of(j * D + 128 * (3 * core + it), 128)
                        r.gq_o[:, pl.ds(at, 128)] = part[:, 128 * j : 128 * j + 128]
                elif it == 3:
                    r.go_o[:, pl.ds(pl.multiple_of(core * HALF, 128), HALF)] = part
                else:
                    at = pl.multiple_of(core * (FF // 2) + (it - 4) * HALF, 128)
                    r.gf_o[:, pl.ds(at, HALF)] = part

    def back1(u):
        for k in (1, 2, 3):
            send((u, "b1", k), gview(u, zshift(k), both, both), r.zL.at[k - 1], zpeer(k))

    def back2(u):
        for k in (1, 2, 3):
            arrive((u, "b1", k), r.zL.at[k - 1])
        for yy in (0, 1):
            for xx in (0, 1):
                here = gview(u, z, yy, xx)
                total = here[...].astype(F32)
                for k in (1, 2, 3):
                    total = total + r.zL[k - 1, yy, xx].astype(F32)
                here[...] = total.astype(BF16)
        send((u, "b2"), gview(u, z, ny, both), r.yL, ypeer)

    def back3(u):
        arrive((u, "b2"), r.yL)
        add_into(gview(u, z, y, both), r.yL)
        send((u, "b3"), gview(u, z, y, nx), r.xL, xpeer)

    def back4(u):
        kind, first, count = u
        arrive((u, "b3"), r.xL)
        r.ptot[pl.ds(first, count), :] = gview(u, z, y, x)[...].astype(F32) + r.xL[...].astype(F32)

    def rs_proj_send():
        give = pl.ds(pl.multiple_of(96 * nc, 32), 96)
        send("pfin", r.ptot.at[give, :], r.pfr, partner)

    def rs_proj_done():
        arrive("pfin", r.pfr)
        keep = pl.ds(pl.multiple_of(96 * c, 32), 96)
        r.gp_o[:, pl.ds(pl.multiple_of(c * HALF, 128), HALF)] = r.ptot[keep, :]
        r.gp_o[:, pl.ds(pl.multiple_of(nc * HALF, 128), HALF)] = r.pfr[...]

    def small_send(key, src, at, peer):
        send(("small", key), src, r.gr.at[at], peer)

    def small_add(keys, first, into):
        total = r.gsm[...] if into is None else r.gs[into]
        for n, key in enumerate(keys):
            arrive(("small", key), r.gr.at[first + n])
            total = total + r.gr[first + n]
        return total

    tasks = {}

    def pairs(body, i):
        def one(h, carry):
            body(3 * h + i)
            return carry

        lax.fori_loop(0, 2, one, 0)

    def comm(name, u):
        tasks["2" + name] = lambda: ag2(u)
        tasks["3a" + name] = lambda: ag3a(u)
        tasks["3b" + name] = lambda: ag3b(u)
        tasks["4a" + name] = lambda: ag4a(u)
        tasks["4b" + name] = lambda: ag4b(u)
        if name != "s":
            tasks["r1" + name] = lambda: rs1(u)
            tasks["r2a" + name] = lambda: rs2a(u)
            tasks["r2b" + name] = lambda: rs2b(u)
            tasks["r3" + name] = lambda: rs3(u)
            tasks["r4" + name] = lambda: rs4(u)
            if name != "p":
                tasks["r5" + name] = lambda: rs5(u)

    for name, u in (
        ("s", US), ("q0", UQ[0]), ("q1", UQ[1]), ("q2", UQ[2]), ("o", UO), ("f0", UF[0]), ("f1", UF[1]), ("p", UP)
    ):
        comm(name, u)
    tasks["l2"] = lambda: late2(UL)
    tasks["l3"] = lambda: late3(UL)
    tasks["l41"] = lambda: late4(UL, 1)
    tasks["l42"] = lambda: late4(UL, 2)
    tasks["l43"] = lambda: late4(UL, 3)
    tasks["b1"] = lambda: back1(UL)
    tasks["b2"] = lambda: back2(UL)
    tasks["b3"] = lambda: back3(UL)
    tasks["b4"] = lambda: back4(UL)

    def task(body):
        tasks[body.__name__] = body

    @task
    def mask():
        build_mask()

    @task
    def first_norm():
        ag5(US)
        for k in (1, 2, 3):
            arrive(("tok", k), r.xb.at[lax.rem(sp + 4 - k, 4)])
        own_tok.wait()
        small_vectors()
        norm_one()
        send("h1", r.h1c.at[0], r.h1c.at[1], partner)

    def qkv(i):
        def run():
            ag5(UQ[i])
            qkv_item(i)

        return run

    def attend(i):
        return lambda: pairs(attend_pair, i)

    def attend_back(i):
        def run():
            pairs(attend_back_pair, i)
            send(("dq", i), r.qkvb.at[3 * nc + i], r.dqp.at[i], partner)

        return run

    def grad_qkv(i):
        def run():
            if i == 0:
                arrive("h1", r.h1c.at[1])
            arrive(("dq", i), r.dqp.at[i])
            qkv_grad(i)

        return run

    for i in range(3):
        tasks["qkv" + str(i)] = qkv(i)
        tasks["attend" + str(i)] = attend(i)
        tasks["attend_back" + str(i)] = attend_back(i)
        tasks["qkv_grad" + str(i)] = grad_qkv(i)

    tasks["tok2"] = lambda: send_pack("tok", r.tok, r.xb, (2,))
    tasks["tok1"] = lambda: send_pack("tok", r.tok, r.xb, (1, 3))
    tasks["dx2"] = lambda: send_rows("dx", r.dx_o, (2,))
    tasks["dx1"] = lambda: send_rows("dx", r.dx_o, (1, 3))
    tasks["cot2"] = lambda: send_pack("cot", r.cot, r.cb, (2,))
    tasks["cot1"] = lambda: send_pack("cot", r.cot, r.cb, (1, 3))

    tasks["l1"] = lambda: late1(UL)

    @task
    def out():
        send("attn", r.attnc.at[0], r.attnc.at[1], partner)
        ag5(UO)
        out_proj()
        send("h2", r.h2c.at[0], r.h2c.at[1], partner)

    @task
    def flip():
        flip_lse()
        build_mask_t()

    @task
    def rows():
        for k in (1, 2, 3):
            arrive(("cot", k), r.cb.at[lax.rem(sp + 4 - k, 4)])
        own_cot.wait()
        mlp_grad_rows()
        send("dml", half_cols(r.dml, nc), r.dml_p, partner)

    def act_cols(core, j, h):
        return r.actc.at[core, :, pl.ds(h * (FF // 2) + j * D, D)]

    def up(j):
        def run():
            ag5(UF[j])

            def one(i, carry):
                up_item(i)
                return carry

            lax.fori_loop(2 * j, 2 * j + 2, one, 0)
            for h in (0, 1):
                send(("act", j, h), act_cols(0, j, h), act_cols(1, j, h), partner)

        return run

    def proj(j):
        def run():
            if j == 0:
                arrive("dml", r.dml_p)
            for h in (0, 1):
                arrive(("act", j, h), act_cols(1, j, h))
            proj_grad(j)

        return run

    def up_weight(j):
        def run():
            if j == 0:
                arrive("h2", r.h2c.at[1])
                arrive("dpre", r.dpre_p)
            up_grad(j)

        return run

    for j in range(2):
        tasks["up" + str(j)] = up(j)
        tasks["proj" + str(j)] = proj(j)
        tasks["up_grad" + str(j)] = up_weight(j)

    @task
    def whole():
        ag5(UP)
        late5(UL)

    own = {}

    @task
    def final():
        layer_out()
        send_rows("out", r.out_o, (2, 1, 3))
        own["out"] = keep_rows(r.out_o, 2)

    @task
    def down():
        down_back()
        send("dpre", r.slope.at[:, pl.ds(pl.multiple_of(nc * (FF // 2), 128), FF // 2)], r.dpre_p, partner)

    @task
    def up_input():
        up_back()

    @task
    def second_norm():
        norm_two_back()
        send("dbr", half_cols(r.dbr, nc), r.dbr_p, partner)

    @task
    def out_input():
        out_back()

    @task
    def out_weight():
        arrive("attn", r.attnc.at[1])
        arrive("dbr", r.dbr_p)
        out_grad()

    @task
    def qkv_input():
        qkv_back()

    @task
    def last_norm():
        own["out"].wait()
        for k in (1, 2, 3):
            started.pop(("out", k)).wait_send()
        norm_one_back()
        r.gsm[12:16, :] = jnp.zeros((4, D), F32)
        small_send("x", r.gsm, 0, xpeer)
        own["dx"] = keep_rows(r.dx_o, 3)

    @task
    def small1():
        r.gs[0] = small_add(["x"], 0, None)
        small_send("core", r.gs.at[0], 1, partner)

    @task
    def small2():
        r.gs[1] = small_add(["core"], 1, 0)
        small_send("y", r.gs.at[1], 2, ypeer)

    @task
    def small3():
        r.gs[2] = small_add(["y"], 2, 1)
        for k in (1, 2, 3):
            small_send(("z", k), r.gs.at[2], 2 + k, zpeer(k))

    @task
    def small4():
        r.gs[3] = small_add([("z", 1), ("z", 2), ("z", 3)], 3, 2)
        pick_small()

    @task
    def proj_send():
        rs_proj_send()

    @task
    def proj_done():
        rs_proj_done()

    t = Bag()
    for name, body in tasks.items():
        setattr(t, "g" + name, body)
    t.gtok2()
    t.gl1()
    t.gmask()
    t.g2s()
    t.g3bs()
    t.gl2()
    t.g3as()
    t.g2q0()
    t.gtok1()
    t.g4bs()
    t.g4as()
    t.g3aq0()
    t.g2q1()
    t.g3bq0()
    t.gfirst_norm()
    t.g2q2()
    t.g3aq1()
    t.g4aq0()
    t.g3bq1()
    t.g4bq0()
    t.g2o()
    t.g3bq2()
    t.gqkv0()
    t.g3aq2()
    t.gattend0()
    t.g4aq1()
    t.g4bq1()
    t.g3ao()
    t.g3bo()
    t.gqkv1()
    t.g2f0()
    t.g4bq2()
    t.gl3()
    t.gcot2()
    t.gcot1()
    t.gattend1()
    t.g4aq2()
    t.g4bo()
    t.gqkv2()
    t.gattend2()
    t.g2f1()
    t.g3af0()
    t.g3bf0()
    t.g4ao()
    t.gflip()
    t.gout()
    t.g3bf1()
    t.grows()
    t.g3af1()
    t.g2p()
    t.g4af0()
    t.g4bf0()
    t.gup0()
    t.g4bf1()
    t.gl41()
    t.g3ap()
    t.g4af1()
    t.gproj0()
    t.g3bp()
    t.gup1()
    t.gl42()
    t.g4bp()
    t.gproj1()
    t.g4ap()
    t.gb1()
    t.gr1p()
    t.gl43()
    t.gwhole()
    t.gdown()
    t.gr2bp()
    t.gfinal()
    t.gup_input()
    t.gr2ap()
    t.gup_grad0()
    t.gr1f0()
    t.gup_grad1()
    t.gr1f1()
    t.gsecond_norm()
    t.gout_input()
    t.gattend_back0()
    t.gr3p()
    t.gr2af0()
    t.gout_weight()
    t.gr2bf0()
    t.gr1o()
    t.gattend_back1()
    t.gr2bf1()
    t.gqkv_grad0()
    t.gr1q0()
    t.gattend_back2()
    t.gr2af1()
    t.gqkv_grad1()
    t.gr1q1()
    t.gqkv_input()
    t.gb2()
    t.gr3f0()
    t.gr2bo()
    t.gr2bq0()
    t.gqkv_grad2()
    t.gr1q2()
    t.glast_norm()
    t.gr4p()
    t.gr3f1()
    t.gr2ao()
    t.gr2bq1()
    t.gr2bq2()
    t.gr2aq0()
    t.gsmall1()
    t.gsmall2()
    t.gr4f0()
    t.gr2aq1()
    t.gr5f0()
    t.gb3()
    t.gr3o()
    t.gr4f1()
    t.gr3q0()
    t.gr5f1()
    t.gb4()
    t.gproj_send()
    t.gproj_done()
    t.gr2aq2()
    t.gdx2()
    t.gdx1()
    t.gr3q1()
    t.gr4o()
    t.gsmall3()
    t.gr5o()
    t.gr3q2()
    t.gr4q0()
    t.gr5q0()
    t.gr4q1()
    t.gr5q1()
    t.gsmall4()
    t.gr4q2()
    t.gr5q2()
    for name, dst in (("out", r.out_o), ("dx", r.dx_o)):
        for k in (1, 2, 3):
            arrive((name, k), dst.at[lax.rem(sp + 4 - k, 4)])
    own["dx"].wait()
    for copy in started.values():
        copy.wait_send()
    assert len(table) <= SEMS, len(table)


def fused(tokens, cotangent, seq_cut, g1, o1, w_qkv, bq, bv, w_out, bo, g2, o2, w_fc, bf, w_proj, bp):
    flat = jnp.concatenate([v[None] for v in (g1, o1, bq, bv, bo, g2, o2, bp, bf)] + [jnp.zeros((1, 96), BF16)], axis=1)
    vmem = pl.BlockSpec(memory_space=pltpu.VMEM)
    anywhere = pl.BlockSpec(memory_space=pl.ANY)
    s = jax.ShapeDtypeStruct
    out, d_x, gq, go, gf, gp, gs = pl.pallas_call(
        mega,
        out_shape=(
            s((4, 128, D), BF16),
            s((4, 128, D), BF16),
            s((24, 3 * D), F32),
            s((24, D), F32),
            s((24, FF), F32),
            s((96, D), F32),
            s((16, 128), F32),
        ),
        in_specs=[anywhere, anywhere] + [vmem] * 6,
        out_specs=(anywhere, anywhere) + (vmem,) * 5,
        scratch_shapes=scratch_shapes(),
        compiler_params=pltpu.CompilerParams(collective_id=0, has_side_effects=True, vmem_limit_bytes=67043328),
    )(tokens, cotangent, seq_cut, w_qkv, w_out, w_fc, w_proj, flat)
    rows, g_bf = gs[:8, :24], gs[8, 32:]
    return (out, d_x.astype(F32), rows[0], rows[1], gq, rows[2], rows[3], go, rows[4], rows[5], rows[6], gf, g_bf, gp, rows[7])


def solution(mesh):
    row = P(AXES, None)
    vec = P(AXES)
    act = P(None, AXES, None)
    body = fused if dict(mesh.shape) == {"dp": 8, "sp": 4} else local
    return jax.shard_map(
        body,
        mesh=mesh,
        in_specs=(act, act, P(None, "dp"), vec, vec, row, vec, vec, row, vec, vec, vec, row, vec, row, vec),
        out_specs=(act, act, vec, vec, row, vec, vec, row, vec, vec, vec, row, vec, row, vec),
        check_vma=False,
    )
```

```python
import functools

import jax
import jax.numpy as jnp
from jax import lax
from jax.experimental import pallas as pl
from jax.experimental.pallas import tpu as pltpu
from jax.sharding import PartitionSpec as P

HEADS = 12
HEAD = 64
EPSILON = 1e-05
BRANCH = 24.0 ** (-0.5)
NEGATIVE = -1e30
GELU_A = 0.7978845608028654
GELU_B = 0.044715
AXES = ("dp", "sp")
F32 = jnp.float32
BF16 = jnp.bfloat16
MESH = pl.DeviceIdType.MESH

def dot(a, b, dims):
    return lax.dot_general(a, b, (dims, ((), ())), preferred_element_type=F32)


def mm(a, b):
    return dot(a, b, ((1,), (0,)))


def mm_nt(a, b):
    return dot(a, b, ((1,), (1,)))


def mm_tn(a, b):
    return dot(a, b, ((0,), (0,)))


def norm_stats(rows):
    center = jnp.mean(rows, axis=-1, keepdims=True)
    centred = rows - center
    inverse = lax.rsqrt(jnp.mean(centred * centred, axis=-1, keepdims=True) + EPSILON)
    return centred * inverse, inverse


def norm_back(xhat, inverse, grad):
    mean_grad = jnp.mean(grad, axis=-1, keepdims=True)
    mean_proj = jnp.mean(grad * xhat, axis=-1, keepdims=True)
    return inverse * (grad - mean_grad - xhat * mean_proj)


def split_heads(rows):
    return rows.reshape(rows.shape[0], HEADS, HEAD).transpose(1, 0, 2)


def join_heads(heads):
    return heads.transpose(1, 0, 2).reshape(heads.shape[1], HEADS * HEAD)


def layer(x16, dy16, cut, big, small):
    w_qkv, w_out, w_fc, w_proj = big
    g1, o1, bq, bv, bo, g2, o2, bf, bp = [v.astype(F32)[None] for v in small]
    length = x16.shape[0]
    x = x16.astype(F32)
    xhat1, inv1 = norm_stats(x)
    h1 = (xhat1 * g1 + o1).astype(BF16)
    bias = jnp.concatenate([bq, jnp.zeros_like(bq), bv], axis=1)
    qkv = (mm(h1, w_qkv) + bias).astype(BF16)
    width = HEADS * HEAD
    q, k, v = (split_heads(qkv[:, i * width : (i + 1) * width]) for i in range(3))
    pos = lax.iota(jnp.int32, length)
    allowed = (pos[None, :] <= pos[:, None]) & ((pos[None, :] >= cut) == (pos[:, None] >= cut))
    scale = HEAD ** (-0.5)
    scores = jnp.einsum("hqd,hkd->hqk", q, k, preferred_element_type=F32) * scale
    scores = jnp.where(allowed[None], scores, NEGATIVE)
    top = jnp.max(scores, axis=-1, keepdims=True)
    expo = jnp.exp(scores - top)
    prob32 = expo / jnp.sum(expo, axis=-1, keepdims=True)
    prob = prob32.astype(BF16)
    attn32 = jnp.einsum("hqk,hkd->hqd", prob, v, preferred_element_type=F32)
    attn = join_heads(attn32).astype(BF16)
    x1 = x + BRANCH * (mm(attn, w_out) + bo)
    xhat2, inv2 = norm_stats(x1)
    h2 = (xhat2 * g2 + o2).astype(BF16)
    pre = mm(h2, w_fc) + bf
    t = jnp.tanh(GELU_A * (pre + GELU_B * pre * pre * pre))
    act = (0.5 * pre * (1 + t)).astype(BF16)
    slope = 0.5 * (1 + t) + 0.5 * pre * (1 - t * t) * (GELU_A * (1 + 3 * GELU_B * pre * pre))
    out = (x1 + BRANCH * (mm(act, w_proj) + bp)).astype(BF16)

    dy = dy16.astype(F32)
    d_mlp = (dy * BRANCH).astype(BF16)
    g_w_proj = mm_tn(act, d_mlp)
    g_b_proj = jnp.sum(d_mlp.astype(F32), axis=0)
    d_pre = (mm_nt(d_mlp, w_proj) * slope).astype(BF16)
    g_w_fc = mm_tn(h2, d_pre)
    g_b_fc = jnp.sum(d_pre.astype(F32), axis=0)
    d_h2 = mm_nt(d_pre, w_fc)
    g_g2 = jnp.sum(d_h2 * xhat2, axis=0)
    g_o2 = jnp.sum(d_h2, axis=0)
    d_x1 = dy + norm_back(xhat2, inv2, d_h2 * g2)
    d_branch = (d_x1 * BRANCH).astype(BF16)
    g_w_out = mm_tn(attn, d_branch)
    g_b_out = jnp.sum(d_branch.astype(F32), axis=0)
    d_attn = split_heads(mm_nt(d_branch, w_out).astype(BF16))
    delta = jnp.sum(d_attn.astype(F32) * attn32, axis=-1, keepdims=True)
    d_prob = jnp.einsum("hqd,hkd->hqk", d_attn, v, preferred_element_type=F32)
    d_scores = (prob32 * (d_prob - delta)).astype(BF16)
    d_q = jnp.einsum("hqk,hkd->hqd", d_scores, k, preferred_element_type=F32) * scale
    d_k = jnp.einsum("hqk,hqd->hkd", d_scores, q, preferred_element_type=F32) * scale
    d_v = jnp.einsum("hqk,hqd->hkd", prob, d_attn, preferred_element_type=F32)
    d_qkv = jnp.concatenate([join_heads(d_q), join_heads(d_k), join_heads(d_v)], axis=1).astype(BF16)
    g_w_qkv = mm_tn(h1, d_qkv)
    g_b_qkv = jnp.sum(d_qkv.astype(F32), axis=0)
    d_h1 = mm_nt(d_qkv, w_qkv)
    g_g1 = jnp.sum(d_h1 * xhat1, axis=0)
    g_o1 = jnp.sum(d_h1, axis=0)
    d_x = d_x1 + norm_back(xhat1, inv1, d_h1 * g1)
    big_grads = (g_w_qkv, g_w_out, g_w_fc, g_w_proj)
    small_grads = (g_g1, g_o1, g_b_qkv[:width], g_b_qkv[2 * width :], g_b_out, g_g2, g_o2, g_b_fc, g_b_proj)
    return out, d_x, big_grads, small_grads


def local(tokens, cotangent, seq_cut, g1, o1, w_qkv, bq, bv, w_out, bo, g2, o2, w_fc, bf, w_proj, bp):
    ways = lax.axis_size("sp")
    devices = ways * lax.axis_size("dp")
    small = (g1, o1, bq, bv, bo, g2, o2, bf, bp)
    sizes = [v.shape[0] for v in small]
    big = [lax.all_gather(w, AXES, axis=0, tiled=True) for w in (w_qkv, w_out, w_fc, w_proj)]
    packed = lax.all_gather(jnp.concatenate(small), AXES, axis=0)
    cuts = [sum(sizes[:i]) for i in range(len(sizes) + 1)]
    vectors = [packed[:, a:b].reshape(-1) for a, b in zip(cuts[:-1], cuts[1:])]
    x16 = lax.all_to_all(tokens, "sp", split_axis=0, concat_axis=1, tiled=True)
    dy16 = lax.all_to_all(cotangent, "sp", split_axis=0, concat_axis=1, tiled=True)
    packs = x16.shape[0]
    first = lax.axis_index("sp") * packs
    outs, grads_in, big_sum, small_sum = [], [], None, None
    for i in range(packs):
        cut = lax.dynamic_slice(seq_cut, (first + i, 0), (1, 1))[0, 0]
        out, d_x, bigs, smalls = layer(x16[i], dy16[i], cut, big, vectors)
        outs.append(out)
        grads_in.append(d_x)
        big_sum = bigs if big_sum is None else [a + b for a, b in zip(big_sum, bigs)]
        small_sum = smalls if small_sum is None else [a + b for a, b in zip(small_sum, smalls)]
    out = lax.all_to_all(jnp.stack(outs), "sp", split_axis=1, concat_axis=0, tiled=True)
    d_x = lax.all_to_all(jnp.stack(grads_in), "sp", split_axis=1, concat_axis=0, tiled=True)
    big_out = [
        lax.psum_scatter(g.astype(BF16), AXES, scatter_dimension=0, tiled=True).astype(F32) for g in big_sum
    ]
    small_pack = jnp.concatenate([g.reshape(devices, -1) for g in small_sum], axis=1)
    small_out = lax.psum_scatter(small_pack, AXES, scatter_dimension=0, tiled=True)[0]
    s = [small_out[a:b] for a, b in zip(cuts[:-1], cuts[1:])]
    return (out, d_x, s[0], s[1], big_out[0], s[2], s[3], big_out[1], s[4], s[5], s[6], big_out[2], s[7], big_out[3], s[8])

T, D, FF, HALF = 512, 768, 3072, 384
ZS = 4
ZA = 3
PZ = 3
ROWS = 32
NORM = 64


class Bag:
    pass


def rows_loop(count, step, body):
    def one(i, carry):
        body(pl.multiple_of(i * step, step))
        return carry

    lax.fori_loop(0, count // step, one, 0)


def fold8(values):
    return jnp.sum(values.reshape(values.shape[0] // 8, 8, values.shape[1]), axis=0)


def zero_sums(count):
    return tuple(jnp.zeros((8, D), F32) for _ in range(count))


NAMES = (
    "tok", "cot", "cut", "wq", "wo", "wf", "wp", "flat", "out_o", "dx_o", "gq_o", "go_o", "gf_o", "gp_o", "gs_o",
    "W", "Wp", "Sw", "sq", "so", "sf", "sp_", "ssm", "vec", "G", "Gp", "rA1", "rB1", "pA1", "pB1", "rA2", "rB2",
    "pA2", "pB2", "rz", "pz", "zL", "yL", "xL", "tot", "ptot", "fr", "pfr", "xb", "cb", "h1c", "qkvb", "attnc", "x1", "h2c", "actc",
    "slope", "dpre_p", "acc", "dbr", "dbr_p", "dml", "dml_p", "dat", "dqp", "ob", "mask", "lse", "lseT", "gsm", "gs",
    "gr", "small", "ssem", "rsem", "lsem",
)
SEMS = 220


def scratch_shapes():
    v = pltpu.VMEM
    return [
        v((8, 2, ZS, 2, 2, 48, HALF), BF16),
        v((2, ZS, 2, 2, 192, HALF), BF16),
        v((2, ZS, 2, 2, 16, HALF), BF16),
        v((24, 3 * D), BF16),
        v((24, D), BF16),
        v((24, FF), BF16),
        v((96, D), BF16),
        v((16, D), BF16),
        v((16, D), F32),
        v((8, ZS, 2, 2, 48, HALF), BF16),
        v((ZS, 2, 2, 192, HALF), BF16),
        v((8, ZA, 2, 48, HALF), BF16),
        v((8, ZS - ZA, 2, 48, HALF), BF16),
        v((PZ, 2, 96, HALF), BF16),
        v((ZS - PZ, 2, 96, HALF), BF16),
        v((8, ZA, 48, HALF), BF16),
        v((8, ZS - ZA, 48, HALF), BF16),
        v((PZ, 96, HALF), BF16),
        v((ZS - PZ, 96, HALF), BF16),
        v((8, 3, 48, HALF), BF16),
        v((3, 96, HALF), BF16),
        v((3, 2, 2, 96, HALF), BF16),
        v((2, 96, HALF), BF16),
        v((96, HALF), BF16),
        v((8, 48, HALF), F32),
        v((192, HALF), F32),
        v((8, 24, HALF), F32),
        v((96, HALF), F32),
        v((4, 128, D), BF16),
        v((4, 128, D), BF16),
        v((2, T, D), BF16),
        v((6, T, HALF), BF16),
        v((2, T, D), BF16),
        v((T, D), F32),
        v((2, T, D), BF16),
        v((2, T, FF), BF16),
        v((T, FF), BF16),
        v((T, FF // 2), BF16),
        v((T, D), F32),
        v((T, D), BF16),
        v((T, HALF), BF16),
        v((T, D), BF16),
        v((T, HALF), BF16),
        v((T, D), BF16),
        v((3, T, HALF), BF16),
        v((T, D), BF16),
        v((T, T), F32),
        v((T, 128), F32),
        v((128, T), F32),
        v((16, D), F32),
        v((4, 16, D), F32),
        v((6, 16, D), F32),
        v((16, D), BF16),
        pltpu.SemaphoreType.DMA((SEMS,)),
        pltpu.SemaphoreType.DMA((SEMS,)),
        pltpu.SemaphoreType.DMA((4,)),
    ]


def mega(*refs):
    r = Bag()
    assert len(refs) == len(NAMES), (len(refs), len(NAMES))
    for name, ref in zip(NAMES, refs):
        setattr(r, name, ref)
    dp, sp = lax.axis_index("dp"), lax.axis_index("sp")
    z, y = dp // 2, lax.rem(dp, 2)
    x, c = sp // 2, lax.rem(sp, 2)
    nx, ny, nc = 1 - x, 1 - y, 1 - c
    partner = {"dp": dp, "sp": x * 2 + nc}
    xpeer = {"dp": dp, "sp": nx * 2 + c}
    ypeer = {"dp": z * 2 + ny, "sp": sp}
    every = pl.ds(0, ZS)

    def low_z(u):
        return pl.ds(0, PZ if u[0] == "p" else ZA)

    def high_z(u):
        first = PZ if u[0] == "p" else ZA
        return pl.ds(first, ZS - first)

    both = pl.ds(0, 2)

    def zshift(k):
        return lax.rem(z + k, ZS)

    def zpeer(k):
        return {"dp": zshift(k) * 2 + y, "sp": sp}

    def speer(k):
        return lax.rem(sp + k, 4)

    table = {}
    started = {}

    def slot(key):
        return table.setdefault(key, len(table))

    def send(key, src, dst, device):
        i = slot(key)
        copy = pltpu.make_async_remote_copy(
            src_ref=src, dst_ref=dst, send_sem=r.ssem.at[i], recv_sem=r.rsem.at[i], device_id=device, device_id_type=MESH
        )
        copy.start()
        started[key] = copy
        return copy

    def arrive(key, dst):
        i = slot(key)
        pltpu.make_async_remote_copy(
            src_ref=dst, dst_ref=dst, send_sem=r.ssem.at[i], recv_sem=r.rsem.at[i], device_id=partner, device_id_type=MESH
        ).wait_recv()

    barrier = pltpu.get_barrier_semaphore()
    peers = [{"dp": dp, "sp": speer(k)} for k in (1, 2, 3)] + [ypeer] + [zpeer(k) for k in (1, 2, 3)]
    for peer in peers:
        pl.semaphore_signal(barrier, inc=1, device_id=peer, device_id_type=MESH)
    pl.semaphore_wait(barrier, len(peers))

    def view(u, h, zs, ys, xs):
        kind, first, count = u
        if kind == "s":
            return r.Sw.at[h, zs, ys, xs]
        if kind in "pl":
            return r.Wp.at[h, zs, ys, xs, pl.ds(first, count), :]
        return r.W.at[pl.ds(first, count), h, zs, ys, xs]

    def ag1(u):
        for k in (1, 2, 3):
            v = view(u, c, z, y, x)
            send((u, "z", k), v, v, zpeer(k))

    def ag2(u):
        for k in (1, 2, 3):
            arrive((u, "z", k), view(u, c, zshift(ZS - k), y, x))
        v = view(u, c, low_z(u), y, x)
        send((u, "2a"), v, v, xpeer)
        v = view(u, c, high_z(u), y, x)
        send((u, "2b"), v, v, ypeer)
        v = view(u, c, every, y, x)
        send((u, "c0"), v, v, partner)

    def ag3a(u):
        arrive((u, "2a"), view(u, c, low_z(u), y, nx))
        v = view(u, c, low_z(u), y, both)
        send((u, "3a"), v, v, ypeer)
        v = view(u, c, low_z(u), y, nx)
        send((u, "c1"), v, v, partner)

    def ag3b(u):
        arrive((u, "2b"), view(u, c, high_z(u), ny, x))
        v = view(u, c, high_z(u), both, x)
        send((u, "3b"), v, v, xpeer)
        v = view(u, c, high_z(u), ny, x)
        send((u, "c2"), v, v, partner)

    def ag4a(u):
        v = view(u, c, low_z(u), ny, both)
        arrive((u, "3a"), v)
        send((u, "c3"), v, v, partner)

    def ag4b(u):
        v = view(u, c, high_z(u), both, nx)
        arrive((u, "3b"), v)
        send((u, "c4"), v, v, partner)

    def ag5(u):
        arrive((u, "c0"), view(u, nc, every, y, x))
        arrive((u, "c1"), view(u, nc, low_z(u), y, nx))
        arrive((u, "c2"), view(u, nc, high_z(u), ny, x))
        arrive((u, "c3"), view(u, nc, low_z(u), ny, both))
        arrive((u, "c4"), view(u, nc, high_z(u), both, nx))

    def late1(u):
        v = view(u, c, z, y, x)
        send((u, "lx"), v, v, xpeer)
        send((u, "ly"), v, v, ypeer)

    def late2(u):
        v = view(u, c, z, y, nx)
        arrive((u, "lx"), v)
        send((u, "ld"), v, v, ypeer)

    def late3(u):
        arrive((u, "ly"), view(u, c, z, ny, x))
        arrive((u, "ld"), view(u, c, z, ny, nx))
        v = view(u, c, z, both, both)
        for k in (1, 2, 3):
            send((u, "lz", k), v, v, zpeer(k))
        send((u, "c", 0), v, v, partner)

    def late4(u, k):
        v = view(u, c, zshift(ZS - k), both, both)
        arrive((u, "lz", k), v)
        send((u, "c", k), v, v, partner)

    def late5(u):
        for k in (0, 1, 2, 3):
            arrive((u, "c", k), view(u, nc, zshift(ZS - k), both, both))

    US = ("s", 0, 16)
    UQ = [("w", i, 1) for i in range(3)]
    UO = ("w", 3, 1)
    UF = [("w", 4, 2), ("w", 6, 2)]
    UP = ("p", 0, 96)
    UL = ("l", 96, 96)

    device = dp * 4 + sp
    low = 24 * device
    wide_row, wide_low = device // 8, 96 * lax.rem(device, 8)

    def build_small():
        i = lax.broadcasted_iota(jnp.int32, (384, 1), 0)
        part = sum((i >= 24 * m).astype(jnp.int32) for m in range(1, 8))
        target = jnp.where(i < 192, low + i - 24 * part, wide_low + i - 192)
        target = jnp.where(i < 288, target, -1)
        j = lax.broadcasted_iota(jnp.int32, (384, D), 1)
        place = jnp.where(j == target, 1.0, 0.0).astype(BF16)
        row = lax.broadcasted_iota(jnp.int32, (16, 384), 0)
        lane = lax.broadcasted_iota(jnp.int32, (16, 384), 1)
        mine = (row < 8) & (lane >= 24 * row) & (lane < 24 * row + 24)
        mine = mine | ((row == 8 + wide_row) & (lane >= 192))
        values = jnp.where(mine, jnp.broadcast_to(r.flat[...].astype(F32), (16, 384)), 0.0).astype(BF16)
        r.small[...] = lax.dot_general(values, place, (((1,), (0,)), ((), ())), preferred_element_type=F32).astype(BF16)

    def pick_small():
        j = lax.broadcasted_iota(jnp.int32, (D, 128), 0)
        lane = lax.broadcasted_iota(jnp.int32, (D, 128), 1)
        take = ((lane < 24) & (j == low + lane)) | ((lane >= 32) & (j == wide_low + lane - 32))
        picked = lax.dot_general(
            r.gs[3], jnp.where(take, 1.0, 0.0), (((1,), (0,)), ((), ())), preferred_element_type=F32,
            precision=lax.Precision.HIGHEST,
        )
        row = lax.broadcasted_iota(jnp.int32, (16, 128), 0)
        one = jnp.sum(jnp.where(row == 8 + wide_row, picked, 0.0), axis=0, keepdims=True)
        r.gs_o[...] = jnp.where(row < 8, picked, one)

    swaps = [("wq", r.wq, r.sq), ("wp", r.wp, r.sp_), ("wo", r.wo, r.so), ("wf", r.wf, r.sf)]
    for key, src, dst in swaps:
        send(key, src, dst, partner)
    build_small()
    send("small", r.small, r.ssm, partner)

    def send_pack(key, src, dst, shifts):
        for k in shifts:
            send((key, k), src.at[speer(k)], dst.at[sp], {"dp": dp, "sp": speer(k)})

    own_tok = pltpu.make_async_copy(r.tok.at[sp], r.xb.at[sp], r.lsem.at[0])
    own_tok.start()
    own_cot = pltpu.make_async_copy(r.cot.at[sp], r.cb.at[sp], r.lsem.at[1])
    own_cot.start()
    first_core = c == 0

    def pair_rows(own, other, col, width):
        a = own[:, pl.ds(pl.multiple_of(col, 128), width)].astype(F32)
        b = other[:, pl.ds(pl.multiple_of(col, 128), width)].astype(F32)
        return jnp.concatenate([jnp.where(first_core, a, b), jnp.where(first_core, b, a)], axis=0).astype(BF16)

    arrive("small", r.ssm)
    cols = pl.ds(pl.multiple_of(c * HALF, 128), HALF)
    r.Sw[c, z, y, x] = (r.small[:, cols].astype(F32) + r.ssm[:, cols].astype(F32)).astype(BF16)
    ag1(US)
    arrive("wq", r.sq)
    for i in range(3):
        for j in range(3):
            r.W[i, c, z, y, x, :, pl.ds(128 * j, 128)] = pair_rows(r.wq, r.sq, j * D + 128 * (3 * c + i), 128)
        ag1(UQ[i])
    arrive("wp", r.sp_)
    r.Wp[c, z, y, x, pl.ds(pl.multiple_of(96 * c, 32), 96), :] = r.wp[:, cols]
    r.Wp[c, z, y, x, pl.ds(pl.multiple_of(96 * nc, 32), 96), :] = r.sp_[:, cols]
    arrive("wo", r.so)
    r.W[3, c, z, y, x] = pair_rows(r.wo, r.so, c * HALF, HALF)
    ag1(UO)
    arrive("wf", r.sf)
    for i in range(4):
        r.W[4 + i, c, z, y, x] = pair_rows(r.wf, r.sf, c * (FF // 2) + i * HALF, HALF)
    ag1(UF[0])
    ag1(UF[1])
    ag1(UP)

    def dot(a, b, ca, cb):
        return lax.dot_general(a, b, (((ca,), (cb,)), ((), ())), preferred_element_type=F32)

    def wide(item):
        return jnp.concatenate([r.W[item, h].reshape(D, HALF) for h in (0, 1)], axis=1)

    def tile_x(buf, row, size):
        return buf[row // 128, pl.ds(pl.multiple_of(lax.rem(row, 128), size), size), :].astype(F32)

    def vrow(i):
        return r.vec[i : i + 1, :]

    def stats(v):
        center = jnp.mean(v, axis=-1, keepdims=True)
        centred = v - center
        inverse = lax.rsqrt(jnp.mean(centred * centred, axis=-1, keepdims=True) + EPSILON)
        return centred * inverse, inverse

    def norm_back(xhat, inverse, grad):
        return inverse * (grad - jnp.mean(grad, axis=-1, keepdims=True) - xhat * jnp.mean(grad * xhat, axis=-1, keepdims=True))

    def build_mask():
        def body(row):
            q = lax.broadcasted_iota(jnp.int32, (ROWS, T), 0) + row
            k = lax.broadcasted_iota(jnp.int32, (ROWS, T), 1)
            cut = r.cut[pl.ds(sp, 1), :]
            ok = (k <= q) & ((k >= cut) == (q >= cut))
            r.mask[pl.ds(row, ROWS), :] = jnp.where(ok, 0.0, NEGATIVE)

        rows_loop(T, ROWS, body)

    def build_mask_t():
        def body(row):
            k = lax.broadcasted_iota(jnp.int32, (ROWS, T), 0) + row
            q = lax.broadcasted_iota(jnp.int32, (ROWS, T), 1)
            cut = r.cut[pl.ds(sp, 1), :]
            ok = (k <= q) & ((k >= cut) == (q >= cut))
            r.mask[pl.ds(row, ROWS), :] = jnp.where(ok, 0.0, NEGATIVE)

        rows_loop(T, ROWS, body)

    def small_vectors():
        for h in (0, 1):
            total = jnp.zeros((16, HALF), F32)
            for zz in range(ZS):
                for yy in (0, 1):
                    for xx in (0, 1):
                        total = total + r.Sw[h, zz, yy, xx].astype(F32)
            r.vec[:, pl.ds(h * HALF, HALF)] = total

    def norm_one():
        def body(row):
            xhat, _ = stats(tile_x(r.xb, row, NORM))
            r.h1c[0, pl.ds(row, NORM), :] = (xhat * vrow(0) + vrow(1)).astype(BF16)

        rows_loop(T, NORM, body)

    def qkv_item(i):
        res = dot(r.h1c[0], wide(i), 1, 0)
        for h in (0, 1):
            p = 3 * h + i
            q = res[:, h * HALF : h * HALF + 128] + r.vec[2:3, 128 * p : 128 * p + 128]
            k = res[:, h * HALF + 128 : h * HALF + 256]
            v = res[:, h * HALF + 256 : h * HALF + 384] + r.vec[3:4, 128 * p : 128 * p + 128]
            r.qkvb[p, :, 0:128] = (q.astype(BF16).astype(F32) * (HEAD**-0.5)).astype(BF16)
            r.qkvb[p, :, 128:256] = k.astype(BF16)
            r.qkvb[p, :, 256:384] = v.astype(BF16)

    QB = 256

    def lane_masks(rows):
        lane = lax.broadcasted_iota(jnp.int32, (rows, 128), 1)
        return lane

    def attend_pair(p):
        lane = lane_masks(QB)

        def block(qb):
            keys = QB * (qb + 1)
            rows = pl.ds(QB * qb, QB)
            q2 = r.qkvb[p, rows, 0:128]
            k2 = r.qkvb[p, 0:keys, 128:256]
            v2 = r.qkvb[p, 0:keys, 256:384]
            outs = []
            for hh in (0, 1):
                mine = (lane < HEAD) if hh == 0 else (lane >= HEAD)
                qm = jnp.where(mine, q2, jnp.zeros_like(q2))
                s = dot(qm, k2, 1, 1) + r.mask[rows, 0:keys]
                top = jnp.max(s, axis=1, keepdims=True)
                e = jnp.exp(s - top)
                total = jnp.sum(e, axis=1, keepdims=True)
                outs.append(dot(e.astype(BF16), v2, 1, 0) / total)
                r.lse[rows, :] = jnp.where(lane == 2 * p + hh, top + jnp.log(total), r.lse[rows, :])
            both_heads = jnp.where(lane < HEAD, outs[0], outs[1]).astype(BF16)
            r.attnc[0, rows, pl.ds(pl.multiple_of(128 * p, 128), 128)] = both_heads

        for qb in range(T // QB):
            block(qb)

    def out_proj():
        r.acc[...] = dot(r.attnc[0], wide(3), 1, 0)

        def body(row):
            v = tile_x(r.xb, row, NORM) + BRANCH * (r.acc[pl.ds(row, NORM), :] + vrow(4))
            r.x1[pl.ds(row, NORM), :] = v
            xhat, _ = stats(v)
            r.h2c[0, pl.ds(row, NORM), :] = (xhat * vrow(5) + vrow(6)).astype(BF16)

        rows_loop(T, NORM, body)

    def up_item(i):
        r.acc[...] = dot(r.h2c[0], wide(4 + i), 1, 0)
        for h in (0, 1):
            col = pl.multiple_of(h * (FF // 2) + i * HALF, 128)
            at = h * 2 + i // 2
            bias = r.vec[pl.ds(8 + at, 1), pl.ds(pl.multiple_of(lax.rem(i, 2) * HALF, 128), HALF)]

            def body(row):
                pre = r.acc[pl.ds(row, ROWS), pl.ds(h * HALF, HALF)] + bias
                square = pre * pre
                t = jnp.tanh(pre * (GELU_A + (GELU_A * GELU_B) * square))
                half_one = 0.5 * (1.0 + t)
                r.actc[0, pl.ds(row, ROWS), pl.ds(col, HALF)] = (pre * half_one).astype(BF16)
                inner = GELU_A + (3.0 * GELU_A * GELU_B) * square
                r.slope[pl.ds(row, ROWS), pl.ds(col, HALF)] = (
                    half_one + (0.5 * pre) * (1.0 - t * t) * inner
                ).astype(BF16)

            rows_loop(T, ROWS, body)

    def wp_group(g):
        return jnp.concatenate([r.Wp[h, g].reshape(D, HALF) for h in (0, 1)], axis=1)

    def group_cols(g):
        return pl.ds(pl.multiple_of(g * D, 128), D)

    def mlp_grad_rows():
        def body(row, sums):
            d = (tile_x(r.cb, row, ROWS) * BRANCH).astype(BF16)
            r.dml[pl.ds(row, ROWS), :] = d
            return sums + fold8(d.astype(F32))

        sums = lax.fori_loop(0, T // ROWS, lambda i, s: body(pl.multiple_of(i * ROWS, ROWS), s), jnp.zeros((8, D), F32))
        r.gsm[7:8, :] = jnp.sum(sums, axis=0, keepdims=True)

    def layer_out():
        r.acc[...] = dot(r.actc[0, :, 0:D], wp_group(0), 1, 0)

        def group(g, carry):
            r.acc[...] += dot(r.actc[0, :, group_cols(g)], wp_group(g), 1, 0)
            return carry

        lax.fori_loop(1, 4, group, 0)

        def body(row):
            v = r.x1[pl.ds(row, ROWS), :] + BRANCH * (r.acc[pl.ds(row, ROWS), :] + vrow(7))
            r.ob[pl.ds(row, ROWS), :] = v.astype(BF16)

        rows_loop(T, ROWS, body)

    def send_rows(key, dst, shifts):
        for k in shifts:
            src = r.ob.at[pl.ds(pl.multiple_of(128 * speer(k), 128), 128), :]
            send((key, k), src, dst.at[sp], {"dp": dp, "sp": speer(k)})
    def keep_rows(dst, sem):
        own = pltpu.make_async_copy(r.ob.at[pl.ds(pl.multiple_of(128 * sp, 128), 128), :], dst.at[sp], r.lsem.at[sem])
        own.start()
        return own

    def down_back():
        def group(g, carry):
            r.acc[...] = dot(r.dml[...], wp_group(g), 1, 1)

            def body(i, sums):
                row = pl.multiple_of(i * ROWS, ROWS)
                here = (pl.ds(row, ROWS), group_cols(g))
                d = (r.acc[pl.ds(row, ROWS), :] * r.slope[here].astype(F32)).astype(BF16)
                r.slope[here] = d
                return sums + fold8(d.astype(F32))

            sums = lax.fori_loop(0, T // ROWS, body, jnp.zeros((8, D), F32))
            r.gsm[pl.ds(8 + g, 1), :] = jnp.sum(sums, axis=0, keepdims=True)
            return carry

        lax.fori_loop(0, 4, group, 0)

    def up_back():
        def one(i):
            lhs = jnp.concatenate(
                [r.slope[:, pl.ds(pl.multiple_of(h * (FF // 2) + i * HALF, 128), HALF)] for h in (0, 1)], axis=1
            )
            return dot(lhs, wide(4 + i), 1, 1)

        r.acc[...] = one(0)

        def item(i, carry):
            r.acc[...] += one(i)
            return carry

        lax.fori_loop(1, 4, item, 0)

    def half_cols(ref, core):
        return ref.at[:, pl.ds(pl.multiple_of(core * HALF, 128), HALF)]

    def proj_grad(first):
        def chunk(n, carry):
            f = 2 * first + lax.rem(n, 2) + 4 * (n // 2)
            at = pl.ds(pl.multiple_of(f * HALF, 128), HALF)
            res = dot(r.actc[0, :, at], half_cols(r.dml, c)[...], 0, 0) + dot(r.actc[1, :, at], r.dml_p[...], 0, 0)
            r.Gp[f // 2, lax.rem(f, 2)] = res.astype(BF16).reshape(2, 192, HALF)
            return carry

        lax.fori_loop(0, 4, chunk, 0)

    def up_grad(u):
        own = r.slope[:, pl.ds(pl.multiple_of(c * (FF // 2) + u * D, 128), D)]
        res = dot(r.h2c[0], own, 0, 0) + dot(r.h2c[1], r.dpre_p[:, u * D : u * D + D], 0, 0)
        for k in (0, 1):
            r.G[4 + 2 * u + k] = res[:, k * HALF : k * HALF + HALF].astype(BF16).reshape(ZS, 2, 2, 48, HALF)

    def norm_two_back():
        def body(i, sums):
            row = pl.multiple_of(i * NORM, NORM)
            here = pl.ds(row, NORM)
            xhat, inverse = stats(r.x1[here, :])
            d_h2 = r.acc[here, :]
            d_x1 = tile_x(r.cb, row, NORM) + norm_back(xhat, inverse, d_h2 * vrow(5))
            r.x1[here, :] = d_x1
            d_branch = (d_x1 * BRANCH).astype(BF16)
            r.dbr[here, :] = d_branch
            return (
                sums[0] + fold8(d_h2 * xhat),
                sums[1] + fold8(d_h2),
                sums[2] + fold8(d_branch.astype(F32)),
            )

        sums = lax.fori_loop(0, T // NORM, body, zero_sums(3))
        for k, at in enumerate((5, 6, 4)):
            r.gsm[at : at + 1, :] = jnp.sum(sums[k], axis=0, keepdims=True)

    def out_back():
        r.dat[...] = dot(r.dbr[...], wide(3), 1, 1).astype(BF16)

    def out_grad():
        res = dot(r.attnc[0], half_cols(r.dbr, c)[...], 0, 0) + dot(r.attnc[1], r.dbr_p[...], 0, 0)
        r.G[3] = res.astype(BF16).reshape(ZS, 2, 2, 48, HALF)

    def flip_lse():
        r.lseT[...] = jnp.transpose(r.lse[...])

    def attend_back_pair(p):
        KB = 256
        cols = pl.ds(pl.multiple_of(128 * p, 128), 128)
        lane = lane_masks(KB)
        da = r.dat[:, cols]
        prod = da.astype(F32) * r.attnc[0, :, cols].astype(F32)
        pick = jnp.where(
            (lax.broadcasted_iota(jnp.int32, (8, 128), 1) // HEAD) == lax.broadcasted_iota(jnp.int32, (8, 128), 0), 1.0, 0.0
        ).astype(F32)
        delta = lax.dot_general(
            pick, prod, (((1,), (1,)), ((), ())), preferred_element_type=F32, precision=lax.Precision.HIGHEST
        )
        q2 = r.qkvb[p, :, 0:128]
        dq_parts = [None, None]
        results = []
        for kb in (0, 1):
            first = KB * kb
            keys = pl.ds(first, KB)
            k2 = r.qkvb[p, keys, 128:256]
            v2 = r.qkvb[p, keys, 256:384]
            dks, dvs, dqs = [], [], []
            for hh in (0, 1):
                mine = (lane < HEAD) if hh == 0 else (lane >= HEAD)
                km = jnp.where(mine, k2, jnp.zeros_like(k2))
                vm = jnp.where(mine, v2, jnp.zeros_like(v2))
                logs = r.lseT[pl.ds(2 * p + hh, 1), :]
                s = dot(km, q2[first:], 1, 1) + r.mask[keys, first:]
                prob = jnp.exp(s - logs[:, first:])
                dprob = dot(vm, da[first:], 1, 1)
                ds = (prob * (dprob - delta[hh : hh + 1, first:])).astype(BF16)
                dvs.append(dot(prob.astype(BF16), da[first:], 1, 0))
                dks.append(dot(ds, q2[first:], 1, 0))
                dqs.append(dot(ds, km, 0, 0))
            dk = jnp.where(lane < HEAD, dks[0], dks[1]).astype(BF16)
            dv = jnp.where(lane < HEAD, dvs[0], dvs[1]).astype(BF16)
            results.append((dk, dv, dqs[0] + dqs[1]))
        (dk0, dv0, dq0), (dk1, dv1, dq1) = results
        scale = HEAD**-0.5
        dq_low = (dq0[:KB] * scale).astype(BF16)
        dq_high = ((dq0[KB:] + dq1) * scale).astype(BF16)
        r.qkvb[p, 0:KB, 0:128] = dq_low
        r.qkvb[p, KB:T, 0:128] = dq_high
        r.qkvb[p, 0:KB, 128:256] = dk0
        r.qkvb[p, KB:T, 128:256] = dk1
        r.qkvb[p, 0:KB, 256:384] = dv0
        r.qkvb[p, KB:T, 256:384] = dv1
        at = pl.ds(pl.multiple_of(128 * p, 128), 128)
        r.gsm[2:3, at] = jnp.sum(dq_low.astype(F32), axis=0, keepdims=True) + jnp.sum(
            dq_high.astype(F32), axis=0, keepdims=True
        )
        r.gsm[3:4, at] = jnp.sum(dv0.astype(F32), axis=0, keepdims=True) + jnp.sum(
            dv1.astype(F32), axis=0, keepdims=True
        )

    def qkv_grad(i):
        res = dot(r.h1c[0], r.qkvb[3 * c + i], 0, 0) + dot(r.h1c[1], r.dqp[i], 0, 0)
        r.G[i] = res.astype(BF16).reshape(ZS, 2, 2, 48, HALF)

    def qkv_back():
        def one(i):
            lhs = jnp.concatenate([r.qkvb[i], r.qkvb[3 + i]], axis=1)
            return dot(lhs, wide(i), 1, 1)

        r.acc[...] = one(0)

        def item(i, carry):
            r.acc[...] += one(i)
            return carry

        lax.fori_loop(1, 3, item, 0)

    def norm_one_back():
        def body(i, sums):
            row = pl.multiple_of(i * NORM, NORM)
            here = pl.ds(row, NORM)
            xhat, inverse = stats(tile_x(r.xb, row, NORM))
            d_h1 = r.acc[here, :]
            d_x = r.x1[here, :] + norm_back(xhat, inverse, d_h1 * vrow(0))
            r.ob[here, :] = d_x.astype(BF16)
            return (sums[0] + fold8(d_h1 * xhat), sums[1] + fold8(d_h1))

        sums = lax.fori_loop(0, T // NORM, body, zero_sums(2))
        for k, at in enumerate((0, 1)):
            r.gsm[at : at + 1, :] = jnp.sum(sums[k], axis=0, keepdims=True)

    def gview(u, zs, ys, xs):
        kind, first, count = u
        if kind in "pl":
            return r.Gp.at[zs, ys, xs, pl.ds(first, count), :]
        return r.G.at[pl.ds(first, count), zs, ys, xs]

    def rview(u, plain, proj):
        kind, first, count = u
        if kind == "p":
            at = (pl.ds(0, proj.shape[0]),) + (pl.ds(0, 2),) * (len(proj.shape) - 3) + (pl.ds(first, count), slice(None))
            return proj.at[at]
        return plain.at[pl.ds(first, count)]

    def add_into(dst, extra):
        dst[...] = (dst[...].astype(F32) + extra[...].astype(F32)).astype(BF16)

    def rs1(u):
        send((u, "r1a"), gview(u, low_z(u), ny, both), rview(u, r.rA1, r.pA1), ypeer)
        send((u, "r1b"), gview(u, high_z(u), both, nx), rview(u, r.rB1, r.pB1), xpeer)

    def rs2a(u):
        va = rview(u, r.rA1, r.pA1)
        arrive((u, "r1a"), va)
        add_into(gview(u, low_z(u), y, both), va)
        send((u, "r2a"), gview(u, low_z(u), y, nx), rview(u, r.rA2, r.pA2), xpeer)

    def rs2b(u):
        vb = rview(u, r.rB1, r.pB1)
        arrive((u, "r1b"), vb)
        add_into(gview(u, high_z(u), both, x), vb)
        send((u, "r2b"), gview(u, high_z(u), ny, x), rview(u, r.rB2, r.pB2), ypeer)

    def zslot(u, k):
        kind, first, count = u
        if kind == "p":
            return r.pz.at[k - 1, pl.ds(first, count), :]
        return r.rz.at[pl.ds(first, count), k - 1]

    def rs3(u):
        va, vb = rview(u, r.rA2, r.pA2), rview(u, r.rB2, r.pB2)
        arrive((u, "r2a"), va)
        add_into(gview(u, low_z(u), y, x), va)
        arrive((u, "r2b"), vb)
        add_into(gview(u, high_z(u), y, x), vb)
        for k in (1, 2, 3):
            send((u, "rz", k), gview(u, zshift(k), y, x), zslot(u, k), zpeer(k))

    def rs4(u):
        kind, first, count = u
        for k in (1, 2, 3):
            arrive((u, "rz", k), zslot(u, k))
        total = gview(u, z, y, x)[...].astype(F32)
        for k in (1, 2, 3):
            total = total + zslot(u, k)[...].astype(F32)
        if kind == "p":
            r.ptot[pl.ds(first, count), :] = total
        else:
            r.tot[pl.ds(first, count)] = total
            give = pl.ds(pl.multiple_of(24 * nc, 8), 24)
            send((u, "fin"), r.tot.at[pl.ds(first, count), give, :], r.fr.at[pl.ds(first, count)], partner)

    def rs5(u):
        kind, first, count = u
        arrive((u, "fin"), r.fr.at[pl.ds(first, count)])
        keep = pl.ds(pl.multiple_of(24 * c, 8), 24)
        for it in range(first, first + count):
            for core, part in ((c, r.tot[it, keep, :]), (nc, r.fr[it])):
                if it < 3:
                    for j in range(3):
                        at = pl.multiple_of(j * D + 128 * (3 * core + it), 128)
                        r.gq_o[:, pl.ds(at, 128)] = part[:, 128 * j : 128 * j + 128]
                elif it == 3:
                    r.go_o[:, pl.ds(pl.multiple_of(core * HALF, 128), HALF)] = part
                else:
                    at = pl.multiple_of(core * (FF // 2) + (it - 4) * HALF, 128)
                    r.gf_o[:, pl.ds(at, HALF)] = part

    def back1(u):
        for k in (1, 2, 3):
            send((u, "b1", k), gview(u, zshift(k), both, both), r.zL.at[k - 1], zpeer(k))

    def back2(u):
        for k in (1, 2, 3):
            arrive((u, "b1", k), r.zL.at[k - 1])
        for yy in (0, 1):
            for xx in (0, 1):
                here = gview(u, z, yy, xx)
                total = here[...].astype(F32)
                for k in (1, 2, 3):
                    total = total + r.zL[k - 1, yy, xx].astype(F32)
                here[...] = total.astype(BF16)
        send((u, "b2"), gview(u, z, ny, both), r.yL, ypeer)

    def back3(u):
        arrive((u, "b2"), r.yL)
        add_into(gview(u, z, y, both), r.yL)
        send((u, "b3"), gview(u, z, y, nx), r.xL, xpeer)

    def back4(u):
        kind, first, count = u
        arrive((u, "b3"), r.xL)
        r.ptot[pl.ds(first, count), :] = gview(u, z, y, x)[...].astype(F32) + r.xL[...].astype(F32)

    def rs_proj_send():
        give = pl.ds(pl.multiple_of(96 * nc, 32), 96)
        send("pfin", r.ptot.at[give, :], r.pfr, partner)

    def rs_proj_done():
        arrive("pfin", r.pfr)
        keep = pl.ds(pl.multiple_of(96 * c, 32), 96)
        r.gp_o[:, pl.ds(pl.multiple_of(c * HALF, 128), HALF)] = r.ptot[keep, :]
        r.gp_o[:, pl.ds(pl.multiple_of(nc * HALF, 128), HALF)] = r.pfr[...]

    def small_send(key, src, at, peer):
        send(("small", key), src, r.gr.at[at], peer)

    def small_add(keys, first, into):
        total = r.gsm[...] if into is None else r.gs[into]
        for n, key in enumerate(keys):
            arrive(("small", key), r.gr.at[first + n])
            total = total + r.gr[first + n]
        return total

    tasks = {}

    def pairs(body, i):
        def one(h, carry):
            body(3 * h + i)
            return carry

        lax.fori_loop(0, 2, one, 0)

    def comm(name, u):
        tasks["2" + name] = lambda: ag2(u)
        tasks["3a" + name] = lambda: ag3a(u)
        tasks["3b" + name] = lambda: ag3b(u)
        tasks["4a" + name] = lambda: ag4a(u)
        tasks["4b" + name] = lambda: ag4b(u)
        if name != "s":
            tasks["r1" + name] = lambda: rs1(u)
            tasks["r2a" + name] = lambda: rs2a(u)
            tasks["r2b" + name] = lambda: rs2b(u)
            tasks["r3" + name] = lambda: rs3(u)
            tasks["r4" + name] = lambda: rs4(u)
            if name != "p":
                tasks["r5" + name] = lambda: rs5(u)

    for name, u in (
        ("s", US), ("q0", UQ[0]), ("q1", UQ[1]), ("q2", UQ[2]), ("o", UO), ("f0", UF[0]), ("f1", UF[1]), ("p", UP)
    ):
        comm(name, u)
    tasks["l2"] = lambda: late2(UL)
    tasks["l3"] = lambda: late3(UL)
    tasks["l41"] = lambda: late4(UL, 1)
    tasks["l42"] = lambda: late4(UL, 2)
    tasks["l43"] = lambda: late4(UL, 3)
    tasks["b1"] = lambda: back1(UL)
    tasks["b2"] = lambda: back2(UL)
    tasks["b3"] = lambda: back3(UL)
    tasks["b4"] = lambda: back4(UL)

    def task(body):
        tasks[body.__name__] = body

    @task
    def mask():
        build_mask()

    @task
    def first_norm():
        ag5(US)
        for k in (1, 2, 3):
            arrive(("tok", k), r.xb.at[lax.rem(sp + 4 - k, 4)])
        own_tok.wait()
        small_vectors()
        norm_one()
        send("h1", r.h1c.at[0], r.h1c.at[1], partner)

    def qkv(i):
        def run():
            ag5(UQ[i])
            qkv_item(i)

        return run

    def attend(i):
        return lambda: pairs(attend_pair, i)

    def attend_back(i):
        def run():
            pairs(attend_back_pair, i)
            send(("dq", i), r.qkvb.at[3 * nc + i], r.dqp.at[i], partner)

        return run

    def grad_qkv(i):
        def run():
            if i == 0:
                arrive("h1", r.h1c.at[1])
            arrive(("dq", i), r.dqp.at[i])
            qkv_grad(i)

        return run

    for i in range(3):
        tasks["qkv" + str(i)] = qkv(i)
        tasks["attend" + str(i)] = attend(i)
        tasks["attend_back" + str(i)] = attend_back(i)
        tasks["qkv_grad" + str(i)] = grad_qkv(i)

    tasks["tok2"] = lambda: send_pack("tok", r.tok, r.xb, (2,))
    tasks["tok1"] = lambda: send_pack("tok", r.tok, r.xb, (1, 3))
    tasks["dx2"] = lambda: send_rows("dx", r.dx_o, (2,))
    tasks["dx1"] = lambda: send_rows("dx", r.dx_o, (1, 3))
    tasks["cot2"] = lambda: send_pack("cot", r.cot, r.cb, (2,))
    tasks["cot1"] = lambda: send_pack("cot", r.cot, r.cb, (1, 3))

    tasks["l1"] = lambda: late1(UL)

    @task
    def out():
        send("attn", r.attnc.at[0], r.attnc.at[1], partner)
        ag5(UO)
        out_proj()
        send("h2", r.h2c.at[0], r.h2c.at[1], partner)

    @task
    def flip():
        flip_lse()
        build_mask_t()

    @task
    def rows():
        for k in (1, 2, 3):
            arrive(("cot", k), r.cb.at[lax.rem(sp + 4 - k, 4)])
        own_cot.wait()
        mlp_grad_rows()
        send("dml", half_cols(r.dml, nc), r.dml_p, partner)

    def act_cols(core, j, h):
        return r.actc.at[core, :, pl.ds(h * (FF // 2) + j * D, D)]

    def up(j):
        def run():
            ag5(UF[j])

            def one(i, carry):
                up_item(i)
                return carry

            lax.fori_loop(2 * j, 2 * j + 2, one, 0)
            for h in (0, 1):
                send(("act", j, h), act_cols(0, j, h), act_cols(1, j, h), partner)

        return run

    def proj(j):
        def run():
            if j == 0:
                arrive("dml", r.dml_p)
            for h in (0, 1):
                arrive(("act", j, h), act_cols(1, j, h))
            proj_grad(j)

        return run

    def up_weight(j):
        def run():
            if j == 0:
                arrive("h2", r.h2c.at[1])
                arrive("dpre", r.dpre_p)
            up_grad(j)

        return run

    for j in range(2):
        tasks["up" + str(j)] = up(j)
        tasks["proj" + str(j)] = proj(j)
        tasks["up_grad" + str(j)] = up_weight(j)

    @task
    def whole():
        ag5(UP)
        late5(UL)

    own = {}

    @task
    def final():
        layer_out()
        send_rows("out", r.out_o, (2, 1, 3))
        own["out"] = keep_rows(r.out_o, 2)

    @task
    def down():
        down_back()
        send("dpre", r.slope.at[:, pl.ds(pl.multiple_of(nc * (FF // 2), 128), FF // 2)], r.dpre_p, partner)

    @task
    def up_input():
        up_back()

    @task
    def second_norm():
        norm_two_back()
        send("dbr", half_cols(r.dbr, nc), r.dbr_p, partner)

    @task
    def out_input():
        out_back()

    @task
    def out_weight():
        arrive("attn", r.attnc.at[1])
        arrive("dbr", r.dbr_p)
        out_grad()

    @task
    def qkv_input():
        qkv_back()

    @task
    def last_norm():
        own["out"].wait()
        for k in (1, 2, 3):
            started.pop(("out", k)).wait_send()
        norm_one_back()
        r.gsm[12:16, :] = jnp.zeros((4, D), F32)
        small_send("x", r.gsm, 0, xpeer)
        own["dx"] = keep_rows(r.dx_o, 3)

    @task
    def small1():
        r.gs[0] = small_add(["x"], 0, None)
        small_send("core", r.gs.at[0], 1, partner)

    @task
    def small2():
        r.gs[1] = small_add(["core"], 1, 0)
        small_send("y", r.gs.at[1], 2, ypeer)

    @task
    def small3():
        r.gs[2] = small_add(["y"], 2, 1)
        for k in (1, 2, 3):
            small_send(("z", k), r.gs.at[2], 2 + k, zpeer(k))

    @task
    def small4():
        r.gs[3] = small_add([("z", 1), ("z", 2), ("z", 3)], 3, 2)
        pick_small()

    @task
    def proj_send():
        rs_proj_send()

    @task
    def proj_done():
        rs_proj_done()

    t = Bag()
    for name, body in tasks.items():
        setattr(t, "g" + name, body)
    t.gtok2()
    t.gl1()
    t.gmask()
    t.g2s()
    t.gl2()
    t.g3bs()
    t.g3as()
    t.g2q0()
    t.gtok1()
    t.g4bs()
    t.g4as()
    t.g2q1()
    t.g3bq0()
    t.g3aq0()
    t.g3bq1()
    t.g2q2()
    t.gfirst_norm()
    t.g3aq1()
    t.g4aq0()
    t.g2o()
    t.g4bq0()
    t.g3bq2()
    t.g4bq1()
    t.gqkv0()
    t.g3aq2()
    t.gattend0()
    t.g4aq1()
    t.g3ao()
    t.g3bo()
    t.g2f0()
    t.gl3()
    t.gcot2()
    t.gcot1()
    t.g4bq2()
    t.gqkv1()
    t.gattend1()
    t.g4aq2()
    t.g4bo()
    t.g2f1()
    t.gqkv2()
    t.g3af0()
    t.g4ao()
    t.gattend2()
    t.g3bf0()
    t.g3bf1()
    t.gout()
    t.gflip()
    t.grows()
    t.g3af1()
    t.g2p()
    t.g4af0()
    t.g4bf0()
    t.gup0()
    t.g4bf1()
    t.gl41()
    t.g3ap()
    t.g4af1()
    t.gproj0()
    t.g3bp()
    t.gl42()
    t.gup1()
    t.gl43()
    t.g4bp()
    t.g4ap()
    t.gproj1()
    t.gb1()
    t.gr1p()
    t.gwhole()
    t.gdown()
    t.gfinal()
    t.gr2bp()
    t.gup_input()
    t.gr2ap()
    t.gup_grad0()
    t.gr1f0()
    t.gup_grad1()
    t.gr1f1()
    t.gsecond_norm()
    t.gout_input()
    t.gattend_back0()
    t.gr3p()
    t.gr2af0()
    t.gout_weight()
    t.gr2bf0()
    t.gr1o()
    t.gattend_back1()
    t.gr2bf1()
    t.gqkv_grad0()
    t.gr1q0()
    t.gattend_back2()
    t.gr2af1()
    t.gr2bo()
    t.gr3f0()
    t.gqkv_grad1()
    t.gr1q1()
    t.gr2bq0()
    t.gqkv_input()
    t.gb2()
    t.gqkv_grad2()
    t.gr1q2()
    t.gr2ao()
    t.glast_norm()
    t.gr3f1()
    t.gr2bq1()
    t.gr2bq2()
    t.gr2aq0()
    t.gr4p()
    t.gr3o()
    t.gsmall1()
    t.gsmall2()
    t.gr2aq1()
    t.gr3q0()
    t.gr4f0()
    t.gb3()
    t.gr5f0()
    t.gb4()
    t.gproj_send()
    t.gr2aq2()
    t.gdx2()
    t.gdx1()
    t.gr3q1()
    t.gproj_done()
    t.gr4f1()
    t.gsmall3()
    t.gr5f1()
    t.gr4o()
    t.gr3q2()
    t.gr5o()
    t.gr4q0()
    t.gr5q0()
    t.gr4q1()
    t.gr5q1()
    t.gsmall4()
    t.gr4q2()
    t.gr5q2()
    for name, dst in (("out", r.out_o), ("dx", r.dx_o)):
        for k in (1, 2, 3):
            arrive((name, k), dst.at[lax.rem(sp + 4 - k, 4)])
    own["dx"].wait()
    for copy in started.values():
        copy.wait_send()
    assert len(table) <= SEMS, len(table)


def finish(out, d_x, gq, go, gf, gp, out_o, dx_o, gq_o, go_o, gf_o, gp_o):
    for src, dst in ((out, out_o), (gq, gq_o), (go, go_o), (gf, gf_o), (gp, gp_o)):
        dst[...] = src[...]
    dx_o[...] = d_x[...].astype(F32)


def fused(tokens, cotangent, seq_cut, g1, o1, w_qkv, bq, bv, w_out, bo, g2, o2, w_fc, bf, w_proj, bp):
    flat = jnp.concatenate([v[None] for v in (g1, o1, bq, bv, bo, g2, o2, bp, bf)] + [jnp.zeros((1, 96), BF16)], axis=1)
    vmem = pl.BlockSpec(memory_space=pltpu.VMEM)
    anywhere = pl.BlockSpec(memory_space=pl.ANY)
    s = jax.ShapeDtypeStruct
    out, d_x, gq, go, gf, gp, gs = pl.pallas_call(
        mega,
        out_shape=(
            s((4, 128, D), BF16),
            s((4, 128, D), BF16),
            s((24, 3 * D), F32),
            s((24, D), F32),
            s((24, FF), F32),
            s((96, D), F32),
            s((16, 128), F32),
        ),
        in_specs=[anywhere, anywhere] + [vmem] * 6,
        out_specs=(anywhere, anywhere) + (vmem,) * 5,
        scratch_shapes=scratch_shapes(),
        compiler_params=pltpu.CompilerParams(collective_id=0, has_side_effects=True, vmem_limit_bytes=67043328),
    )(tokens, cotangent, seq_cut, w_qkv, w_out, w_fc, w_proj, flat)
    out, d_x, gq, go, gf, gp = pl.pallas_call(
        finish,
        out_shape=(
            s((4, 128, D), BF16),
            s((4, 128, D), F32),
            s((24, 3 * D), F32),
            s((24, D), F32),
            s((24, FF), F32),
            s((96, D), F32),
        ),
        in_specs=[vmem] * 6,
        out_specs=(vmem,) * 6,
    )(out, d_x, gq, go, gf, gp)
    rows, g_bf = gs[:8, :24], gs[8, 32:]
    return (out, d_x, rows[0], rows[1], gq, rows[2], rows[3], go, rows[4], rows[5], rows[6], gf, g_bf, gp, rows[7])


def solution(mesh):
    row = P(AXES, None)
    vec = P(AXES)
    act = P(None, AXES, None)
    body = fused if dict(mesh.shape) == {"dp": 8, "sp": 4} else local
    return jax.shard_map(
        body,
        mesh=mesh,
        in_specs=(act, act, P(None, "dp"), vec, vec, row, vec, vec, row, vec, vec, vec, row, vec, row, vec),
        out_specs=(act, act, vec, vec, row, vec, vec, row, vec, vec, vec, row, vec, row, vec),
        check_vma=False,
    )
```

```python
import functools

import jax
import jax.numpy as jnp
from jax import lax
from jax.experimental import pallas as pl
from jax.experimental.pallas import tpu as pltpu
from jax.sharding import PartitionSpec as P

HEADS = 12
HEAD = 64
EPSILON = 1e-05
BRANCH = 24.0 ** (-0.5)
NEGATIVE = -1e30
GELU_A = 0.7978845608028654
GELU_B = 0.044715
AXES = ("dp", "sp")
F32 = jnp.float32
BF16 = jnp.bfloat16
MESH = pl.DeviceIdType.MESH

def dot(a, b, dims):
    return lax.dot_general(a, b, (dims, ((), ())), preferred_element_type=F32)


def mm(a, b):
    return dot(a, b, ((1,), (0,)))


def mm_nt(a, b):
    return dot(a, b, ((1,), (1,)))


def mm_tn(a, b):
    return dot(a, b, ((0,), (0,)))


def norm_stats(rows):
    center = jnp.mean(rows, axis=-1, keepdims=True)
    centred = rows - center
    inverse = lax.rsqrt(jnp.mean(centred * centred, axis=-1, keepdims=True) + EPSILON)
    return centred * inverse, inverse


def norm_back(xhat, inverse, grad):
    mean_grad = jnp.mean(grad, axis=-1, keepdims=True)
    mean_proj = jnp.mean(grad * xhat, axis=-1, keepdims=True)
    return inverse * (grad - mean_grad - xhat * mean_proj)


def split_heads(rows):
    return rows.reshape(rows.shape[0], HEADS, HEAD).transpose(1, 0, 2)


def join_heads(heads):
    return heads.transpose(1, 0, 2).reshape(heads.shape[1], HEADS * HEAD)


def layer(x16, dy16, cut, big, small):
    w_qkv, w_out, w_fc, w_proj = big
    g1, o1, bq, bv, bo, g2, o2, bf, bp = [v.astype(F32)[None] for v in small]
    length = x16.shape[0]
    x = x16.astype(F32)
    xhat1, inv1 = norm_stats(x)
    h1 = (xhat1 * g1 + o1).astype(BF16)
    bias = jnp.concatenate([bq, jnp.zeros_like(bq), bv], axis=1)
    qkv = (mm(h1, w_qkv) + bias).astype(BF16)
    width = HEADS * HEAD
    q, k, v = (split_heads(qkv[:, i * width : (i + 1) * width]) for i in range(3))
    pos = lax.iota(jnp.int32, length)
    allowed = (pos[None, :] <= pos[:, None]) & ((pos[None, :] >= cut) == (pos[:, None] >= cut))
    scale = HEAD ** (-0.5)
    scores = jnp.einsum("hqd,hkd->hqk", q, k, preferred_element_type=F32) * scale
    scores = jnp.where(allowed[None], scores, NEGATIVE)
    top = jnp.max(scores, axis=-1, keepdims=True)
    expo = jnp.exp(scores - top)
    prob32 = expo / jnp.sum(expo, axis=-1, keepdims=True)
    prob = prob32.astype(BF16)
    attn32 = jnp.einsum("hqk,hkd->hqd", prob, v, preferred_element_type=F32)
    attn = join_heads(attn32).astype(BF16)
    x1 = x + BRANCH * (mm(attn, w_out) + bo)
    xhat2, inv2 = norm_stats(x1)
    h2 = (xhat2 * g2 + o2).astype(BF16)
    pre = mm(h2, w_fc) + bf
    t = jnp.tanh(GELU_A * (pre + GELU_B * pre * pre * pre))
    act = (0.5 * pre * (1 + t)).astype(BF16)
    slope = 0.5 * (1 + t) + 0.5 * pre * (1 - t * t) * (GELU_A * (1 + 3 * GELU_B * pre * pre))
    out = (x1 + BRANCH * (mm(act, w_proj) + bp)).astype(BF16)

    dy = dy16.astype(F32)
    d_mlp = (dy * BRANCH).astype(BF16)
    g_w_proj = mm_tn(act, d_mlp)
    g_b_proj = jnp.sum(d_mlp.astype(F32), axis=0)
    d_pre = (mm_nt(d_mlp, w_proj) * slope).astype(BF16)
    g_w_fc = mm_tn(h2, d_pre)
    g_b_fc = jnp.sum(d_pre.astype(F32), axis=0)
    d_h2 = mm_nt(d_pre, w_fc)
    g_g2 = jnp.sum(d_h2 * xhat2, axis=0)
    g_o2 = jnp.sum(d_h2, axis=0)
    d_x1 = dy + norm_back(xhat2, inv2, d_h2 * g2)
    d_branch = (d_x1 * BRANCH).astype(BF16)
    g_w_out = mm_tn(attn, d_branch)
    g_b_out = jnp.sum(d_branch.astype(F32), axis=0)
    d_attn = split_heads(mm_nt(d_branch, w_out).astype(BF16))
    delta = jnp.sum(d_attn.astype(F32) * attn32, axis=-1, keepdims=True)
    d_prob = jnp.einsum("hqd,hkd->hqk", d_attn, v, preferred_element_type=F32)
    d_scores = (prob32 * (d_prob - delta)).astype(BF16)
    d_q = jnp.einsum("hqk,hkd->hqd", d_scores, k, preferred_element_type=F32) * scale
    d_k = jnp.einsum("hqk,hqd->hkd", d_scores, q, preferred_element_type=F32) * scale
    d_v = jnp.einsum("hqk,hqd->hkd", prob, d_attn, preferred_element_type=F32)
    d_qkv = jnp.concatenate([join_heads(d_q), join_heads(d_k), join_heads(d_v)], axis=1).astype(BF16)
    g_w_qkv = mm_tn(h1, d_qkv)
    g_b_qkv = jnp.sum(d_qkv.astype(F32), axis=0)
    d_h1 = mm_nt(d_qkv, w_qkv)
    g_g1 = jnp.sum(d_h1 * xhat1, axis=0)
    g_o1 = jnp.sum(d_h1, axis=0)
    d_x = d_x1 + norm_back(xhat1, inv1, d_h1 * g1)
    big_grads = (g_w_qkv, g_w_out, g_w_fc, g_w_proj)
    small_grads = (g_g1, g_o1, g_b_qkv[:width], g_b_qkv[2 * width :], g_b_out, g_g2, g_o2, g_b_fc, g_b_proj)
    return out, d_x, big_grads, small_grads


def local(tokens, cotangent, seq_cut, g1, o1, w_qkv, bq, bv, w_out, bo, g2, o2, w_fc, bf, w_proj, bp):
    ways = lax.axis_size("sp")
    devices = ways * lax.axis_size("dp")
    small = (g1, o1, bq, bv, bo, g2, o2, bf, bp)
    sizes = [v.shape[0] for v in small]
    big = [lax.all_gather(w, AXES, axis=0, tiled=True) for w in (w_qkv, w_out, w_fc, w_proj)]
    packed = lax.all_gather(jnp.concatenate(small), AXES, axis=0)
    cuts = [sum(sizes[:i]) for i in range(len(sizes) + 1)]
    vectors = [packed[:, a:b].reshape(-1) for a, b in zip(cuts[:-1], cuts[1:])]
    x16 = lax.all_to_all(tokens, "sp", split_axis=0, concat_axis=1, tiled=True)
    dy16 = lax.all_to_all(cotangent, "sp", split_axis=0, concat_axis=1, tiled=True)
    packs = x16.shape[0]
    first = lax.axis_index("sp") * packs
    outs, grads_in, big_sum, small_sum = [], [], None, None
    for i in range(packs):
        cut = lax.dynamic_slice(seq_cut, (first + i, 0), (1, 1))[0, 0]
        out, d_x, bigs, smalls = layer(x16[i], dy16[i], cut, big, vectors)
        outs.append(out)
        grads_in.append(d_x)
        big_sum = bigs if big_sum is None else [a + b for a, b in zip(big_sum, bigs)]
        small_sum = smalls if small_sum is None else [a + b for a, b in zip(small_sum, smalls)]
    out = lax.all_to_all(jnp.stack(outs), "sp", split_axis=1, concat_axis=0, tiled=True)
    d_x = lax.all_to_all(jnp.stack(grads_in), "sp", split_axis=1, concat_axis=0, tiled=True)
    big_out = [
        lax.psum_scatter(g.astype(BF16), AXES, scatter_dimension=0, tiled=True).astype(F32) for g in big_sum
    ]
    small_pack = jnp.concatenate([g.reshape(devices, -1) for g in small_sum], axis=1)
    small_out = lax.psum_scatter(small_pack, AXES, scatter_dimension=0, tiled=True)[0]
    s = [small_out[a:b] for a, b in zip(cuts[:-1], cuts[1:])]
    return (out, d_x, s[0], s[1], big_out[0], s[2], s[3], big_out[1], s[4], s[5], s[6], big_out[2], s[7], big_out[3], s[8])

T, D, FF, HALF = 512, 768, 3072, 384
ZS = 4
ZA = 3
PZ = 3
ROWS = 32
NORM = 64


class Bag:
    pass


def rows_loop(count, step, body):
    def one(i, carry):
        body(pl.multiple_of(i * step, step))
        return carry

    lax.fori_loop(0, count // step, one, 0)


def fold8(values):
    return jnp.sum(values.reshape(values.shape[0] // 8, 8, values.shape[1]), axis=0)


def zero_sums(count):
    return tuple(jnp.zeros((8, D), F32) for _ in range(count))


NAMES = (
    "tok", "cot", "cut", "wq", "wo", "wf", "wp", "flat", "out_o", "dx_o", "gq_o", "go_o", "gf_o", "gp_o", "gs_o",
    "W", "Wp", "Sw", "sq", "so", "sf", "sp_", "ssm", "vec", "G", "Gp", "rA1", "rB1", "pA1", "pB1", "rA2", "rB2",
    "pA2", "pB2", "rz", "pz", "zL", "yL", "xL", "tot", "ptot", "fr", "pfr", "xb", "cb", "h1c", "qkvb", "attnc", "x1", "h2c", "actc",
    "slope", "dpre_p", "acc", "dbr", "dbr_p", "dml", "dml_p", "dat", "dqp", "ob", "mask", "lse", "lseT", "gsm", "gs",
    "gr", "small", "ssem", "rsem", "lsem",
)
SEMS = 220


def scratch_shapes():
    v = pltpu.VMEM
    return [
        v((8, 2, ZS, 2, 2, 48, HALF), BF16),
        v((2, ZS, 2, 2, 192, HALF), BF16),
        v((2, ZS, 2, 2, 16, HALF), BF16),
        v((24, 3 * D), BF16),
        v((24, D), BF16),
        v((24, FF), BF16),
        v((96, D), BF16),
        v((16, D), BF16),
        v((16, D), F32),
        v((8, ZS, 2, 2, 48, HALF), BF16),
        v((ZS, 2, 2, 192, HALF), BF16),
        v((8, ZA, 2, 48, HALF), BF16),
        v((8, ZS - ZA, 2, 48, HALF), BF16),
        v((PZ, 2, 96, HALF), BF16),
        v((ZS - PZ, 2, 96, HALF), BF16),
        v((8, ZA, 48, HALF), BF16),
        v((8, ZS - ZA, 48, HALF), BF16),
        v((PZ, 96, HALF), BF16),
        v((ZS - PZ, 96, HALF), BF16),
        v((8, 3, 48, HALF), BF16),
        v((3, 96, HALF), BF16),
        v((3, 2, 2, 96, HALF), BF16),
        v((2, 96, HALF), BF16),
        v((96, HALF), BF16),
        v((8, 48, HALF), F32),
        v((192, HALF), F32),
        v((8, 24, HALF), F32),
        v((96, HALF), F32),
        v((4, 128, D), BF16),
        v((4, 128, D), BF16),
        v((2, T, D), BF16),
        v((6, T, HALF), BF16),
        v((2, T, D), BF16),
        v((T, D), F32),
        v((2, T, D), BF16),
        v((2, T, FF), BF16),
        v((T, FF), BF16),
        v((T, FF // 2), BF16),
        v((T, D), F32),
        v((T, D), BF16),
        v((T, HALF), BF16),
        v((T, D), BF16),
        v((T, HALF), BF16),
        v((T, D), BF16),
        v((3, T, HALF), BF16),
        v((T, D), BF16),
        v((T, T), F32),
        v((T, 128), F32),
        v((128, T), F32),
        v((16, D), F32),
        v((4, 16, D), F32),
        v((6, 16, D), F32),
        v((16, D), BF16),
        pltpu.SemaphoreType.DMA((SEMS,)),
        pltpu.SemaphoreType.DMA((SEMS,)),
        pltpu.SemaphoreType.DMA((4,)),
    ]


def mega(*refs):
    r = Bag()
    assert len(refs) == len(NAMES), (len(refs), len(NAMES))
    for name, ref in zip(NAMES, refs):
        setattr(r, name, ref)
    dp, sp = lax.axis_index("dp"), lax.axis_index("sp")
    z, y = dp // 2, lax.rem(dp, 2)
    x, c = sp // 2, lax.rem(sp, 2)
    nx, ny, nc = 1 - x, 1 - y, 1 - c
    partner = {"dp": dp, "sp": x * 2 + nc}
    xpeer = {"dp": dp, "sp": nx * 2 + c}
    ypeer = {"dp": z * 2 + ny, "sp": sp}
    every = pl.ds(0, ZS)

    def low_z(u):
        return pl.ds(0, PZ if u[0] == "p" else ZA)

    def high_z(u):
        first = PZ if u[0] == "p" else ZA
        return pl.ds(first, ZS - first)

    both = pl.ds(0, 2)

    def zshift(k):
        return lax.rem(z + k, ZS)

    def zpeer(k):
        return {"dp": zshift(k) * 2 + y, "sp": sp}

    def speer(k):
        return lax.rem(sp + k, 4)

    table = {}
    started = {}

    def slot(key):
        return table.setdefault(key, len(table))

    def send(key, src, dst, device):
        i = slot(key)
        copy = pltpu.make_async_remote_copy(
            src_ref=src, dst_ref=dst, send_sem=r.ssem.at[i], recv_sem=r.rsem.at[i], device_id=device, device_id_type=MESH
        )
        copy.start()
        started[key] = copy
        return copy

    def arrive(key, dst):
        i = slot(key)
        pltpu.make_async_remote_copy(
            src_ref=dst, dst_ref=dst, send_sem=r.ssem.at[i], recv_sem=r.rsem.at[i], device_id=partner, device_id_type=MESH
        ).wait_recv()

    barrier = pltpu.get_barrier_semaphore()
    peers = [{"dp": dp, "sp": speer(k)} for k in (1, 2, 3)] + [ypeer] + [zpeer(k) for k in (1, 2, 3)]
    for peer in peers:
        pl.semaphore_signal(barrier, inc=1, device_id=peer, device_id_type=MESH)
    pl.semaphore_wait(barrier, len(peers))

    def view(u, h, zs, ys, xs):
        kind, first, count = u
        if kind == "s":
            return r.Sw.at[h, zs, ys, xs]
        if kind in "pl":
            return r.Wp.at[h, zs, ys, xs, pl.ds(first, count), :]
        return r.W.at[pl.ds(first, count), h, zs, ys, xs]

    def ag1(u):
        for k in (1, 2, 3):
            v = view(u, c, z, y, x)
            send((u, "z", k), v, v, zpeer(k))

    def ag2(u):
        for k in (1, 2, 3):
            arrive((u, "z", k), view(u, c, zshift(ZS - k), y, x))
        v = view(u, c, low_z(u), y, x)
        send((u, "2a"), v, v, xpeer)
        v = view(u, c, high_z(u), y, x)
        send((u, "2b"), v, v, ypeer)
        v = view(u, c, every, y, x)
        send((u, "c0"), v, v, partner)

    def ag3a(u):
        arrive((u, "2a"), view(u, c, low_z(u), y, nx))
        v = view(u, c, low_z(u), y, both)
        send((u, "3a"), v, v, ypeer)
        v = view(u, c, low_z(u), y, nx)
        send((u, "c1"), v, v, partner)

    def ag3b(u):
        arrive((u, "2b"), view(u, c, high_z(u), ny, x))
        v = view(u, c, high_z(u), both, x)
        send((u, "3b"), v, v, xpeer)
        v = view(u, c, high_z(u), ny, x)
        send((u, "c2"), v, v, partner)

    def ag4a(u):
        v = view(u, c, low_z(u), ny, both)
        arrive((u, "3a"), v)
        send((u, "c3"), v, v, partner)

    def ag4b(u):
        v = view(u, c, high_z(u), both, nx)
        arrive((u, "3b"), v)
        send((u, "c4"), v, v, partner)

    def ag5(u):
        arrive((u, "c0"), view(u, nc, every, y, x))
        arrive((u, "c1"), view(u, nc, low_z(u), y, nx))
        arrive((u, "c2"), view(u, nc, high_z(u), ny, x))
        arrive((u, "c3"), view(u, nc, low_z(u), ny, both))
        arrive((u, "c4"), view(u, nc, high_z(u), both, nx))

    def late1(u):
        v = view(u, c, z, y, x)
        send((u, "lx"), v, v, xpeer)
        send((u, "ly"), v, v, ypeer)

    def late2(u):
        v = view(u, c, z, y, nx)
        arrive((u, "lx"), v)
        send((u, "ld"), v, v, ypeer)

    def late3(u):
        arrive((u, "ly"), view(u, c, z, ny, x))
        arrive((u, "ld"), view(u, c, z, ny, nx))
        v = view(u, c, z, both, both)
        for k in (1, 2, 3):
            send((u, "lz", k), v, v, zpeer(k))
        send((u, "c", 0), v, v, partner)

    def late4(u, k):
        v = view(u, c, zshift(ZS - k), both, both)
        arrive((u, "lz", k), v)
        send((u, "c", k), v, v, partner)

    def late5(u):
        for k in (0, 1, 2, 3):
            arrive((u, "c", k), view(u, nc, zshift(ZS - k), both, both))

    US = ("s", 0, 16)
    UQ = [("w", i, 1) for i in range(3)]
    UO = ("w", 3, 1)
    UF = [("w", 4, 2), ("w", 6, 2)]
    UP = ("p", 0, 96)
    UL = ("l", 96, 96)

    device = dp * 4 + sp
    low = 24 * device
    wide_row, wide_low = device // 8, 96 * lax.rem(device, 8)

    def build_small():
        i = lax.broadcasted_iota(jnp.int32, (384, 1), 0)
        part = sum((i >= 24 * m).astype(jnp.int32) for m in range(1, 8))
        target = jnp.where(i < 192, low + i - 24 * part, wide_low + i - 192)
        target = jnp.where(i < 288, target, -1)
        j = lax.broadcasted_iota(jnp.int32, (384, D), 1)
        place = jnp.where(j == target, 1.0, 0.0).astype(BF16)
        row = lax.broadcasted_iota(jnp.int32, (16, 384), 0)
        lane = lax.broadcasted_iota(jnp.int32, (16, 384), 1)
        mine = (row < 8) & (lane >= 24 * row) & (lane < 24 * row + 24)
        mine = mine | ((row == 8 + wide_row) & (lane >= 192))
        values = jnp.where(mine, jnp.broadcast_to(r.flat[...].astype(F32), (16, 384)), 0.0).astype(BF16)
        r.small[...] = lax.dot_general(values, place, (((1,), (0,)), ((), ())), preferred_element_type=F32).astype(BF16)

    def pick_small():
        j = lax.broadcasted_iota(jnp.int32, (D, 128), 0)
        lane = lax.broadcasted_iota(jnp.int32, (D, 128), 1)
        take = ((lane < 24) & (j == low + lane)) | ((lane >= 32) & (j == wide_low + lane - 32))
        picked = lax.dot_general(
            r.gs[3], jnp.where(take, 1.0, 0.0), (((1,), (0,)), ((), ())), preferred_element_type=F32,
            precision=lax.Precision.HIGHEST,
        )
        row = lax.broadcasted_iota(jnp.int32, (16, 128), 0)
        one = jnp.sum(jnp.where(row == 8 + wide_row, picked, 0.0), axis=0, keepdims=True)
        r.gs_o[...] = jnp.where(row < 8, picked, one)

    swaps = [("wq", r.wq, r.sq), ("wp", r.wp, r.sp_), ("wo", r.wo, r.so), ("wf", r.wf, r.sf)]
    for key, src, dst in swaps:
        send(key, src, dst, partner)
    build_small()
    send("small", r.small, r.ssm, partner)

    def send_pack(key, src, dst, shifts):
        for k in shifts:
            send((key, k), src.at[speer(k)], dst.at[sp], {"dp": dp, "sp": speer(k)})

    own_tok = pltpu.make_async_copy(r.tok.at[sp], r.xb.at[sp], r.lsem.at[0])
    own_tok.start()
    own_cot = pltpu.make_async_copy(r.cot.at[sp], r.cb.at[sp], r.lsem.at[1])
    own_cot.start()
    first_core = c == 0

    def pair_rows(own, other, col, width):
        a = own[:, pl.ds(pl.multiple_of(col, 128), width)].astype(F32)
        b = other[:, pl.ds(pl.multiple_of(col, 128), width)].astype(F32)
        return jnp.concatenate([jnp.where(first_core, a, b), jnp.where(first_core, b, a)], axis=0).astype(BF16)

    arrive("small", r.ssm)
    cols = pl.ds(pl.multiple_of(c * HALF, 128), HALF)
    r.Sw[c, z, y, x] = (r.small[:, cols].astype(F32) + r.ssm[:, cols].astype(F32)).astype(BF16)
    ag1(US)
    arrive("wq", r.sq)
    for i in range(3):
        for j in range(3):
            r.W[i, c, z, y, x, :, pl.ds(128 * j, 128)] = pair_rows(r.wq, r.sq, j * D + 128 * (3 * c + i), 128)
        ag1(UQ[i])
    arrive("wp", r.sp_)
    r.Wp[c, z, y, x, pl.ds(pl.multiple_of(96 * c, 32), 96), :] = r.wp[:, cols]
    r.Wp[c, z, y, x, pl.ds(pl.multiple_of(96 * nc, 32), 96), :] = r.sp_[:, cols]
    arrive("wo", r.so)
    r.W[3, c, z, y, x] = pair_rows(r.wo, r.so, c * HALF, HALF)
    ag1(UO)
    arrive("wf", r.sf)
    for i in range(4):
        r.W[4 + i, c, z, y, x] = pair_rows(r.wf, r.sf, c * (FF // 2) + i * HALF, HALF)
    ag1(UF[0])
    ag1(UF[1])
    ag1(UP)

    def dot(a, b, ca, cb):
        return lax.dot_general(a, b, (((ca,), (cb,)), ((), ())), preferred_element_type=F32)

    def wide(item):
        return jnp.concatenate([r.W[item, h].reshape(D, HALF) for h in (0, 1)], axis=1)

    def tile_x(buf, row, size):
        return buf[row // 128, pl.ds(pl.multiple_of(lax.rem(row, 128), size), size), :].astype(F32)

    def vrow(i):
        return r.vec[i : i + 1, :]

    def stats(v):
        center = jnp.mean(v, axis=-1, keepdims=True)
        centred = v - center
        inverse = lax.rsqrt(jnp.mean(centred * centred, axis=-1, keepdims=True) + EPSILON)
        return centred * inverse, inverse

    def norm_back(xhat, inverse, grad):
        return inverse * (grad - jnp.mean(grad, axis=-1, keepdims=True) - xhat * jnp.mean(grad * xhat, axis=-1, keepdims=True))

    def build_mask():
        def body(row):
            q = lax.broadcasted_iota(jnp.int32, (ROWS, T), 0) + row
            k = lax.broadcasted_iota(jnp.int32, (ROWS, T), 1)
            cut = r.cut[pl.ds(sp, 1), :]
            ok = (k <= q) & ((k >= cut) == (q >= cut))
            r.mask[pl.ds(row, ROWS), :] = jnp.where(ok, 0.0, NEGATIVE)

        rows_loop(T, ROWS, body)

    def build_mask_t():
        def body(row):
            k = lax.broadcasted_iota(jnp.int32, (ROWS, T), 0) + row
            q = lax.broadcasted_iota(jnp.int32, (ROWS, T), 1)
            cut = r.cut[pl.ds(sp, 1), :]
            ok = (k <= q) & ((k >= cut) == (q >= cut))
            r.mask[pl.ds(row, ROWS), :] = jnp.where(ok, 0.0, NEGATIVE)

        rows_loop(T, ROWS, body)

    def small_vectors():
        for h in (0, 1):
            total = jnp.zeros((16, HALF), F32)
            for zz in range(ZS):
                for yy in (0, 1):
                    for xx in (0, 1):
                        total = total + r.Sw[h, zz, yy, xx].astype(F32)
            r.vec[:, pl.ds(h * HALF, HALF)] = total

    def norm_one():
        def body(row):
            xhat, _ = stats(tile_x(r.xb, row, NORM))
            r.h1c[0, pl.ds(row, NORM), :] = (xhat * vrow(0) + vrow(1)).astype(BF16)

        rows_loop(T, NORM, body)

    def qkv_item(i):
        res = dot(r.h1c[0], wide(i), 1, 0)
        for h in (0, 1):
            p = 3 * h + i
            q = res[:, h * HALF : h * HALF + 128] + r.vec[2:3, 128 * p : 128 * p + 128]
            k = res[:, h * HALF + 128 : h * HALF + 256]
            v = res[:, h * HALF + 256 : h * HALF + 384] + r.vec[3:4, 128 * p : 128 * p + 128]
            r.qkvb[p, :, 0:128] = (q.astype(BF16).astype(F32) * (HEAD**-0.5)).astype(BF16)
            r.qkvb[p, :, 128:256] = k.astype(BF16)
            r.qkvb[p, :, 256:384] = v.astype(BF16)

    QB = 256

    def lane_masks(rows):
        lane = lax.broadcasted_iota(jnp.int32, (rows, 128), 1)
        return lane

    def attend_pair(p):
        lane = lane_masks(QB)

        def block(qb):
            keys = QB * (qb + 1)
            rows = pl.ds(QB * qb, QB)
            q2 = r.qkvb[p, rows, 0:128]
            k2 = r.qkvb[p, 0:keys, 128:256]
            v2 = r.qkvb[p, 0:keys, 256:384]
            outs = []
            for hh in (0, 1):
                mine = (lane < HEAD) if hh == 0 else (lane >= HEAD)
                qm = jnp.where(mine, q2, jnp.zeros_like(q2))
                s = dot(qm, k2, 1, 1) + r.mask[rows, 0:keys]
                top = jnp.max(s, axis=1, keepdims=True)
                e = jnp.exp(s - top)
                total = jnp.sum(e, axis=1, keepdims=True)
                outs.append(dot(e.astype(BF16), v2, 1, 0) / total)
                r.lse[rows, :] = jnp.where(lane == 2 * p + hh, top + jnp.log(total), r.lse[rows, :])
            both_heads = jnp.where(lane < HEAD, outs[0], outs[1]).astype(BF16)
            r.attnc[0, rows, pl.ds(pl.multiple_of(128 * p, 128), 128)] = both_heads

        for qb in range(T // QB):
            block(qb)

    def out_proj():
        r.acc[...] = dot(r.attnc[0], wide(3), 1, 0)

        def body(row):
            v = tile_x(r.xb, row, NORM) + BRANCH * (r.acc[pl.ds(row, NORM), :] + vrow(4))
            r.x1[pl.ds(row, NORM), :] = v
            xhat, _ = stats(v)
            r.h2c[0, pl.ds(row, NORM), :] = (xhat * vrow(5) + vrow(6)).astype(BF16)

        rows_loop(T, NORM, body)

    def up_item(i):
        r.acc[...] = dot(r.h2c[0], wide(4 + i), 1, 0)
        for h in (0, 1):
            col = pl.multiple_of(h * (FF // 2) + i * HALF, 128)
            at = h * 2 + i // 2
            bias = r.vec[pl.ds(8 + at, 1), pl.ds(pl.multiple_of(lax.rem(i, 2) * HALF, 128), HALF)]

            def body(row):
                pre = r.acc[pl.ds(row, ROWS), pl.ds(h * HALF, HALF)] + bias
                square = pre * pre
                t = jnp.tanh(pre * (GELU_A + (GELU_A * GELU_B) * square))
                half_one = 0.5 * (1.0 + t)
                r.actc[0, pl.ds(row, ROWS), pl.ds(col, HALF)] = (pre * half_one).astype(BF16)
                inner = GELU_A + (3.0 * GELU_A * GELU_B) * square
                r.slope[pl.ds(row, ROWS), pl.ds(col, HALF)] = (
                    half_one + (0.5 * pre) * (1.0 - t * t) * inner
                ).astype(BF16)

            rows_loop(T, ROWS, body)

    def wp_group(g):
        return jnp.concatenate([r.Wp[h, g].reshape(D, HALF) for h in (0, 1)], axis=1)

    def group_cols(g):
        return pl.ds(pl.multiple_of(g * D, 128), D)

    def mlp_grad_rows():
        def body(row, sums):
            d = (tile_x(r.cb, row, ROWS) * BRANCH).astype(BF16)
            r.dml[pl.ds(row, ROWS), :] = d
            return sums + fold8(d.astype(F32))

        sums = lax.fori_loop(0, T // ROWS, lambda i, s: body(pl.multiple_of(i * ROWS, ROWS), s), jnp.zeros((8, D), F32))
        r.gsm[7:8, :] = jnp.sum(sums, axis=0, keepdims=True)

    def layer_out():
        r.acc[...] = dot(r.actc[0, :, 0:D], wp_group(0), 1, 0)

        def group(g, carry):
            r.acc[...] += dot(r.actc[0, :, group_cols(g)], wp_group(g), 1, 0)
            return carry

        lax.fori_loop(1, 4, group, 0)

        def body(row):
            v = r.x1[pl.ds(row, ROWS), :] + BRANCH * (r.acc[pl.ds(row, ROWS), :] + vrow(7))
            r.ob[pl.ds(row, ROWS), :] = v.astype(BF16)

        rows_loop(T, ROWS, body)

    def send_rows(key, dst, shifts):
        for k in shifts:
            src = r.ob.at[pl.ds(pl.multiple_of(128 * speer(k), 128), 128), :]
            send((key, k), src, dst.at[sp], {"dp": dp, "sp": speer(k)})
    def keep_rows(dst, sem):
        own = pltpu.make_async_copy(r.ob.at[pl.ds(pl.multiple_of(128 * sp, 128), 128), :], dst.at[sp], r.lsem.at[sem])
        own.start()
        return own

    def down_back():
        def group(g, carry):
            r.acc[...] = dot(r.dml[...], wp_group(g), 1, 1)

            def body(i, sums):
                row = pl.multiple_of(i * ROWS, ROWS)
                here = (pl.ds(row, ROWS), group_cols(g))
                d = (r.acc[pl.ds(row, ROWS), :] * r.slope[here].astype(F32)).astype(BF16)
                r.slope[here] = d
                return sums + fold8(d.astype(F32))

            sums = lax.fori_loop(0, T // ROWS, body, jnp.zeros((8, D), F32))
            r.gsm[pl.ds(8 + g, 1), :] = jnp.sum(sums, axis=0, keepdims=True)
            return carry

        lax.fori_loop(0, 4, group, 0)

    def up_back():
        def one(i):
            lhs = jnp.concatenate(
                [r.slope[:, pl.ds(pl.multiple_of(h * (FF // 2) + i * HALF, 128), HALF)] for h in (0, 1)], axis=1
            )
            return dot(lhs, wide(4 + i), 1, 1)

        r.acc[...] = one(0)

        def item(i, carry):
            r.acc[...] += one(i)
            return carry

        lax.fori_loop(1, 4, item, 0)

    def half_cols(ref, core):
        return ref.at[:, pl.ds(pl.multiple_of(core * HALF, 128), HALF)]

    def proj_grad(first):
        def chunk(n, carry):
            f = 2 * first + lax.rem(n, 2) + 4 * (n // 2)
            at = pl.ds(pl.multiple_of(f * HALF, 128), HALF)
            res = dot(r.actc[0, :, at], half_cols(r.dml, c)[...], 0, 0) + dot(r.actc[1, :, at], r.dml_p[...], 0, 0)
            r.Gp[f // 2, lax.rem(f, 2)] = res.astype(BF16).reshape(2, 192, HALF)
            return carry

        lax.fori_loop(0, 4, chunk, 0)

    def up_grad(u):
        own = r.slope[:, pl.ds(pl.multiple_of(c * (FF // 2) + u * D, 128), D)]
        res = dot(r.h2c[0], own, 0, 0) + dot(r.h2c[1], r.dpre_p[:, u * D : u * D + D], 0, 0)
        for k in (0, 1):
            r.G[4 + 2 * u + k] = res[:, k * HALF : k * HALF + HALF].astype(BF16).reshape(ZS, 2, 2, 48, HALF)

    def norm_two_back():
        def body(i, sums):
            row = pl.multiple_of(i * NORM, NORM)
            here = pl.ds(row, NORM)
            xhat, inverse = stats(r.x1[here, :])
            d_h2 = r.acc[here, :]
            d_x1 = tile_x(r.cb, row, NORM) + norm_back(xhat, inverse, d_h2 * vrow(5))
            r.x1[here, :] = d_x1
            d_branch = (d_x1 * BRANCH).astype(BF16)
            r.dbr[here, :] = d_branch
            return (
                sums[0] + fold8(d_h2 * xhat),
                sums[1] + fold8(d_h2),
                sums[2] + fold8(d_branch.astype(F32)),
            )

        sums = lax.fori_loop(0, T // NORM, body, zero_sums(3))
        for k, at in enumerate((5, 6, 4)):
            r.gsm[at : at + 1, :] = jnp.sum(sums[k], axis=0, keepdims=True)

    def out_back():
        r.dat[...] = dot(r.dbr[...], wide(3), 1, 1).astype(BF16)

    def out_grad():
        res = dot(r.attnc[0], half_cols(r.dbr, c)[...], 0, 0) + dot(r.attnc[1], r.dbr_p[...], 0, 0)
        r.G[3] = res.astype(BF16).reshape(ZS, 2, 2, 48, HALF)

    def flip_lse():
        r.lseT[...] = jnp.transpose(r.lse[...])

    def attend_back_pair(p):
        KB = 256
        cols = pl.ds(pl.multiple_of(128 * p, 128), 128)
        lane = lane_masks(KB)
        da = r.dat[:, cols]
        prod = da.astype(F32) * r.attnc[0, :, cols].astype(F32)
        pick = jnp.where(
            (lax.broadcasted_iota(jnp.int32, (8, 128), 1) // HEAD) == lax.broadcasted_iota(jnp.int32, (8, 128), 0), 1.0, 0.0
        ).astype(F32)
        delta = lax.dot_general(
            pick, prod, (((1,), (1,)), ((), ())), preferred_element_type=F32, precision=lax.Precision.HIGHEST
        )
        q2 = r.qkvb[p, :, 0:128]
        dq_parts = [None, None]
        results = []
        for kb in (0, 1):
            first = KB * kb
            keys = pl.ds(first, KB)
            k2 = r.qkvb[p, keys, 128:256]
            v2 = r.qkvb[p, keys, 256:384]
            dks, dvs, dqs = [], [], []
            for hh in (0, 1):
                mine = (lane < HEAD) if hh == 0 else (lane >= HEAD)
                km = jnp.where(mine, k2, jnp.zeros_like(k2))
                vm = jnp.where(mine, v2, jnp.zeros_like(v2))
                logs = r.lseT[pl.ds(2 * p + hh, 1), :]
                s = dot(km, q2[first:], 1, 1) + r.mask[keys, first:]
                prob = jnp.exp(s - logs[:, first:])
                dprob = dot(vm, da[first:], 1, 1)
                ds = (prob * (dprob - delta[hh : hh + 1, first:])).astype(BF16)
                dvs.append(dot(prob.astype(BF16), da[first:], 1, 0))
                dks.append(dot(ds, q2[first:], 1, 0))
                dqs.append(dot(ds, km, 0, 0))
            dk = jnp.where(lane < HEAD, dks[0], dks[1]).astype(BF16)
            dv = jnp.where(lane < HEAD, dvs[0], dvs[1]).astype(BF16)
            results.append((dk, dv, dqs[0] + dqs[1]))
        (dk0, dv0, dq0), (dk1, dv1, dq1) = results
        scale = HEAD**-0.5
        dq_low = (dq0[:KB] * scale).astype(BF16)
        dq_high = ((dq0[KB:] + dq1) * scale).astype(BF16)
        r.qkvb[p, 0:KB, 0:128] = dq_low
        r.qkvb[p, KB:T, 0:128] = dq_high
        r.qkvb[p, 0:KB, 128:256] = dk0
        r.qkvb[p, KB:T, 128:256] = dk1
        r.qkvb[p, 0:KB, 256:384] = dv0
        r.qkvb[p, KB:T, 256:384] = dv1
        at = pl.ds(pl.multiple_of(128 * p, 128), 128)
        r.gsm[2:3, at] = jnp.sum(dq_low.astype(F32), axis=0, keepdims=True) + jnp.sum(
            dq_high.astype(F32), axis=0, keepdims=True
        )
        r.gsm[3:4, at] = jnp.sum(dv0.astype(F32), axis=0, keepdims=True) + jnp.sum(
            dv1.astype(F32), axis=0, keepdims=True
        )

    def qkv_grad(i):
        res = dot(r.h1c[0], r.qkvb[3 * c + i], 0, 0) + dot(r.h1c[1], r.dqp[i], 0, 0)
        r.G[i] = res.astype(BF16).reshape(ZS, 2, 2, 48, HALF)

    def qkv_back():
        def one(i):
            lhs = jnp.concatenate([r.qkvb[i], r.qkvb[3 + i]], axis=1)
            return dot(lhs, wide(i), 1, 1)

        r.acc[...] = one(0)

        def item(i, carry):
            r.acc[...] += one(i)
            return carry

        lax.fori_loop(1, 3, item, 0)

    def norm_one_back():
        def body(i, sums):
            row = pl.multiple_of(i * NORM, NORM)
            here = pl.ds(row, NORM)
            xhat, inverse = stats(tile_x(r.xb, row, NORM))
            d_h1 = r.acc[here, :]
            d_x = r.x1[here, :] + norm_back(xhat, inverse, d_h1 * vrow(0))
            r.ob[here, :] = d_x.astype(BF16)
            return (sums[0] + fold8(d_h1 * xhat), sums[1] + fold8(d_h1))

        sums = lax.fori_loop(0, T // NORM, body, zero_sums(2))
        for k, at in enumerate((0, 1)):
            r.gsm[at : at + 1, :] = jnp.sum(sums[k], axis=0, keepdims=True)

    def gview(u, zs, ys, xs):
        kind, first, count = u
        if kind in "pl":
            return r.Gp.at[zs, ys, xs, pl.ds(first, count), :]
        return r.G.at[pl.ds(first, count), zs, ys, xs]

    def rview(u, plain, proj):
        kind, first, count = u
        if kind == "p":
            at = (pl.ds(0, proj.shape[0]),) + (pl.ds(0, 2),) * (len(proj.shape) - 3) + (pl.ds(first, count), slice(None))
            return proj.at[at]
        return plain.at[pl.ds(first, count)]

    def add_into(dst, extra):
        dst[...] = (dst[...].astype(F32) + extra[...].astype(F32)).astype(BF16)

    def rs1(u):
        send((u, "r1a"), gview(u, low_z(u), ny, both), rview(u, r.rA1, r.pA1), ypeer)
        send((u, "r1b"), gview(u, high_z(u), both, nx), rview(u, r.rB1, r.pB1), xpeer)

    def rs2a(u):
        va = rview(u, r.rA1, r.pA1)
        arrive((u, "r1a"), va)
        add_into(gview(u, low_z(u), y, both), va)
        send((u, "r2a"), gview(u, low_z(u), y, nx), rview(u, r.rA2, r.pA2), xpeer)

    def rs2b(u):
        vb = rview(u, r.rB1, r.pB1)
        arrive((u, "r1b"), vb)
        add_into(gview(u, high_z(u), both, x), vb)
        send((u, "r2b"), gview(u, high_z(u), ny, x), rview(u, r.rB2, r.pB2), ypeer)

    def zslot(u, k):
        kind, first, count = u
        if kind == "p":
            return r.pz.at[k - 1, pl.ds(first, count), :]
        return r.rz.at[pl.ds(first, count), k - 1]

    def rs3(u):
        va, vb = rview(u, r.rA2, r.pA2), rview(u, r.rB2, r.pB2)
        arrive((u, "r2a"), va)
        add_into(gview(u, low_z(u), y, x), va)
        arrive((u, "r2b"), vb)
        add_into(gview(u, high_z(u), y, x), vb)
        for k in (1, 2, 3):
            send((u, "rz", k), gview(u, zshift(k), y, x), zslot(u, k), zpeer(k))

    def rs4(u):
        kind, first, count = u
        for k in (1, 2, 3):
            arrive((u, "rz", k), zslot(u, k))
        total = gview(u, z, y, x)[...].astype(F32)
        for k in (1, 2, 3):
            total = total + zslot(u, k)[...].astype(F32)
        if kind == "p":
            r.ptot[pl.ds(first, count), :] = total
        else:
            r.tot[pl.ds(first, count)] = total
            give = pl.ds(pl.multiple_of(24 * nc, 8), 24)
            send((u, "fin"), r.tot.at[pl.ds(first, count), give, :], r.fr.at[pl.ds(first, count)], partner)

    def rs5(u):
        kind, first, count = u
        arrive((u, "fin"), r.fr.at[pl.ds(first, count)])
        keep = pl.ds(pl.multiple_of(24 * c, 8), 24)
        for it in range(first, first + count):
            for core, part in ((c, r.tot[it, keep, :]), (nc, r.fr[it])):
                if it < 3:
                    for j in range(3):
                        at = pl.multiple_of(j * D + 128 * (3 * core + it), 128)
                        r.gq_o[:, pl.ds(at, 128)] = part[:, 128 * j : 128 * j + 128]
                elif it == 3:
                    r.go_o[:, pl.ds(pl.multiple_of(core * HALF, 128), HALF)] = part
                else:
                    at = pl.multiple_of(core * (FF // 2) + (it - 4) * HALF, 128)
                    r.gf_o[:, pl.ds(at, HALF)] = part

    def back1(u):
        for k in (1, 2, 3):
            send((u, "b1", k), gview(u, zshift(k), both, both), r.zL.at[k - 1], zpeer(k))

    def back2(u):
        for k in (1, 2, 3):
            arrive((u, "b1", k), r.zL.at[k - 1])
        for yy in (0, 1):
            for xx in (0, 1):
                here = gview(u, z, yy, xx)
                total = here[...].astype(F32)
                for k in (1, 2, 3):
                    total = total + r.zL[k - 1, yy, xx].astype(F32)
                here[...] = total.astype(BF16)
        send((u, "b2"), gview(u, z, ny, both), r.yL, ypeer)

    def back3(u):
        arrive((u, "b2"), r.yL)
        add_into(gview(u, z, y, both), r.yL)
        send((u, "b3"), gview(u, z, y, nx), r.xL, xpeer)

    def back4(u):
        kind, first, count = u
        arrive((u, "b3"), r.xL)
        r.ptot[pl.ds(first, count), :] = gview(u, z, y, x)[...].astype(F32) + r.xL[...].astype(F32)

    def rs_proj_send():
        give = pl.ds(pl.multiple_of(96 * nc, 32), 96)
        send("pfin", r.ptot.at[give, :], r.pfr, partner)

    def rs_proj_done():
        arrive("pfin", r.pfr)
        keep = pl.ds(pl.multiple_of(96 * c, 32), 96)
        r.gp_o[:, pl.ds(pl.multiple_of(c * HALF, 128), HALF)] = r.ptot[keep, :]
        r.gp_o[:, pl.ds(pl.multiple_of(nc * HALF, 128), HALF)] = r.pfr[...]

    def small_send(key, src, at, peer):
        send(("small", key), src, r.gr.at[at], peer)

    def small_add(keys, first, into):
        total = r.gsm[...] if into is None else r.gs[into]
        for n, key in enumerate(keys):
            arrive(("small", key), r.gr.at[first + n])
            total = total + r.gr[first + n]
        return total

    tasks = {}

    def pairs(body, i):
        def one(h, carry):
            body(3 * h + i)
            return carry

        lax.fori_loop(0, 2, one, 0)

    def comm(name, u):
        tasks["2" + name] = lambda: ag2(u)
        tasks["3a" + name] = lambda: ag3a(u)
        tasks["3b" + name] = lambda: ag3b(u)
        tasks["4a" + name] = lambda: ag4a(u)
        tasks["4b" + name] = lambda: ag4b(u)
        if name != "s":
            tasks["r1" + name] = lambda: rs1(u)
            tasks["r2a" + name] = lambda: rs2a(u)
            tasks["r2b" + name] = lambda: rs2b(u)
            tasks["r3" + name] = lambda: rs3(u)
            tasks["r4" + name] = lambda: rs4(u)
            if name != "p":
                tasks["r5" + name] = lambda: rs5(u)

    for name, u in (
        ("s", US), ("q0", UQ[0]), ("q1", UQ[1]), ("q2", UQ[2]), ("o", UO), ("f0", UF[0]), ("f1", UF[1]), ("p", UP)
    ):
        comm(name, u)
    tasks["l2"] = lambda: late2(UL)
    tasks["l3"] = lambda: late3(UL)
    tasks["l41"] = lambda: late4(UL, 1)
    tasks["l42"] = lambda: late4(UL, 2)
    tasks["l43"] = lambda: late4(UL, 3)
    tasks["b1"] = lambda: back1(UL)
    tasks["b2"] = lambda: back2(UL)
    tasks["b3"] = lambda: back3(UL)
    tasks["b4"] = lambda: back4(UL)

    def task(body):
        tasks[body.__name__] = body

    @task
    def mask():
        build_mask()

    @task
    def first_norm():
        ag5(US)
        for k in (1, 2, 3):
            arrive(("tok", k), r.xb.at[lax.rem(sp + 4 - k, 4)])
        own_tok.wait()
        small_vectors()
        norm_one()
        send("h1", r.h1c.at[0], r.h1c.at[1], partner)

    def qkv(i):
        def run():
            ag5(UQ[i])
            qkv_item(i)

        return run

    def attend(i):
        return lambda: pairs(attend_pair, i)

    def attend_back(i):
        def run():
            pairs(attend_back_pair, i)
            send(("dq", i), r.qkvb.at[3 * nc + i], r.dqp.at[i], partner)

        return run

    def grad_qkv(i):
        def run():
            if i == 0:
                arrive("h1", r.h1c.at[1])
            arrive(("dq", i), r.dqp.at[i])
            qkv_grad(i)

        return run

    for i in range(3):
        tasks["qkv" + str(i)] = qkv(i)
        tasks["attend" + str(i)] = attend(i)
        tasks["attend_back" + str(i)] = attend_back(i)
        tasks["qkv_grad" + str(i)] = grad_qkv(i)

    tasks["tok2"] = lambda: send_pack("tok", r.tok, r.xb, (2,))
    tasks["tok1"] = lambda: send_pack("tok", r.tok, r.xb, (1, 3))
    tasks["dx2"] = lambda: send_rows("dx", r.dx_o, (2,))
    tasks["dx1"] = lambda: send_rows("dx", r.dx_o, (1, 3))
    tasks["cot2"] = lambda: send_pack("cot", r.cot, r.cb, (2,))
    tasks["cot1"] = lambda: send_pack("cot", r.cot, r.cb, (1, 3))

    tasks["l1"] = lambda: late1(UL)

    @task
    def out():
        send("attn", r.attnc.at[0], r.attnc.at[1], partner)
        ag5(UO)
        out_proj()
        send("h2", r.h2c.at[0], r.h2c.at[1], partner)

    @task
    def flip():
        flip_lse()
        build_mask_t()

    @task
    def rows():
        for k in (1, 2, 3):
            arrive(("cot", k), r.cb.at[lax.rem(sp + 4 - k, 4)])
        own_cot.wait()
        mlp_grad_rows()
        send("dml", half_cols(r.dml, nc), r.dml_p, partner)

    def act_cols(core, j, h):
        return r.actc.at[core, :, pl.ds(h * (FF // 2) + j * D, D)]

    def up(j):
        def run():
            ag5(UF[j])

            def one(i, carry):
                up_item(i)
                return carry

            lax.fori_loop(2 * j, 2 * j + 2, one, 0)
            for h in (0, 1):
                send(("act", j, h), act_cols(0, j, h), act_cols(1, j, h), partner)

        return run

    def proj(j):
        def run():
            if j == 0:
                arrive("dml", r.dml_p)
            for h in (0, 1):
                arrive(("act", j, h), act_cols(1, j, h))
            proj_grad(j)

        return run

    def up_weight(j):
        def run():
            if j == 0:
                arrive("h2", r.h2c.at[1])
                arrive("dpre", r.dpre_p)
            up_grad(j)

        return run

    for j in range(2):
        tasks["up" + str(j)] = up(j)
        tasks["proj" + str(j)] = proj(j)
        tasks["up_grad" + str(j)] = up_weight(j)

    @task
    def whole():
        ag5(UP)
        late5(UL)

    own = {}

    @task
    def final():
        layer_out()
        send_rows("out", r.out_o, (2, 1, 3))
        own["out"] = keep_rows(r.out_o, 2)

    @task
    def down():
        down_back()
        send("dpre", r.slope.at[:, pl.ds(pl.multiple_of(nc * (FF // 2), 128), FF // 2)], r.dpre_p, partner)

    @task
    def up_input():
        up_back()

    @task
    def second_norm():
        norm_two_back()
        send("dbr", half_cols(r.dbr, nc), r.dbr_p, partner)

    @task
    def out_input():
        out_back()

    @task
    def out_weight():
        arrive("attn", r.attnc.at[1])
        arrive("dbr", r.dbr_p)
        out_grad()

    @task
    def qkv_input():
        qkv_back()

    @task
    def last_norm():
        own["out"].wait()
        for k in (1, 2, 3):
            started.pop(("out", k)).wait_send()
        norm_one_back()
        r.gsm[12:16, :] = jnp.zeros((4, D), F32)
        small_send("x", r.gsm, 0, xpeer)
        own["dx"] = keep_rows(r.dx_o, 3)

    @task
    def small1():
        r.gs[0] = small_add(["x"], 0, None)
        small_send("core", r.gs.at[0], 1, partner)

    @task
    def small2():
        r.gs[1] = small_add(["core"], 1, 0)
        small_send("y", r.gs.at[1], 2, ypeer)

    @task
    def small3():
        r.gs[2] = small_add(["y"], 2, 1)
        for k in (1, 2, 3):
            small_send(("z", k), r.gs.at[2], 2 + k, zpeer(k))

    @task
    def small4():
        r.gs[3] = small_add([("z", 1), ("z", 2), ("z", 3)], 3, 2)
        pick_small()

    @task
    def proj_send():
        rs_proj_send()

    @task
    def proj_done():
        rs_proj_done()

    t = Bag()
    for name, body in tasks.items():
        setattr(t, "g" + name, body)
    t.gtok2()
    t.gl1()
    t.gmask()
    t.g2s()
    t.gl2()
    t.g3bs()
    t.g3as()
    t.g2q0()
    t.gtok1()
    t.g4bs()
    t.g4as()
    t.g2q1()
    t.g3bq0()
    t.g3aq0()
    t.g3bq1()
    t.gfirst_norm()
    t.g2q2()
    t.g3aq1()
    t.g4aq0()
    t.g4bq0()
    t.g2o()
    t.g3bq2()
    t.g4bq1()
    t.gqkv0()
    t.gattend0()
    t.g3aq2()
    t.g4aq1()
    t.g3bo()
    t.g3ao()
    t.g4bq2()
    t.g2f0()
    t.gl3()
    t.gcot2()
    t.gcot1()
    t.gqkv1()
    t.gattend1()
    t.g4bo()
    t.g4aq2()
    t.g2f1()
    t.gqkv2()
    t.g3af0()
    t.gattend2()
    t.g4ao()
    t.gflip()
    t.g3bf0()
    t.gout()
    t.g3bf1()
    t.grows()
    t.g3af1()
    t.g2p()
    t.g4af0()
    t.g4bf0()
    t.gup0()
    t.g4bf1()
    t.gl41()
    t.g3ap()
    t.g4af1()
    t.g3bp()
    t.gproj0()
    t.gl42()
    t.gup1()
    t.g4bp()
    t.gl43()
    t.g4ap()
    t.gproj1()
    t.gb1()
    t.gr1p()
    t.gwhole()
    t.gdown()
    t.gfinal()
    t.gr2bp()
    t.gup_input()
    t.gup_grad0()
    t.gr2ap()
    t.gr1f0()
    t.gup_grad1()
    t.gr1f1()
    t.gsecond_norm()
    t.gout_input()
    t.gattend_back0()
    t.gout_weight()
    t.gr1o()
    t.gattend_back1()
    t.gr3p()
    t.gr2af0()
    t.gqkv_grad0()
    t.gr2bf0()
    t.gr1q0()
    t.gattend_back2()
    t.gr2bf1()
    t.gqkv_grad1()
    t.gr2bo()
    t.gr1q1()
    t.gqkv_input()
    t.gqkv_grad2()
    t.gr2af1()
    t.gr1q2()
    t.glast_norm()
    t.gr2bq0()
    t.gr2ao()
    t.gr2bq1()
    t.gr3f0()
    t.gb2()
    t.gr2aq0()
    t.gr2bq2()
    t.gr4p()
    t.gsmall1()
    t.gr3f1()
    t.gsmall2()
    t.gr3o()
    t.gr2aq1()
    t.gr4f0()
    t.gr5f0()
    t.gr2aq2()
    t.gdx2()
    t.gdx1()
    t.gr3q0()
    t.gr3q1()
    t.gr4f1()
    t.gb3()
    t.gr5f1()
    t.gr3q2()
    t.gsmall3()
    t.gr4o()
    t.gr5o()
    t.gr4q0()
    t.gr5q0()
    t.gb4()
    t.gproj_send()
    t.gr4q1()
    t.gproj_done()
    t.gr5q1()
    t.gr4q2()
    t.gr5q2()
    t.gsmall4()
    for name, dst in (("out", r.out_o), ("dx", r.dx_o)):
        for k in (1, 2, 3):
            arrive((name, k), dst.at[lax.rem(sp + 4 - k, 4)])
    own["dx"].wait()
    for copy in started.values():
        copy.wait_send()
    assert len(table) <= SEMS, len(table)


def finish(out, d_x, gq, go, gf, gp, out_o, dx_o, gq_o, go_o, gf_o, gp_o):
    for src, dst in ((out, out_o), (gq, gq_o), (go, go_o), (gf, gf_o), (gp, gp_o)):
        dst[...] = src[...]
    dx_o[...] = d_x[...].astype(F32)


def fused(tokens, cotangent, seq_cut, g1, o1, w_qkv, bq, bv, w_out, bo, g2, o2, w_fc, bf, w_proj, bp):
    flat = jnp.concatenate([v[None] for v in (g1, o1, bq, bv, bo, g2, o2, bp, bf)] + [jnp.zeros((1, 96), BF16)], axis=1)
    vmem = pl.BlockSpec(memory_space=pltpu.VMEM)
    anywhere = pl.BlockSpec(memory_space=pl.ANY)
    s = jax.ShapeDtypeStruct
    out, d_x, gq, go, gf, gp, gs = pl.pallas_call(
        mega,
        out_shape=(
            s((4, 128, D), BF16),
            s((4, 128, D), BF16),
            s((24, 3 * D), F32),
            s((24, D), F32),
            s((24, FF), F32),
            s((96, D), F32),
            s((16, 128), F32),
        ),
        in_specs=[anywhere, anywhere] + [vmem] * 6,
        out_specs=(anywhere, anywhere) + (vmem,) * 5,
        scratch_shapes=scratch_shapes(),
        compiler_params=pltpu.CompilerParams(collective_id=0, has_side_effects=True, vmem_limit_bytes=67043328),
    )(tokens, cotangent, seq_cut, w_qkv, w_out, w_fc, w_proj, flat)
    out, d_x, gq, go, gf, gp = pl.pallas_call(
        finish,
        out_shape=(
            s((4, 128, D), BF16),
            s((4, 128, D), F32),
            s((24, 3 * D), F32),
            s((24, D), F32),
            s((24, FF), F32),
            s((96, D), F32),
        ),
        in_specs=[vmem] * 6,
        out_specs=(vmem,) * 6,
    )(out, d_x, gq, go, gf, gp)
    rows, g_bf = gs[:8, :24], gs[8, 32:]
    return (out, d_x, rows[0], rows[1], gq, rows[2], rows[3], go, rows[4], rows[5], rows[6], gf, g_bf, gp, rows[7])


def solution(mesh):
    row = P(AXES, None)
    vec = P(AXES)
    act = P(None, AXES, None)
    body = fused if dict(mesh.shape) == {"dp": 8, "sp": 4} else local
    return jax.shard_map(
        body,
        mesh=mesh,
        in_specs=(act, act, P(None, "dp"), vec, vec, row, vec, vec, row, vec, vec, vec, row, vec, row, vec),
        out_specs=(act, act, vec, vec, row, vec, vec, row, vec, vec, vec, row, vec, row, vec),
        check_vma=False,
    )
```
